32 devices in a mesh: dp: 8 (over y, x, core), seq: 4 (over z).
Axes of the slice: x: 2, y: 2, z: 4, core: 2. Of those that a mesh axis runs over, the one named last changes fastest.
Arguments:
- block_input: bfloat16 [4096, 1024], P(('dp', 'seq')), may hold values from -6 to 6
- cotangent: bfloat16 [4096, 1024], P(('dp', 'seq')), may hold values from -6 to 6
- ln1_gain: bfloat16 [1024], P(('dp', 'seq')), may hold values from 0.5 to 1.5
- ln1_bias: bfloat16 [1024], P(('dp', 'seq')), may hold values from -3 to 3
- qkv_weight: bfloat16 [1024, 3072], P(('dp', 'seq')), may hold values from -0.25 to 0.25
- qv_bias: bfloat16 [2048], P(('dp', 'seq')), may hold values from -3 to 3
- out_weight: bfloat16 [1024, 1024], P(('dp', 'seq')), may hold values from -0.75 to 0.75
- out_bias: bfloat16 [1024], P(('dp', 'seq')), may hold values from -3 to 3
- ln2_gain: bfloat16 [1024], P(('dp', 'seq')), may hold values from 0.5 to 1.5
- ln2_bias: bfloat16 [1024], P(('dp', 'seq')), may hold values from -3 to 3
- fc_weight: bfloat16 [1024, 4096], P(('dp', 'seq')), may hold values from -0.1875 to 0.1875
- fc_bias: bfloat16 [4096], P(('dp', 'seq')), may hold values from -3 to 3
- proj_weight: bfloat16 [4096, 1024], P(('dp', 'seq')), may hold values from -0.09375 to 0.09375
- proj_bias: bfloat16 [1024], P(('dp', 'seq')), may hold values from -3 to 3
Outputs:
- block_output: float32 [4096, 1024], P(('dp', 'seq'))
- grad_input: float32 [4096, 1024], P(('dp', 'seq'))
- grad_ln1_gain: float32 [1024], P(('dp', 'seq'))
- grad_ln1_bias: float32 [1024], P(('dp', 'seq'))
- grad_qkv_weight: float32 [1024, 3072], P(('dp', 'seq'))
- grad_qv_bias: float32 [2048], P(('dp', 'seq'))
- grad_out_weight: float32 [1024, 1024], P(('dp', 'seq'))
- grad_out_bias: float32 [1024], P(('dp', 'seq'))
- grad_ln2_gain: float32 [1024], P(('dp', 'seq'))
- grad_ln2_bias: float32 [1024], P(('dp', 'seq'))
- grad_fc_weight: float32 [1024, 4096], P(('dp', 'seq'))
- grad_fc_bias: float32 [4096], P(('dp', 'seq'))
- grad_proj_weight: float32 [4096, 1024], P(('dp', 'seq'))
- grad_proj_bias: float32 [1024], P(('dp', 'seq'))
The draws below stay inside these ranges and needn't reach their ends.
All inputs are finite; a program needn't handle non-finite values.
Results may differ from the reference program's by a relative error of at most 0.02.
Values may be sent and summed in bfloat16 or wider, within the bound.
A program may use at most 192 MiB of HBM per device.

```python
import math
import jax
import jax.numpy as jnp
from jax import lax

D = 1024
H = 16
HD = 64
FF = 4096
SEQ_LEN = 512
SEQS = 8
TOKENS = 4096


def draw_cotangent(key, part):
    rising = 0.5 + jnp.arange(TOKENS, dtype=jnp.float32) / TOKENS
    base_draw = jax.random.truncated_normal(key, -4.0, 4.0, (TOKENS, D), jnp.float32)
    return (base_draw * rising[:, None]).astype(jnp.bfloat16)


def block_scale(key, shape, split, least, top_value):
    def one(axis_at, shards_of):
        draws = jax.random.uniform(jax.random.fold_in(jax.random.fold_in(key, 6), axis_at), (shards_of,), jnp.float32, least / len(split), top_value / len(split))
        return jnp.repeat(jnp.exp(draws), shape[axis_at] // shards_of).reshape((-1,) + (1,) * (len(shape) - axis_at - 1))

    loudness = one(*split[0])
    for cut in split[1:]:
        loudness = loudness * one(*cut)
    return loudness


def gaussian(own_key, dims, deviation, reach, cuts=(), kind=jnp.bfloat16):
    loudness = block_scale(own_key, dims, cuts, -0.22, 0.18) if cuts else 1.0
    values = jax.random.normal(own_key, dims, jnp.float32) * deviation * loudness
    return jnp.minimum(jnp.maximum(values, -reach), reach).astype(kind)


def setup_inputs(seed: int = 0) -> dict:
    arg_keys = jax.random.split(jax.random.key(seed), 15)
    block_input = gaussian(arg_keys[0], (TOKENS, D), 1.0, 6.0, ((0, 32),))
    cotangent = draw_cotangent(jax.random.fold_in(arg_keys[14], 71), 0)
    ln1_gain = jnp.clip(1.0 + 0.1 * jax.random.normal(arg_keys[2], (D,), jnp.float32), 0.5, 1.5).astype(jnp.bfloat16)
    ln1_bias = gaussian(arg_keys[3], (D,), 0.5, 3.0, ((0, 32),))
    qkv_weight = gaussian(arg_keys[4], (D, 3 * D), (D // 2) ** -0.5, 0.25, ((0, 32),))
    qv_bias = gaussian(arg_keys[5], (2 * D,), 0.5, 3.0, ((0, 32),))
    out_weight = gaussian(arg_keys[6], (D, D), (D // 16) ** -0.5, 0.75, ((0, 32),))
    out_bias = gaussian(arg_keys[7], (D,), 0.5, 3.0, ((0, 32),))
    ln2_gain = jnp.clip(1.0 + 0.1 * jax.random.normal(arg_keys[8], (D,), jnp.float32), 0.5, 1.5).astype(jnp.bfloat16)
    ln2_bias = gaussian(arg_keys[9], (D,), 0.5, 3.0, ((0, 32),))
    fc_weight = gaussian(arg_keys[10], (D, FF), D ** -0.5, 0.1875, ((0, 32),))
    fc_bias = gaussian(arg_keys[11], (FF,), 0.5, 3.0, ((0, 32),))
    proj_weight = gaussian(arg_keys[12], (FF, D), FF ** -0.5, 0.09375, ((0, 32),))
    proj_bias = gaussian(arg_keys[13], (D,), 0.5, 3.0, ((0, 32),))
    return {"block_input": block_input, "cotangent": cotangent, "ln1_gain": ln1_gain, "ln1_bias": ln1_bias, "qkv_weight": qkv_weight, "qv_bias": qv_bias, "out_weight": out_weight, "out_bias": out_bias, "ln2_gain": ln2_gain, "ln2_bias": ln2_bias, "fc_weight": fc_weight, "fc_bias": fc_bias, "proj_weight": proj_weight, "proj_bias": proj_bias}


EPS = 1e-05
GELU_COEF = math.sqrt(2.0 / math.pi)

def layer_norm(values, norm_gain, offset):
    center = lax.optimization_barrier(jnp.mean(values, axis=-1, keepdims=True))
    centred = values - center
    spread = lax.optimization_barrier(jnp.mean(centred * centred, axis=-1, keepdims=True))
    return centred * lax.rsqrt(spread + EPS) * norm_gain + offset

def gelu_tanh(pre_act):
    return 0.5 * pre_act * (1.0 + jnp.tanh(GELU_COEF * (pre_act + 0.044715 * pre_act * pre_act * pre_act)))

def halved(values):
    return values.astype(jnp.bfloat16)

def widened(values):
    return values.astype(jnp.float32)

def matmul(left, right):
    return jnp.dot(left, right, preferred_element_type=jnp.float32)

def run_sequence(inputs, upstream, params):
    ln1_gain, ln1_bias, qkv_weight, qv_bias, out_weight, out_bias, ln2_gain, ln2_bias, fc_weight, fc_bias, proj_weight, proj_bias = params
    length = inputs.shape[0]
    score_scale = HD ** (-0.5)
    gain_one = widened(ln1_gain)
    bias_one = widened(ln1_bias)
    gain_two = widened(ln2_gain)
    bias_two = widened(ln2_bias)
    stream = widened(inputs)
    normed_one = halved(layer_norm(stream, gain_one, bias_one))
    projected = matmul(normed_one, qkv_weight)
    queries = halved(projected[:, :D] + widened(qv_bias[:D]))
    key_rows = halved(projected[:, D:2 * D])
    value_rows = halved(projected[:, 2 * D:] + widened(qv_bias[D:]))
    query_heads = widened(queries).reshape(length, H, HD)
    key_heads = widened(key_rows).reshape(length, H, HD)
    value_heads = widened(value_rows).reshape(length, H, HD)
    causal = jnp.tril(jnp.ones((length, length), dtype=bool))
    scores = jnp.einsum('qhd,khd->hqk', query_heads, key_heads) * score_scale
    row_total = lax.optimization_barrier(jnp.sum(jnp.where(causal, jnp.exp(scores), 0.0), axis=-1))
    log_total = jnp.log(row_total)
    shares = jnp.where(causal, jnp.exp(scores - log_total[:, :, None]), 0.0)
    shares_half = widened(halved(shares))
    attended = halved(jnp.einsum('hqk,khd->qhd', shares_half, value_heads).reshape(length, D))
    middle = stream + matmul(attended, out_weight) + widened(out_bias)
    normed_two = halved(layer_norm(middle, gain_two, bias_two))
    pre_act = matmul(normed_two, fc_weight) + widened(fc_bias)
    hidden = halved(gelu_tanh(pre_act))
    output = middle + matmul(hidden, proj_weight) + widened(proj_bias)
    grad_out = widened(upstream)
    grad_half = halved(grad_out)
    d_proj_weight = matmul(hidden.T, grad_half)
    d_proj_bias = lax.optimization_barrier(jnp.sum(grad_out, axis=0))
    grad_hidden = matmul(grad_half, proj_weight.T)
    _, gelu_back = jax.vjp(gelu_tanh, pre_act)
    grad_pre = gelu_back(grad_hidden)[0]
    pre_half = halved(grad_pre)
    d_fc_weight = matmul(normed_two.T, pre_half)
    d_fc_bias = lax.optimization_barrier(jnp.sum(grad_pre, axis=0))
    grad_normed_two = matmul(pre_half, fc_weight.T)
    _, norm_back_two = jax.vjp(layer_norm, middle, gain_two, bias_two)
    mid_branch, d_ln2_gain, d_ln2_bias = norm_back_two(grad_normed_two)
    grad_middle = grad_out + mid_branch
    middle_half = halved(grad_middle)
    d_out_weight = matmul(attended.T, middle_half)
    d_out_bias = lax.optimization_barrier(jnp.sum(grad_middle, axis=0))
    grad_attended = matmul(middle_half, out_weight.T)
    row_delta = jnp.einsum('qhd,qhd->hq', grad_attended.reshape(length, H, HD), widened(attended).reshape(length, H, HD))
    attended_grad_half = widened(halved(grad_attended)).reshape(length, H, HD)
    grad_shares = jnp.einsum('qhd,khd->hqk', attended_grad_half, value_heads)
    grad_scores = widened(halved(shares * (grad_shares - row_delta[:, :, None])))
    grad_queries = jnp.einsum('hqk,khd->qhd', grad_scores, key_heads).reshape(length, D) * score_scale
    grad_keys = jnp.einsum('hqk,qhd->khd', grad_scores, query_heads).reshape(length, D) * score_scale
    grad_values = jnp.einsum('hqk,qhd->khd', shares_half, attended_grad_half).reshape(length, D)
    grad_qkv = jnp.concatenate([grad_queries, grad_keys, grad_values], axis=1)
    qkv_half = halved(grad_qkv)
    d_qkv_weight = matmul(normed_one.T, qkv_half)
    d_qv_bias = jnp.concatenate([lax.optimization_barrier(jnp.sum(grad_queries, axis=0)), lax.optimization_barrier(jnp.sum(grad_values, axis=0))])
    grad_normed_one = matmul(qkv_half, qkv_weight.T)
    _, norm_back_one = jax.vjp(layer_norm, stream, gain_one, bias_one)
    stream_branch, d_ln1_gain, d_ln1_bias = norm_back_one(grad_normed_one)
    grad_stream = grad_middle + stream_branch
    grads = (d_ln1_gain, d_ln1_bias, d_qkv_weight, d_qv_bias, d_out_weight, d_out_bias, d_ln2_gain, d_ln2_bias, d_fc_weight, d_fc_bias, d_proj_weight, d_proj_bias)
    return (output, grad_stream, grads)

def reference(block_input, cotangent, ln1_gain, ln1_bias, qkv_weight, qv_bias, out_weight, out_bias, ln2_gain, ln2_bias, fc_weight, fc_bias, proj_weight, proj_bias):
    params = (ln1_gain, ln1_bias, qkv_weight, qv_bias, out_weight, out_bias, ln2_gain, ln2_bias, fc_weight, fc_bias, proj_weight, proj_bias)
    inputs_all = block_input.reshape(SEQS, SEQ_LEN, D)
    upstream_all = cotangent.reshape(SEQS, SEQ_LEN, D)
    zero_grads = tuple((jnp.zeros(param.shape, jnp.float32) for param in params))

    def one_sequence(carry, operands):
        output, grad_stream, grads = run_sequence(operands[0], operands[1], params)
        summed = tuple((acc + part_grad for acc, part_grad in zip(carry, grads)))
        return (summed, (output, grad_stream))
    sums, (outputs, grad_streams) = lax.scan(one_sequence, zero_grads, (inputs_all, upstream_all))
    return (outputs.reshape(TOKENS, D), grad_streams.reshape(TOKENS, D), sums[0], sums[1], sums[2], sums[3], sums[4], sums[5], sums[6], sums[7], sums[8], sums[9], sums[10], sums[11])
```

```python
import math

import jax
import jax.numpy as jnp
from jax import lax
from jax.experimental import pallas as pl
from jax.experimental.pallas import tpu as pltpu
from jax.sharding import PartitionSpec as P

D = 1024
H = 16
HD = 64
FF = 4096


EPS = 1e-05
GELU_COEF = math.sqrt(2.0 / math.pi)
MESH = pl.DeviceIdType.MESH


def layer_norm(values, norm_gain, offset):
    center = jnp.mean(values, axis=-1, keepdims=True)
    centred = values - center
    spread = jnp.mean(centred * centred, axis=-1, keepdims=True)
    return centred * lax.rsqrt(spread + EPS) * norm_gain + offset


def gelu_tanh(pre_act):
    return (
        0.5
        * pre_act
        * (1.0 + jnp.tanh(GELU_COEF * (pre_act + 0.044715 * pre_act * pre_act * pre_act)))
    )


def halved(values):
    return values.astype(jnp.bfloat16)


def widened(values):
    return values.astype(jnp.float32)


def matmul(left, right):
    return jnp.dot(left, right, preferred_element_type=jnp.float32)


def place():
    return lax.axis_index("dp"), lax.axis_index("seq")


def counts():
    return lax.axis_size("dp"), lax.axis_size("seq")


def remote(src, dst, send, recv, device):
    return pltpu.make_async_remote_copy(
        src_ref=src, dst_ref=dst, send_sem=send, recv_sem=recv, device_id=device, device_id_type=MESH
    )


def dma(*shape):
    return pltpu.SemaphoreType.DMA(shape)


def greet_all():
    dp, s = place()
    dpc, n = counts()
    barrier = pltpu.get_barrier_semaphore()

    def greet(i, carry):
        @pl.when(i != dp * n + s)
        def _():
            pl.semaphore_signal(barrier, inc=1, device_id=(i // n, i % n), device_id_type=MESH)

        return carry

    lax.fori_loop(0, dpc * n, greet, 0)
    pl.semaphore_wait(barrier, dpc * n - 1)


def greet_near():
    dp, s = place()
    dpc, n = counts()
    nc = dpc // 2
    barrier = pltpu.get_barrier_semaphore()
    for k in range(1, n):
        pl.semaphore_signal(barrier, inc=1, device_id=(dp, (s + k) % n), device_id_type=MESH)
    for k in range(1, nc):
        pl.semaphore_signal(barrier, inc=1, device_id=((dp + 2 * k) % dpc, s), device_id_type=MESH)
    pl.semaphore_signal(barrier, inc=1, device_id=(other_core(dp), s), device_id_type=MESH)
    pl.semaphore_wait(barrier, n - 1 + nc)


def greet_seq():
    dp, s = place()
    _, n = counts()
    barrier = pltpu.get_barrier_semaphore()
    for k in range(1, n):
        pl.semaphore_signal(barrier, inc=1, device_id=(dp, (s + k) % n), device_id_type=MESH)
    pl.semaphore_wait(barrier, n - 1)


def other_core(dp):
    return dp + 1 - 2 * (dp % 2)


class Exchange:
    def __init__(self, value):
        _, n = counts()
        self.operands = (value,)
        self.outs = (value,)
        self.sems = (dma(n), dma(n))

    def copies(self, ins, outs, sems):
        dp, s = place()
        _, n = counts()
        return [
            remote(
                ins[0].at[(s + k) % n], outs[0].at[s], sems[0].at[k], sems[1].at[k], (dp, (s + k) % n)
            )
            for k in range(n - 1, 0, -1)
        ]

    def start(self, ins, outs, sems):
        for copy in self.copies(ins, outs, sems):
            copy.start()

    def finish(self, ins, outs, sems):
        for copy in self.copies(ins, outs, sems):
            copy.wait()


class Plane(Exchange):
    def __init__(self, value):
        dpc, _ = counts()
        self.operands = (value,)
        self.outs = (value,)
        self.sems = (dma(dpc // 2), dma(dpc // 2))

    def copies(self, ins, outs, sems):
        dp, s = place()
        dpc, _ = counts()
        chip, core, nc = dp // 2, dp % 2, dpc // 2
        return [
            remote(
                ins[0].at[(chip + k) % nc],
                outs[0].at[chip],
                sems[0].at[k],
                sems[1].at[k],
                ((chip + k) % nc * 2 + core, s),
            )
            for k in range(1, nc)
        ]


class Partner(Exchange):
    def __init__(self, value):
        self.operands = (value,)
        self.outs = (jax.ShapeDtypeStruct(value.shape[1:], value.dtype),)
        self.sems = (dma(1), dma(1))

    def copies(self, ins, outs, sems):
        dp, s = place()
        return [
            remote(
                ins[0].at[1 - dp % 2], outs[0], sems[0].at[0], sems[1].at[0], (other_core(dp), s)
            )
        ]


class Everyone:
    def __init__(self, value):
        dpc, n = counts()
        self.operands = (value,)
        self.outs = (value,)
        self.sems = (dma(dpc * n), dma(dpc * n))

    def copy(self, ins, outs, sems, k):
        dp, s = place()
        dpc, n = counts()
        me = dp * n + s
        peer = (me + k) % (dpc * n)
        return remote(
            ins[0].at[peer], outs[0].at[me], sems[0].at[k], sems[1].at[k], (peer // n, peer % n)
        )

    def start(self, ins, outs, sems):
        def step(k, carry):
            self.copy(ins, outs, sems, k).start()
            return carry

        lax.fori_loop(1, self.outs[0].shape[0], step, 0)

    def finish(self, ins, outs, sems):
        def step(k, carry):
            self.copy(ins, outs, sems, k).wait()
            return carry

        lax.fori_loop(1, self.outs[0].shape[0], step, 0)


class Walk:
    def __init__(self, source, block, sems, pair=False, keep=True):
        self.source, self.block, self.sems, self.pair, self.keep = source, block, sems, pair, keep

    @staticmethod
    def scratch(pair=False):
        _, n = counts()
        return (dma(2, n), dma(2, n), dma(1)) + ((dma(2, n), dma(2, n)) if pair else ())

    def hand_on(self, way, k):
        dp, s = place()
        sign = 1 - 2 * way
        block = self.block(s - sign * k, dp % 2)
        return remote(
            self.source if k == 0 else block, block,
            self.sems[0].at[way, k], self.sems[1].at[way, k], (dp, s + sign),
        )

    def over(self, way, k, core):
        dp, s = place()
        block = self.block(s - (1 - 2 * way) * k, core)
        return remote(
            self.source if k == 0 else block, block,
            self.sems[3].at[way, k], self.sems[4].at[way, k], (other_core(dp), s),
        )

    def own(self):
        dp, s = place()
        return pltpu.make_async_copy(self.source, self.block(s, dp % 2), self.sems[2].at[0])

    def guard(self, way, k):
        _, s = place()
        _, n = counts()
        return (s >= k) if way == 0 else (s < n - k)

    def follows(self, way):
        _, s = place()
        _, n = counts()
        return (s < n - 1) if way == 0 else (s > 0)

    def start(self):
        dp, _ = place()
        for way in (0, 1):

            @pl.when(self.follows(way))
            def _():
                self.hand_on(way, 0).start()

        if self.keep:
            self.own().start()
        if self.pair:
            self.over(0, 0, dp % 2).start()

    def step(self, k):
        dp, s = place()
        _, n = counts()
        for way in (0, 1):
            sign = 1 - 2 * way

            @pl.when(self.guard(way, k))
            def _():
                block = self.block(s - sign * k, dp % 2)
                remote(
                    block, block, self.sems[0].at[way, k - 1], self.sems[1].at[way, k - 1],
                    (dp, s - sign),
                ).wait_recv()
                if k < n - 1:

                    @pl.when(self.follows(way))
                    def _():
                        self.hand_on(way, k).start()

                if self.pair:
                    self.over(way, k, dp % 2).start()

    def close(self):
        dp, _ = place()
        _, n = counts()
        for way in (0, 1):
            for k in range(n - 1):

                @pl.when(jnp.logical_and(self.follows(way), self.guard(way, k)))
                def _():
                    self.hand_on(way, k).wait_send()

        if self.keep:
            self.own().wait()
        if self.pair:
            self.over(0, 0, dp % 2).wait_send()
            self.over(0, 0, 1 - dp % 2).wait_recv()
            for way in (0, 1):
                for k in range(1, n):

                    @pl.when(self.guard(way, k))
                    def _():
                        self.over(way, k, dp % 2).wait_send()
                        self.over(way, k, 1 - dp % 2).wait_recv()


class Spread:
    def __init__(self, source, block, sems, pair=False):
        self.source, self.block, self.sems, self.pair = source, block, sems, pair

    @staticmethod
    def scratch(pair=False):
        dpc, _ = counts()
        nc = dpc // 2
        return (dma(nc), dma(nc)) + ((dma(nc), dma(nc)) if pair else ())

    def to_chips(self):
        dp, s = place()
        dpc, _ = counts()
        nc = dpc // 2
        return [
            remote(
                self.source, self.block(dp // 2, dp % 2), self.sems[0].at[k], self.sems[1].at[k],
                ((dp // 2 + k) % nc * 2 + dp % 2, s),
            )
            for k in range(1, nc)
        ]

    def over(self, k, core):
        dp, s = place()
        dpc, _ = counts()
        nc = dpc // 2
        block = self.block((dp // 2 - k + nc) % nc, core)
        return remote(
            self.source if k == 0 else block, block, self.sems[2].at[k], self.sems[3].at[k],
            (other_core(dp), s),
        )

    def start(self):
        dp, _ = place()
        for copy in self.to_chips():
            copy.start()
        if self.pair:
            self.over(0, dp % 2).start()

    def step(self):
        dp, s = place()
        dpc, _ = counts()
        nc = dpc // 2
        for k in range(1, nc):
            chip = (dp // 2 - k + nc) % nc
            block = self.block(chip, dp % 2)
            remote(
                block, block, self.sems[0].at[k], self.sems[1].at[k], (chip * 2 + dp % 2, s)
            ).wait_recv()
            if self.pair:
                self.over(k, dp % 2).start()

    def close(self):
        dp, _ = place()
        dpc, _ = counts()
        for copy in self.to_chips():
            copy.wait_send()
        if self.pair:
            for k in range(dpc // 2):
                self.over(k, dp % 2).wait_send()
                self.over(k, 1 - dp % 2).wait_recv()


class Gather:
    def __init__(self, value):
        dpc, _ = counts()
        self.operands = (value,)
        self.outs = (jax.ShapeDtypeStruct((dpc // 2,) + value.shape, value.dtype),)
        self.sems = Spread.scratch() + (dma(1),)

    def spread(self, ins, outs, sems):
        return Spread(ins[0], lambda chip, core: outs[0].at[chip], sems)

    def own(self, ins, outs, sems):
        dp, _ = place()
        return pltpu.make_async_copy(ins[0], outs[0].at[dp // 2], sems[2].at[0])

    def start(self, ins, outs, sems):
        self.spread(ins, outs, sems).start()
        self.own(ins, outs, sems).start()

    def finish(self, ins, outs, sems):
        self.spread(ins, outs, sems).step()
        self.spread(ins, outs, sems).close()
        self.own(ins, outs, sems).wait()


def run(number, greet, *tasks):
    spans = []
    a = b = c = 0
    for task in tasks:
        spans.append((a, b, c))
        a += len(task.operands)
        b += len(task.outs)
        c += len(task.sems)
    n_in, n_out = a, b

    def kernel(*refs):
        ins, outs, sems = refs[:n_in], refs[n_in : n_in + n_out], refs[n_in + n_out :]
        greet()
        views = [
            (
                ins[i : i + len(t.operands)],
                outs[o : o + len(t.outs)],
                sems[m : m + len(t.sems)],
            )
            for t, (i, o, m) in zip(tasks, spans)
        ]
        for t, view in zip(tasks, views):
            t.start(*view)
        for t, view in zip(tasks, views):
            t.finish(*view)

    return pl.pallas_call(
        kernel,
        out_shape=[jax.ShapeDtypeStruct(o.shape, o.dtype) for t in tasks for o in t.outs],
        in_specs=[pl.BlockSpec(memory_space=pl.ANY)] * n_in,
        out_specs=[pl.BlockSpec(memory_space=pl.ANY)] * n_out,
        scratch_shapes=[s for t in tasks for s in t.sems],
        compiler_params=pltpu.CompilerParams(collective_id=number, has_side_effects=True),
    )(*[v for t in tasks for v in t.operands])


def gather_inputs(block_input, cotangent, pack, small, out_rows, fc_rows, proj_rows):
    dpc, n = counts()
    nc = dpc // 2
    units = fc_rows.shape[1] // nc
    whole = pack.ndim == 2
    wide = block_input.shape[1] // n
    pieces = 3 if whole else 1
    rows = out_rows.shape[0]

    def kernel(
        x_in, g_in, pack_in, small_in, out_in, fc_in, proj_in,
        x_all, g_all, pack_all, small_all, out_all, fc_all, proj_all, fc_own, *sems,
    ):
        dp, s = place()
        chip, core = dp // 2, dp % 2

        def take(count):
            nonlocal sems
            head, sems = sems[:count], sems[count:]
            return head

        pack_send, pack_recv, small_send, small_recv, fc_send, fc_recv, local = take(7)
        x = Walk(x_in, lambda i, c: x_all.at[i], take(3))
        out = Walk(out_in, lambda i, c: out_all.at[dp, i], take(3))
        fc = Walk(fc_own, lambda i, c: fc_all.at[:, c, i], take(5), pair=True)
        proj = Walk(proj_in, lambda i, c: proj_all.at[c, i], take(5), pair=True)
        grads = Spread(g_in, lambda p, c: g_all.at[p], take(2))
        spread_pack = Spread(pack_all.at[dp], lambda p, c: pack_all.at[p * 2 + c], take(4), pair=True)
        spread_small = Spread(small_all.at[dp], lambda p, c: small_all.at[p * 2 + c], take(4), pair=True)
        spread_out = Spread(out_all.at[dp], lambda p, c: out_all.at[p * 2 + c], take(4), pair=True)

        def piece(to, j):
            if whole:
                source = pack_in.at[:, pl.ds(pl.multiple_of(j * n * wide + to * wide, 128), wide)]
                return source, pack_all.at[dp, s, :, pl.ds(j * wide, wide)]
            return pack_in.at[to], pack_all.at[dp, s]

        shuffles = []
        for k in range(n - 1, 0, -1):
            to = (s + k) % n
            for j in range(pieces):
                source, target = piece(to, j)
                shuffles.append(
                    remote(source, target, pack_send.at[j, k], pack_recv.at[j, k], (dp, to))
                )
            shuffles.append(
                remote(small_in, small_all.at[dp, s], small_send.at[k], small_recv.at[k], (dp, to))
            )

        def cut(to):
            return fc_in.at[:, pl.ds(pl.multiple_of(to * units, 128), units)]

        turns = [
            remote(
                cut((chip + k) % nc), fc_own.at[chip], fc_send.at[k], fc_recv.at[k],
                ((chip + k) % nc * 2 + core, s),
            )
            for k in range(1, nc)
        ]
        keeps = [
            pltpu.make_async_copy(*piece(s, j), local.at[j]) for j in range(pieces)
        ] + [
            pltpu.make_async_copy(small_in, small_all.at[dp, s], local.at[3]),
            pltpu.make_async_copy(cut(chip), fc_own.at[chip], local.at[4]),
        ]
        keep_g = pltpu.make_async_copy(g_in, g_all.at[chip], local.at[5])

        greet_near()
        for copy in shuffles + keeps:
            copy.start()
        x.start()
        out.start()
        for copy in turns:
            copy.start()
        for copy in shuffles + keeps:
            copy.wait()
        spread_pack.start()
        spread_small.start()
        grads.start()
        keep_g.start()
        for k in range(1, n):
            x.step(k)
            out.step(k)
        out.own().wait()
        spread_out.start()
        for copy in turns:
            copy.wait()
        fc.start()
        proj.start()
        spread_pack.step()
        spread_small.step()
        for k in range(1, n):
            fc.step(k)
            proj.step(k)
        spread_out.step()
        grads.step()
        x.close()
        out.keep = False
        out.close()
        fc.close()
        proj.close()
        for spread in (spread_pack, spread_small, spread_out, grads):
            spread.close()
        keep_g.wait()

    def grown(value, *lead):
        return jax.ShapeDtypeStruct(lead, value.dtype)

    depth = block_input.shape[1]
    return pl.pallas_call(
        kernel,
        out_shape=[
            grown(block_input, n, *block_input.shape), grown(cotangent, nc, *cotangent.shape),
            grown(pack, dpc, n, rows, 3 * wide), grown(small, dpc, n, *small.shape),
            grown(out_rows, dpc, n, *out_rows.shape), grown(fc_rows, nc, 2, n, rows, units),
            grown(proj_rows, 2, n, *proj_rows.shape), grown(fc_rows, nc, rows, units),
        ],
        in_specs=[pl.BlockSpec(memory_space=pl.ANY)] * 7,
        out_specs=[pl.BlockSpec(memory_space=pl.ANY)] * 8,
        scratch_shapes=[
            dma(pieces, n), dma(pieces, n), dma(n), dma(n), dma(nc), dma(nc), dma(6),
            *Walk.scratch(), *Walk.scratch(), *Walk.scratch(True), *Walk.scratch(True),
            *Spread.scratch(), *Spread.scratch(True), *Spread.scratch(True), *Spread.scratch(True),
        ],
        compiler_params=pltpu.CompilerParams(collective_id=0, has_side_effects=True),
    )(block_input, cotangent, pack, small, out_rows, fc_rows, proj_rows)[:7]


def total(own, received, mine):
    picked = [
        jnp.where(k == mine, widened(own[k]), widened(received[k])) for k in range(own.shape[0])
    ]
    result = picked[0]
    for value in picked[1:]:
        result = result + value
    return result


def fill(own, received, mine):
    slots = lax.broadcasted_iota(jnp.int32, (own.shape[0],) + (1,) * (own.ndim - 1), 0)
    return jnp.where(slots == mine, own, received)


def local(
    block_input, cotangent, ln1_gain, ln1_bias, qkv_weight, qv_bias, out_weight, out_bias, ln2_gain,
    ln2_bias, fc_weight, fc_bias, proj_weight, proj_bias,
):
    dp, s = place()
    dpc, n = counts()
    nc, ranks = dpc // 2, dpc * n
    core, chip = dp % 2, dp // 2
    tok_rows = block_input.shape[0]
    rows = qkv_weight.shape[0]
    own_units = fc_bias.shape[0]
    units = FF // nc
    heads = H // n
    wide = heads * HD
    length = n * tok_rows
    score_scale = HD ** (-0.5)

    def row_of(value, i):
        return jnp.pad(value[None], ((i, 15 - i), (0, 128 - value.shape[0])))

    parts = (ln1_gain, ln1_bias, out_bias, ln2_gain, ln2_bias, proj_bias, qv_bias, fc_bias)
    small = row_of(parts[0], 0)
    for i in range(1, 8):
        small = small + row_of(parts[i], i)
    pack = qkv_weight
    if wide % 128:
        pack = (
            qkv_weight.reshape(rows, 3, n, wide).transpose(2, 0, 1, 3).reshape(n, rows, 3 * wide)
        )
    x_all, g_all, pack_all, small_all, out_all, fc_all, proj_all = gather_inputs(
        block_input, cotangent, pack, small, out_weight, fc_weight, proj_weight
    )
    stream_seq = widened(x_all.reshape(length, D))
    grad_ff = g_all.reshape(nc * tok_rows, D)
    qkv_cols = pack_all.reshape(D, 3 * wide)
    out_full = out_all.reshape(D, D)
    fc_cols = fc_all.reshape(D, units)
    proj_rows = proj_all.reshape(units, D)
    smalls = small_all.reshape(ranks, 16, 128)
    gain_one, bias_one, out_bias_full, gain_two, bias_two, proj_bias_full = (
        widened(smalls[:, i, :rows].reshape(D)) for i in range(6)
    )
    qv_full = smalls[:, 6, : qv_bias.shape[0]].reshape(2, n, wide)
    qv_own = widened(lax.dynamic_index_in_dim(qv_full, s, 1, keepdims=False))
    fc_bias_cols = widened(
        lax.dynamic_index_in_dim(
            smalls[:, 7, :own_units].reshape(nc, units), chip, 0, keepdims=False
        )
    )

    normed_one = halved(layer_norm(stream_seq, gain_one, bias_one))
    projected = matmul(normed_one, qkv_cols)

    def by_head(values):
        return values.reshape(length, heads, HD).transpose(1, 0, 2)

    def by_token(values):
        return values.transpose(1, 0, 2).reshape(length, wide)

    def side_by_side(own, got):
        return fill(own, got, s).transpose(1, 0, 2).reshape(tok_rows, n * wide)

    queries = by_head(halved(projected[:, :wide] + qv_own[0]))
    keys = by_head(halved(projected[:, wide : 2 * wide]))
    values = by_head(halved(projected[:, 2 * wide :] + qv_own[1]))
    position = jnp.arange(length, dtype=jnp.int32)
    visible = position[None, :] <= position[:, None]
    scores = (
        jnp.einsum("hqd,hkd->hqk", queries, keys, preferred_element_type=jnp.float32) * score_scale
    )
    log_total = jnp.log(
        jnp.sum(jnp.where(visible, jnp.exp(scores), 0.0), axis=-1, keepdims=True)
    )
    probs = jnp.where(visible, jnp.exp(scores - log_total), 0.0)
    shares = halved(probs)
    attended_heads = halved(
        jnp.einsum("hqk,hkd->hqd", shares, values, preferred_element_type=jnp.float32)
    )
    attended = by_token(attended_heads).reshape(n, tok_rows, wide)
    (attended_got,) = run(1, greet_seq, Exchange(attended))
    attended_own = side_by_side(attended, attended_got)
    stream = widened(block_input)
    middle = stream + matmul(attended_own, out_full) + out_bias_full
    normed_two = halved(layer_norm(middle, gain_two, bias_two))
    (normed_all,) = run(2, greet_near, Gather(normed_two))
    normed_ff = normed_all.reshape(nc * tok_rows, D)
    grad_out = widened(cotangent)
    d_proj_bias = jnp.sum(grad_out, axis=0)
    pre_act = matmul(normed_ff, fc_cols) + fc_bias_cols
    hidden = halved(gelu_tanh(pre_act))
    grad_hidden = matmul(grad_ff, proj_rows.T)
    _, gelu_back = jax.vjp(gelu_tanh, pre_act)
    grad_pre = gelu_back(grad_hidden)[0]
    pre_half = halved(grad_pre)
    back_two = halved(matmul(pre_half, fc_cols.T)).reshape(nc, tok_rows, D)
    ff_part = halved(matmul(hidden, proj_rows)).reshape(nc, tok_rows, D)
    d_proj = halved(matmul(hidden.T, grad_ff)).reshape(2, n, own_units, D)
    d_fc = (
        halved(matmul(normed_ff.T, pre_half))
        .reshape(nc, 2, n, rows, units)
        .transpose(1, 2, 0, 3, 4)
    )
    d_fc_bias = jnp.sum(grad_pre, axis=0)
    back_two_got, d_proj_got, d_fc_got = run(
        3, greet_near, Plane(back_two), Partner(d_proj), Partner(d_fc)
    )

    def pair(own, received):
        kept = lax.dynamic_index_in_dim(own, core, 0, keepdims=False)
        return halved(widened(kept) + widened(received))

    _, norm_back_two = jax.vjp(layer_norm, middle, gain_two, bias_two)
    mid_branch, d_ln2_gain, d_ln2_bias = norm_back_two(total(back_two, back_two_got, chip))
    grad_middle = grad_out + mid_branch
    d_out_bias = jnp.sum(grad_middle, axis=0)
    middle_half = halved(grad_middle)
    d_out = (
        halved(matmul(attended_own.T, middle_half))
        .reshape(nc, 2, n * rows, D)
        .transpose(1, 0, 2, 3)
    )
    grad_attended = halved(matmul(middle_half, out_full.T))
    grad_attended = grad_attended.reshape(tok_rows, n, wide).transpose(1, 0, 2)
    d_proj, d_fc = pair(d_proj, d_proj_got), pair(d_fc, d_fc_got)
    grad_att_got, ff_got, d_proj_parts, d_out_got = run(
        4, greet_near, Exchange(grad_attended), Plane(ff_part), Exchange(d_proj), Partner(d_out)
    )
    proj_grad = total(d_proj, d_proj_parts, s)
    output = middle + total(ff_part, ff_got, chip) + proj_bias_full
    grad_att = by_head(fill(grad_attended, grad_att_got, s).reshape(length, wide))
    row_delta = jnp.sum(widened(grad_att) * widened(attended_heads), axis=-1, keepdims=True)
    grad_shares = jnp.einsum("hqd,hkd->hqk", grad_att, values, preferred_element_type=jnp.float32)
    grad_scores = halved(probs * (grad_shares - row_delta))
    grad_q = (
        jnp.einsum("hqk,hkd->hqd", grad_scores, keys, preferred_element_type=jnp.float32)
        * score_scale
    )
    grad_k = (
        jnp.einsum("hqk,hqd->hkd", grad_scores, queries, preferred_element_type=jnp.float32)
        * score_scale
    )
    grad_v = jnp.einsum("hqk,hqd->hkd", shares, grad_att, preferred_element_type=jnp.float32)
    grad_qkv = jnp.concatenate([by_token(grad_q), by_token(grad_k), by_token(grad_v)], axis=1)
    qkv_half = halved(grad_qkv)
    back_one = halved(matmul(qkv_half, qkv_cols.T)).reshape(n, tok_rows, D)
    d_qkv = (
        halved(matmul(normed_one.T, qkv_half))
        .reshape(nc, 2, n * rows, 3 * wide)
        .transpose(1, 0, 2, 3)
    )
    sums = jnp.sum(grad_qkv, axis=0)
    d_qv = jnp.stack([sums[:wide], sums[2 * wide :]])[:, None]
    d_out = pair(d_out, d_out_got)
    back_one_got, d_fc_parts, d_out_parts, d_qkv_got = run(
        5, greet_near, Exchange(back_one), Exchange(d_fc), Plane(d_out), Partner(d_qkv)
    )
    d_qkv = pair(d_qkv, d_qkv_got)
    fc_cut = halved(total(d_fc, d_fc_parts, s))
    out_cut = halved(total(d_out, d_out_parts, chip)).reshape(n, rows, D)
    _, norm_back_one = jax.vjp(layer_norm, stream, gain_one, bias_one)
    stream_branch, d_ln1_gain, d_ln1_bias = norm_back_one(total(back_one, back_one_got, s))
    grad_stream = grad_middle + stream_branch
    turn = jnp.arange(n, dtype=jnp.int32)[None, :, None] == s
    mine = jnp.arange(nc, dtype=jnp.int32)[:, None] == chip
    vectors = jnp.concatenate(
        [
            v.reshape(ranks, rows)
            for v in (d_ln1_gain, d_ln1_bias, d_out_bias, d_ln2_gain, d_ln2_bias, d_proj_bias)
        ]
        + [
            jnp.where(turn, d_qv, 0.0).reshape(ranks, -1),
            jnp.where(mine, d_fc_bias, 0.0).reshape(ranks, own_units),
        ],
        axis=1,
    )
    used = vectors.shape[1]
    vectors = jnp.pad(vectors, ((0, 0), (0, -used % 128))).reshape(ranks, -1, 128)
    d_qkv_parts, fc_got, d_out_last, vectors_got = run(
        6, greet_all, Plane(d_qkv), Plane(fc_cut), Exchange(out_cut), Everyone(vectors)
    )
    fc_grad = widened(fill(fc_cut, fc_got, chip)).transpose(1, 0, 2).reshape(rows, FF)
    out_grad = total(out_cut, d_out_last, s)
    qkv_rows = halved(total(d_qkv, d_qkv_parts, chip)).reshape(n, rows, 3 * wide)
    vector = jnp.sum(fill(vectors, vectors_got, dp * n + s), axis=0).reshape(-1)
    firsts = [vector[i * rows : (i + 1) * rows] for i in range(6)]
    at = 6 * rows
    qv_grad = vector[at : at + qv_bias.shape[0]]
    at += qv_bias.shape[0]
    fc_bias_grad = vector[at : at + own_units]
    (qkv_got,) = run(7, greet_seq, Exchange(qkv_rows))
    qkv_grad = (
        widened(fill(qkv_rows, qkv_got, s))
        .reshape(n, rows, 3, wide)
        .transpose(1, 2, 0, 3)
        .reshape(rows, 3 * D)
    )
    return (
        output, grad_stream, firsts[0], firsts[1], qkv_grad, qv_grad, out_grad, firsts[2],
        firsts[3], firsts[4], fc_grad, fc_bias_grad, proj_grad, firsts[5],
    )


def solution(mesh):
    in_specs = (
        P(("dp", "seq"), None),
        P(("dp", "seq"), None),
        P(("dp", "seq")),
        P(("dp", "seq")),
        P(("dp", "seq"), None),
        P(("dp", "seq")),
        P(("dp", "seq"), None),
        P(("dp", "seq")),
        P(("dp", "seq")),
        P(("dp", "seq")),
        P(("dp", "seq"), None),
        P(("dp", "seq")),
        P(("dp", "seq"), None),
        P(("dp", "seq")),
    )
    out_specs = (
        P(("dp", "seq"), None),
        P(("dp", "seq"), None),
        P(("dp", "seq")),
        P(("dp", "seq")),
        P(("dp", "seq"), None),
        P(("dp", "seq")),
        P(("dp", "seq"), None),
        P(("dp", "seq")),
        P(("dp", "seq")),
        P(("dp", "seq")),
        P(("dp", "seq"), None),
        P(("dp", "seq")),
        P(("dp", "seq"), None),
        P(("dp", "seq")),
    )
    return jax.shard_map(local, mesh=mesh, in_specs=in_specs, out_specs=out_specs, check_vma=False)
```

```python
import math

import jax
import jax.numpy as jnp
from jax import lax
from jax.experimental import pallas as pl
from jax.experimental.pallas import tpu as pltpu
from jax.sharding import PartitionSpec as P

D = 1024
H = 16
HD = 64
FF = 4096


EPS = 1e-05
GELU_COEF = math.sqrt(2.0 / math.pi)
MESH = pl.DeviceIdType.MESH


def layer_norm(values, norm_gain, offset):
    center = jnp.mean(values, axis=-1, keepdims=True)
    centred = values - center
    spread = jnp.mean(centred * centred, axis=-1, keepdims=True)
    return centred * lax.rsqrt(spread + EPS) * norm_gain + offset


def gelu_tanh(pre_act):
    return (
        0.5
        * pre_act
        * (1.0 + jnp.tanh(GELU_COEF * (pre_act + 0.044715 * pre_act * pre_act * pre_act)))
    )


def halved(values):
    return values.astype(jnp.bfloat16)


def widened(values):
    return values.astype(jnp.float32)


def matmul(left, right):
    return jnp.dot(left, right, preferred_element_type=jnp.float32)


def place():
    return lax.axis_index("dp"), lax.axis_index("seq")


def counts():
    return lax.axis_size("dp"), lax.axis_size("seq")


def remote(src, dst, send, recv, device):
    return pltpu.make_async_remote_copy(
        src_ref=src, dst_ref=dst, send_sem=send, recv_sem=recv, device_id=device, device_id_type=MESH
    )


def dma(*shape):
    return pltpu.SemaphoreType.DMA(shape)


def greet_all():
    dp, s = place()
    dpc, n = counts()
    barrier = pltpu.get_barrier_semaphore()

    def greet(i, carry):
        @pl.when(i != dp * n + s)
        def _():
            pl.semaphore_signal(barrier, inc=1, device_id=(i // n, i % n), device_id_type=MESH)

        return carry

    lax.fori_loop(0, dpc * n, greet, 0)
    pl.semaphore_wait(barrier, dpc * n - 1)


def greet_near():
    dp, s = place()
    dpc, n = counts()
    nc = dpc // 2
    barrier = pltpu.get_barrier_semaphore()
    for k in range(1, n):
        pl.semaphore_signal(barrier, inc=1, device_id=(dp, (s + k) % n), device_id_type=MESH)
    for k in range(1, nc):
        pl.semaphore_signal(barrier, inc=1, device_id=((dp + 2 * k) % dpc, s), device_id_type=MESH)
    pl.semaphore_signal(barrier, inc=1, device_id=(other_core(dp), s), device_id_type=MESH)
    pl.semaphore_wait(barrier, n - 1 + nc)


def greet_seq():
    dp, s = place()
    _, n = counts()
    barrier = pltpu.get_barrier_semaphore()
    for k in range(1, n):
        pl.semaphore_signal(barrier, inc=1, device_id=(dp, (s + k) % n), device_id_type=MESH)
    pl.semaphore_wait(barrier, n - 1)


def other_core(dp):
    return dp + 1 - 2 * (dp % 2)


class Exchange:
    def __init__(self, value):
        _, n = counts()
        self.operands = (value,)
        self.outs = (value,)
        self.sems = (dma(n), dma(n))

    def copies(self, ins, outs, sems):
        dp, s = place()
        _, n = counts()
        return [
            remote(
                ins[0].at[(s + k) % n], outs[0].at[s], sems[0].at[k], sems[1].at[k], (dp, (s + k) % n)
            )
            for k in range(n - 1, 0, -1)
        ]

    def start(self, ins, outs, sems):
        for copy in self.copies(ins, outs, sems):
            copy.start()

    def finish(self, ins, outs, sems):
        for copy in self.copies(ins, outs, sems):
            copy.wait()


class Plane(Exchange):
    def __init__(self, value):
        dpc, _ = counts()
        self.operands = (value,)
        self.outs = (value,)
        self.sems = (dma(dpc // 2), dma(dpc // 2))

    def copies(self, ins, outs, sems):
        dp, s = place()
        dpc, _ = counts()
        chip, core, nc = dp // 2, dp % 2, dpc // 2
        return [
            remote(
                ins[0].at[(chip + k) % nc],
                outs[0].at[chip],
                sems[0].at[k],
                sems[1].at[k],
                ((chip + k) % nc * 2 + core, s),
            )
            for k in range(1, nc)
        ]


class Partner(Exchange):
    def __init__(self, value):
        self.operands = (value,)
        self.outs = (jax.ShapeDtypeStruct(value.shape[1:], value.dtype),)
        self.sems = (dma(1), dma(1))

    def copies(self, ins, outs, sems):
        dp, s = place()
        return [
            remote(
                ins[0].at[1 - dp % 2], outs[0], sems[0].at[0], sems[1].at[0], (other_core(dp), s)
            )
        ]


class Everyone:
    def __init__(self, value):
        dpc, n = counts()
        self.operands = (value,)
        self.outs = (value,)
        self.sems = (dma(dpc * n), dma(dpc * n))

    def copy(self, ins, outs, sems, k):
        dp, s = place()
        dpc, n = counts()
        me = dp * n + s
        peer = (me + k) % (dpc * n)
        return remote(
            ins[0].at[peer], outs[0].at[me], sems[0].at[k], sems[1].at[k], (peer // n, peer % n)
        )

    def start(self, ins, outs, sems):
        def step(k, carry):
            self.copy(ins, outs, sems, k).start()
            return carry

        lax.fori_loop(1, self.outs[0].shape[0], step, 0)

    def finish(self, ins, outs, sems):
        def step(k, carry):
            self.copy(ins, outs, sems, k).wait()
            return carry

        lax.fori_loop(1, self.outs[0].shape[0], step, 0)


class Walk:
    def __init__(self, source, block, sems, pair=False, keep=True):
        self.source, self.block, self.sems, self.pair, self.keep = source, block, sems, pair, keep

    @staticmethod
    def scratch(pair=False):
        _, n = counts()
        return (dma(2, n), dma(2, n), dma(1)) + ((dma(2, n), dma(2, n)) if pair else ())

    def hand_on(self, way, k):
        dp, s = place()
        sign = 1 - 2 * way
        block = self.block(s - sign * k, dp % 2)
        return remote(
            self.source if k == 0 else block, block,
            self.sems[0].at[way, k], self.sems[1].at[way, k], (dp, s + sign),
        )

    def over(self, way, k, core):
        dp, s = place()
        block = self.block(s - (1 - 2 * way) * k, core)
        return remote(
            self.source if k == 0 else block, block,
            self.sems[3].at[way, k], self.sems[4].at[way, k], (other_core(dp), s),
        )

    def own(self):
        dp, s = place()
        return pltpu.make_async_copy(self.source, self.block(s, dp % 2), self.sems[2].at[0])

    def guard(self, way, k):
        _, s = place()
        _, n = counts()
        return (s >= k) if way == 0 else (s < n - k)

    def follows(self, way):
        _, s = place()
        _, n = counts()
        return (s < n - 1) if way == 0 else (s > 0)

    def start(self):
        dp, _ = place()
        for way in (0, 1):

            @pl.when(self.follows(way))
            def _():
                self.hand_on(way, 0).start()

        if self.keep:
            self.own().start()
        if self.pair:
            self.over(0, 0, dp % 2).start()

    def step(self, k):
        dp, s = place()
        _, n = counts()
        for way in (0, 1):
            sign = 1 - 2 * way

            @pl.when(self.guard(way, k))
            def _():
                block = self.block(s - sign * k, dp % 2)
                remote(
                    block, block, self.sems[0].at[way, k - 1], self.sems[1].at[way, k - 1],
                    (dp, s - sign),
                ).wait_recv()
                if k < n - 1:

                    @pl.when(self.follows(way))
                    def _():
                        self.hand_on(way, k).start()

                if self.pair:
                    self.over(way, k, dp % 2).start()

    def close(self):
        dp, _ = place()
        _, n = counts()
        for way in (0, 1):
            for k in range(n - 1):

                @pl.when(jnp.logical_and(self.follows(way), self.guard(way, k)))
                def _():
                    self.hand_on(way, k).wait_send()

        if self.keep:
            self.own().wait()
        if self.pair:
            self.over(0, 0, dp % 2).wait_send()
            self.over(0, 0, 1 - dp % 2).wait_recv()
            for way in (0, 1):
                for k in range(1, n):

                    @pl.when(self.guard(way, k))
                    def _():
                        self.over(way, k, dp % 2).wait_send()
                        self.over(way, k, 1 - dp % 2).wait_recv()


class Spread:
    def __init__(self, source, block, sems, pair=False):
        self.source, self.block, self.sems, self.pair = source, block, sems, pair

    @staticmethod
    def scratch(pair=False):
        dpc, _ = counts()
        nc = dpc // 2
        return (dma(nc), dma(nc)) + ((dma(nc), dma(nc)) if pair else ())

    def to_chips(self):
        dp, s = place()
        dpc, _ = counts()
        nc = dpc // 2
        return [
            remote(
                self.source, self.block(dp // 2, dp % 2), self.sems[0].at[k], self.sems[1].at[k],
                ((dp // 2 + k) % nc * 2 + dp % 2, s),
            )
            for k in range(1, nc)
        ]

    def over(self, k, core):
        dp, s = place()
        dpc, _ = counts()
        nc = dpc // 2
        block = self.block((dp // 2 - k + nc) % nc, core)
        return remote(
            self.source if k == 0 else block, block, self.sems[2].at[k], self.sems[3].at[k],
            (other_core(dp), s),
        )

    def start(self):
        dp, _ = place()
        for copy in self.to_chips():
            copy.start()
        if self.pair:
            self.over(0, dp % 2).start()

    def step(self):
        dp, s = place()
        dpc, _ = counts()
        nc = dpc // 2
        for k in range(1, nc):
            chip = (dp // 2 - k + nc) % nc
            block = self.block(chip, dp % 2)
            remote(
                block, block, self.sems[0].at[k], self.sems[1].at[k], (chip * 2 + dp % 2, s)
            ).wait_recv()
            if self.pair:
                self.over(k, dp % 2).start()

    def close(self):
        dp, _ = place()
        dpc, _ = counts()
        for copy in self.to_chips():
            copy.wait_send()
        if self.pair:
            for k in range(dpc // 2):
                self.over(k, dp % 2).wait_send()
                self.over(k, 1 - dp % 2).wait_recv()


class Gather:
    def __init__(self, value):
        dpc, _ = counts()
        self.operands = (value,)
        self.outs = (jax.ShapeDtypeStruct((dpc // 2,) + value.shape, value.dtype),)
        self.sems = Spread.scratch() + (dma(1),)

    def spread(self, ins, outs, sems):
        return Spread(ins[0], lambda chip, core: outs[0].at[chip], sems)

    def own(self, ins, outs, sems):
        dp, _ = place()
        return pltpu.make_async_copy(ins[0], outs[0].at[dp // 2], sems[2].at[0])

    def start(self, ins, outs, sems):
        self.spread(ins, outs, sems).start()
        self.own(ins, outs, sems).start()

    def finish(self, ins, outs, sems):
        self.spread(ins, outs, sems).step()
        self.spread(ins, outs, sems).close()
        self.own(ins, outs, sems).wait()


def run(number, greet, *tasks):
    spans = []
    a = b = c = 0
    for task in tasks:
        spans.append((a, b, c))
        a += len(task.operands)
        b += len(task.outs)
        c += len(task.sems)
    n_in, n_out = a, b

    def kernel(*refs):
        ins, outs, sems = refs[:n_in], refs[n_in : n_in + n_out], refs[n_in + n_out :]
        greet()
        views = [
            (
                ins[i : i + len(t.operands)],
                outs[o : o + len(t.outs)],
                sems[m : m + len(t.sems)],
            )
            for t, (i, o, m) in zip(tasks, spans)
        ]
        for t, view in zip(tasks, views):
            t.start(*view)
        for t, view in zip(tasks, views):
            t.finish(*view)

    return pl.pallas_call(
        kernel,
        out_shape=[jax.ShapeDtypeStruct(o.shape, o.dtype) for t in tasks for o in t.outs],
        in_specs=[pl.BlockSpec(memory_space=pl.ANY)] * n_in,
        out_specs=[pl.BlockSpec(memory_space=pl.ANY)] * n_out,
        scratch_shapes=[s for t in tasks for s in t.sems],
        compiler_params=pltpu.CompilerParams(collective_id=number, has_side_effects=True),
    )(*[v for t in tasks for v in t.operands])


def gather_inputs(block_input, cotangent, pack, small, out_rows, fc_rows, proj_rows):
    dpc, n = counts()
    nc = dpc // 2
    units = fc_rows.shape[1] // nc
    whole = pack.ndim == 2
    wide = block_input.shape[1] // n
    pieces = 3 if whole else 1
    rows = out_rows.shape[0]

    def kernel(
        x_in, g_in, pack_in, small_in, out_in, fc_in, proj_in,
        x_all, g_all, pack_all, small_all, out_all, fc_all, proj_all, fc_own, *sems,
    ):
        dp, s = place()
        chip, core = dp // 2, dp % 2

        def take(count):
            nonlocal sems
            head, sems = sems[:count], sems[count:]
            return head

        pack_send, pack_recv, small_send, small_recv, fc_send, fc_recv, local = take(7)
        x = Walk(x_in, lambda i, c: x_all.at[i], take(3))
        out = Walk(out_in, lambda i, c: out_all.at[dp, i], take(3))
        fc = Walk(fc_own, lambda i, c: fc_all.at[:, c, i], take(5), pair=True)
        proj = Walk(proj_in, lambda i, c: proj_all.at[c, i], take(5), pair=True)
        grads = Spread(g_in, lambda p, c: g_all.at[p], take(2))
        spread_pack = Spread(pack_all.at[dp], lambda p, c: pack_all.at[p * 2 + c], take(4), pair=True)
        spread_small = Spread(small_all.at[dp], lambda p, c: small_all.at[p * 2 + c], take(4), pair=True)
        spread_out = Spread(out_all.at[dp], lambda p, c: out_all.at[p * 2 + c], take(4), pair=True)

        def piece(to, j):
            if whole:
                source = pack_in.at[:, pl.ds(pl.multiple_of(j * n * wide + to * wide, 128), wide)]
                return source, pack_all.at[dp, s, :, pl.ds(j * wide, wide)]
            return pack_in.at[to], pack_all.at[dp, s]

        shuffles = []
        for k in range(n - 1, 0, -1):
            to = (s + k) % n
            for j in range(pieces):
                source, target = piece(to, j)
                shuffles.append(
                    remote(source, target, pack_send.at[j, k], pack_recv.at[j, k], (dp, to))
                )
            shuffles.append(
                remote(small_in, small_all.at[dp, s], small_send.at[k], small_recv.at[k], (dp, to))
            )

        def cut(to):
            return fc_in.at[:, pl.ds(pl.multiple_of(to * units, 128), units)]

        turns = [
            remote(
                cut((chip + k) % nc), fc_own.at[chip], fc_send.at[k], fc_recv.at[k],
                ((chip + k) % nc * 2 + core, s),
            )
            for k in range(1, nc)
        ]
        keeps = [
            pltpu.make_async_copy(*piece(s, j), local.at[j]) for j in range(pieces)
        ] + [
            pltpu.make_async_copy(small_in, small_all.at[dp, s], local.at[3]),
            pltpu.make_async_copy(cut(chip), fc_own.at[chip], local.at[4]),
        ]
        keep_g = pltpu.make_async_copy(g_in, g_all.at[chip], local.at[5])

        greet_near()
        for copy in shuffles + keeps:
            copy.start()
        x.start()
        out.start()
        for copy in turns:
            copy.start()
        for copy in shuffles + keeps:
            copy.wait()
        spread_pack.start()
        spread_small.start()
        grads.start()
        keep_g.start()
        for k in range(1, n):
            x.step(k)
            out.step(k)
        out.own().wait()
        spread_out.start()
        for copy in turns:
            copy.wait()
        fc.start()
        proj.start()
        spread_pack.step()
        spread_small.step()
        for k in range(1, n):
            fc.step(k)
            proj.step(k)
        spread_out.step()
        grads.step()
        x.close()
        out.keep = False
        out.close()
        fc.close()
        proj.close()
        for spread in (spread_pack, spread_small, spread_out, grads):
            spread.close()
        keep_g.wait()

    def grown(value, *lead):
        return jax.ShapeDtypeStruct(lead, value.dtype)

    depth = block_input.shape[1]
    return pl.pallas_call(
        kernel,
        out_shape=[
            grown(block_input, n, *block_input.shape), grown(cotangent, nc, *cotangent.shape),
            grown(pack, dpc, n, rows, 3 * wide), grown(small, dpc, n, *small.shape),
            grown(out_rows, dpc, n, *out_rows.shape), grown(fc_rows, nc, 2, n, rows, units),
            grown(proj_rows, 2, n, *proj_rows.shape), grown(fc_rows, nc, rows, units),
        ],
        in_specs=[pl.BlockSpec(memory_space=pl.ANY)] * 7,
        out_specs=[pl.BlockSpec(memory_space=pl.ANY)] * 8,
        scratch_shapes=[
            dma(pieces, n), dma(pieces, n), dma(n), dma(n), dma(nc), dma(nc), dma(6),
            *Walk.scratch(), *Walk.scratch(), *Walk.scratch(True), *Walk.scratch(True),
            *Spread.scratch(), *Spread.scratch(True), *Spread.scratch(True), *Spread.scratch(True),
        ],
        compiler_params=pltpu.CompilerParams(collective_id=0, has_side_effects=True),
    )(block_input, cotangent, pack, small, out_rows, fc_rows, proj_rows)[:7]


def total(own, received, mine):
    picked = [
        jnp.where(k == mine, widened(own[k]), widened(received[k])) for k in range(own.shape[0])
    ]
    result = picked[0]
    for value in picked[1:]:
        result = result + value
    return result


def fill(own, received, mine):
    slots = lax.broadcasted_iota(jnp.int32, (own.shape[0],) + (1,) * (own.ndim - 1), 0)
    return jnp.where(slots == mine, own, received)


def mask_of(half, shape):
    lane = lax.broadcasted_iota(jnp.int32, shape, len(shape) - 1)
    return (lane // HD) % 2 == half


def contract(left, right, dims):
    return lax.dot_general(
        left, right, ((dims[:1], dims[1:]), ((), ())), preferred_element_type=jnp.float32
    )


def unit_rows(values):
    center = jnp.mean(values, axis=-1, keepdims=True)
    centred = values - center
    spread = jnp.mean(centred * centred, axis=-1, keepdims=True)
    return centred, lax.rsqrt(spread + EPS)


def part(ref, i, size):
    return ref.at[pl.ds(pl.multiple_of(i * size, size), size)]


def lanes(ref, i, size):
    return ref.at[:, pl.ds(pl.multiple_of(i * size, size), size)]


def softmax_block(q_masked, k, log_total, diagonal):
    scores = contract(q_masked, k, (1, 1)) * HD ** (-0.5)
    row = lax.broadcasted_iota(jnp.int32, scores.shape, 0) + diagonal
    visible = lax.broadcasted_iota(jnp.int32, scores.shape, 1) <= row
    if log_total is None:
        log_total = jnp.log(
            jnp.sum(jnp.where(visible, jnp.exp(scores), 0.0), axis=-1, keepdims=True)
        )
    return jnp.where(visible, jnp.exp(scores - log_total), 0.0), log_total


def forward(block_input, cotangent, qkv_weight, small, out_weight, fc_weight, proj_weight):
    dpc, n = counts()
    nc, ranks = dpc // 2, dpc * n
    tok, depth = block_input.shape
    rows, units, own_units = out_weight.shape[0], fc_weight.shape[1] // nc, proj_weight.shape[0]
    wide, length = depth // n, n * tok
    heads = wide // HD
    bias_own = 2 * depth // ranks

    def kernel(*refs):
        refs = list(refs)

        def take(count):
            head = refs[:count]
            del refs[:count]
            return head

        x_in, g_in, qkv_in, small_in, out_in, fc_in, proj_in = take(7)
        (
            nv_o, g_o, wf_o, wp_o, fc_own, wq_o, wo_o, xn_o, qkv_o, att_o, atto_o, mid_o, par_o,
            fcb_o, lt_o,
        ) = take(15)
        xv, xn, wq, wo, sm, qkv, att, atto, mid, n2, par, qvb, fcb, lt = take(14)
        (
            pack_send, pack_recv, small_send, small_recv, fc_send, fc_recv, local, att_send,
            att_recv, save,
        ) = take(10)
        dp, s = place()
        chip, core = dp // 2, dp % 2
        me = dp * n + s

        x = Walk(x_in, lambda i, c: part(xv, i, tok), take(3))
        out = Walk(out_in, lambda i, c: part(wo, dp * n + i, rows), take(3))
        fc = Walk(fc_own, lambda i, c: wf_o.at[:, c, i], take(5), pair=True)
        proj = Walk(proj_in, lambda i, c: wp_o.at[c, i], take(5), pair=True)
        grads = Spread(g_in, lambda p, c: g_o.at[p], take(2))

        def strip(ref, size):
            return lambda p, c: part(ref, p * 2 + c, size)

        spread_pack = Spread(part(wq, dp, n * rows), strip(wq, n * rows), take(4), pair=True)
        spread_small = Spread(part(sm, dp, n * 16), strip(sm, n * 16), take(4), pair=True)
        spread_out = Spread(part(wo, dp, n * rows), strip(wo, n * rows), take(4), pair=True)
        normed = Spread(n2, lambda p, c: nv_o.at[p], take(2))

        def piece(to, j):
            return (
                qkv_in.at[:, pl.ds(pl.multiple_of(j * depth + to * wide, 128), wide)],
                part(wq, me, rows).at[:, pl.ds(j * wide, wide)],
            )

        shuffles = []
        for k in range(n - 1, 0, -1):
            to = (s + k) % n
            for j in range(3):
                source, target = piece(to, j)
                shuffles.append(
                    remote(source, target, pack_send.at[j, k], pack_recv.at[j, k], (dp, to))
                )
            shuffles.append(
                remote(small_in, part(sm, me, 16), small_send.at[k], small_recv.at[k], (dp, to))
            )

        turns = [
            remote(
                lanes(fc_in, (chip + k) % nc, units), fc_own.at[chip], fc_send.at[k], fc_recv.at[k],
                ((chip + k) % nc * 2 + core, s),
            )
            for k in range(1, nc)
        ]
        keeps = [pltpu.make_async_copy(*piece(s, j), local.at[j]) for j in range(3)] + [
            pltpu.make_async_copy(small_in, part(sm, me, 16), local.at[3]),
            pltpu.make_async_copy(lanes(fc_in, chip, units), fc_own.at[chip], local.at[4]),
        ]
        keep_g = pltpu.make_async_copy(g_in, g_o.at[chip], local.at[5])

        greet_near()
        for copy in shuffles + keeps:
            copy.start()
        x.start()
        out.start()
        for copy in turns:
            copy.start()
        for copy in shuffles + keeps:
            copy.wait()
        spread_pack.start()
        spread_small.start()
        x.step(1)
        out.step(1)
        spread_small.step()
        spread_small.close()
        for size, target, width, at in (
            (rows, par, depth, 0), (bias_own, qvb, 2 * depth, 6), (own_units, fcb, FF, 7)
        ):
            group = 128 // size
            for j in range(width // 128):
                total_tile = widened(sm[pl.ds(j * group * 16, 16)])
                for r in range(1, group):
                    tile = widened(sm[pl.ds((j * group + r) * 16, 16)])
                    total_tile = total_tile + pltpu.roll(tile, r * size, 1)
                target[:, pl.ds(j * 128, 128)] = total_tile
        for k in range(2, n):
            x.step(k)
            out.step(k)
        out.own().wait()
        out.keep = False
        spread_out.start()
        for copy in turns:
            copy.wait()
        fc.start()
        proj.start()
        grads.start()
        keep_g.start()
        spread_pack.step()
        spread_pack.close()
        x.close()
        qv_rows = [
            qvb[6:7, pl.ds(pl.multiple_of(j * depth + s * wide, 128), wide)] for j in range(2)
        ]
        shift = jnp.concatenate([qv_rows[0], jnp.zeros((1, wide), jnp.float32), qv_rows[1]], axis=1)

        def project(i, carry):
            at = pl.ds(pl.multiple_of(i * tok, tok), tok)
            centred, scale = unit_rows(widened(xv[at]))
            normed_one = halved(centred * scale * par[0:1] + par[1:2])
            xn[at] = normed_one
            qkv[at] = halved(matmul(normed_one, wq[...]) + shift)
            return carry

        lax.fori_loop(0, n, project, 0)
        saves = [
            pltpu.make_async_copy(a, b, save.at[i])
            for i, (a, b) in enumerate(
                ((wq, wq_o), (xn, xn_o), (qkv, qkv_o), (par, par_o), (fcb, fcb_o), (att, att_o),
                 (lt, lt_o), (wo, wo_o), (atto, atto_o), (mid, mid_o))
            )
        ]
        for copy in saves[:5]:
            copy.start()

        def att_copy(i):
            k = (i - s + n) % n
            return remote(
                part(att, i, tok), lanes(atto, s, wide), att_send.at[k], att_recv.at[k], (dp, i)
            )

        for i in range(n - 1, -1, -1):
            seen = (i + 1) * tok
            here = pl.ds(i * tok, tok)
            for p in range(wide // 128):
                q2 = qkv[here, pl.ds(p * 128, 128)]
                k2 = qkv[pl.ds(0, seen), pl.ds(wide + p * 128, 128)]
                v2 = qkv[pl.ds(0, seen), pl.ds(2 * wide + p * 128, 128)]
                outs = []
                for h in range(2):
                    probs, log_total = softmax_block(
                        jnp.where(mask_of(h, q2.shape), q2, jnp.zeros_like(q2)), k2, None, i * tok
                    )
                    lt[2 * p + h, here] = log_total
                    outs.append(matmul(halved(probs), v2))
                att[here, pl.ds(p * 128, 128)] = halved(
                    jnp.where(mask_of(0, outs[0].shape), outs[0], outs[1])
                )

            @pl.when(i != s)
            def _():
                att_copy(i).start()

            @pl.when(i == s)
            def _():
                pltpu.make_async_copy(
                    part(att, i, tok), lanes(atto, s, wide), local.at[6]
                ).start()

            if i == n - 1:
                fc.step(1)
            if i == 1:
                proj.step(1)
        for copy in saves[5:7]:
            copy.start()
        spread_out.step()
        spread_out.close()
        saves[7].start()
        pltpu.make_async_copy(part(att, s, tok), lanes(atto, s, wide), local.at[6]).wait()
        for k in range(1, n):
            to = (s + k) % n
            remote(
                part(att, to, tok), lanes(atto, s, wide), att_send.at[k], att_recv.at[k], (dp, to)
            ).wait_send()
            back = (s - k + n) % n
            remote(
                part(att, s, tok), lanes(atto, back, wide), att_send.at[k], att_recv.at[k],
                (dp, back),
            ).wait_recv()
        middle = widened(xv[pl.ds(pl.multiple_of(s * tok, tok), tok)]) + matmul(
            atto[...], wo[...]
        ) + par[2:3]
        mid[...] = middle
        centred, scale = unit_rows(middle)
        n2[...] = halved(centred * scale * par[3:4] + par[4:5])
        normed.start()
        keep_n = pltpu.make_async_copy(n2, nv_o.at[chip], local.at[7])
        keep_n.start()
        for copy in saves[8:]:
            copy.start()
        for k in range(2, n):
            fc.step(k)
            proj.step(k)
        grads.step()
        normed.step()
        out.close()
        fc.close()
        proj.close()
        grads.close()
        normed.close()
        keep_g.wait()
        keep_n.wait()
        for copy in saves:
            copy.wait()

    half = jnp.bfloat16

    def shape(kind, *dims):
        return jax.ShapeDtypeStruct(dims, kind)

    return pl.pallas_call(
        kernel,
        out_shape=[
            shape(half, nc, tok, depth), shape(half, nc, tok, depth),
            shape(half, nc, 2, n, rows, units), shape(half, 2, n, own_units, depth),
            shape(half, nc, rows, units), shape(half, depth, 3 * wide), shape(half, depth, depth),
            shape(half, length, depth), shape(half, length, 3 * wide), shape(half, length, wide),
            shape(half, tok, depth), shape(jnp.float32, tok, depth), shape(jnp.float32, 16, depth),
            shape(jnp.float32, 16, FF), shape(jnp.float32, heads, length, 1),
        ],
        in_specs=[pl.BlockSpec(memory_space=pl.ANY)] * 7,
        out_specs=[pl.BlockSpec(memory_space=pl.ANY)] * 15,
        scratch_shapes=[
            pltpu.VMEM((length, depth), half), pltpu.VMEM((length, depth), half),
            pltpu.VMEM((depth, 3 * wide), half), pltpu.VMEM((depth, depth), half),
            pltpu.VMEM((ranks * 16, 128), half), pltpu.VMEM((length, 3 * wide), half),
            pltpu.VMEM((length, wide), half), pltpu.VMEM((tok, depth), half),
            pltpu.VMEM((tok, depth), jnp.float32), pltpu.VMEM((tok, depth), half),
            pltpu.VMEM((16, depth), jnp.float32), pltpu.VMEM((16, 2 * depth), jnp.float32),
            pltpu.VMEM((16, FF), jnp.float32), pltpu.VMEM((heads, length, 1), jnp.float32),
            dma(3, n), dma(3, n), dma(n), dma(n), dma(nc), dma(nc), dma(8), dma(n), dma(n), dma(10),
            *Walk.scratch(), *Walk.scratch(), *Walk.scratch(True), *Walk.scratch(True),
            *Spread.scratch(), *Spread.scratch(True), *Spread.scratch(True), *Spread.scratch(True),
            *Spread.scratch(),
        ],
        compiler_params=pltpu.CompilerParams(
            collective_id=10, has_side_effects=True, vmem_limit_bytes=48 << 20
        ),
    )(block_input, cotangent, qkv_weight, small, out_weight, fc_weight, proj_weight)


def plain(
    block_input, cotangent, ln1_gain, ln1_bias, qkv_weight, qv_bias, out_weight, out_bias, ln2_gain,
    ln2_bias, fc_weight, fc_bias, proj_weight, proj_bias,
):
    dp, s = place()
    dpc, n = counts()
    nc, ranks = dpc // 2, dpc * n
    core, chip = dp % 2, dp // 2
    tok_rows = block_input.shape[0]
    rows = qkv_weight.shape[0]
    own_units = fc_bias.shape[0]
    units = FF // nc
    heads = H // n
    wide = heads * HD
    length = n * tok_rows
    score_scale = HD ** (-0.5)

    def row_of(value, i):
        return jnp.pad(value[None], ((i, 15 - i), (0, 128 - value.shape[0])))

    parts = (ln1_gain, ln1_bias, out_bias, ln2_gain, ln2_bias, proj_bias, qv_bias, fc_bias)
    small = row_of(parts[0], 0)
    for i in range(1, 8):
        small = small + row_of(parts[i], i)
    pack = qkv_weight
    if wide % 128:
        pack = (
            qkv_weight.reshape(rows, 3, n, wide).transpose(2, 0, 1, 3).reshape(n, rows, 3 * wide)
        )
    x_all, g_all, pack_all, small_all, out_all, fc_all, proj_all = gather_inputs(
        block_input, cotangent, pack, small, out_weight, fc_weight, proj_weight
    )
    stream_seq = widened(x_all.reshape(length, D))
    grad_ff = g_all.reshape(nc * tok_rows, D)
    qkv_cols = pack_all.reshape(D, 3 * wide)
    out_full = out_all.reshape(D, D)
    fc_cols = fc_all.reshape(D, units)
    proj_rows = proj_all.reshape(units, D)
    smalls = small_all.reshape(ranks, 16, 128)
    gain_one, bias_one, out_bias_full, gain_two, bias_two, proj_bias_full = (
        widened(smalls[:, i, :rows].reshape(D)) for i in range(6)
    )
    qv_full = smalls[:, 6, : qv_bias.shape[0]].reshape(2, n, wide)
    qv_own = widened(lax.dynamic_index_in_dim(qv_full, s, 1, keepdims=False))
    fc_bias_cols = widened(
        lax.dynamic_index_in_dim(
            smalls[:, 7, :own_units].reshape(nc, units), chip, 0, keepdims=False
        )
    )

    normed_one = halved(layer_norm(stream_seq, gain_one, bias_one))
    projected = matmul(normed_one, qkv_cols)

    def by_head(values):
        return values.reshape(length, heads, HD).transpose(1, 0, 2)

    def by_token(values):
        return values.transpose(1, 0, 2).reshape(length, wide)

    def side_by_side(own, got):
        return fill(own, got, s).transpose(1, 0, 2).reshape(tok_rows, n * wide)

    queries = by_head(halved(projected[:, :wide] + qv_own[0]))
    keys = by_head(halved(projected[:, wide : 2 * wide]))
    values = by_head(halved(projected[:, 2 * wide :] + qv_own[1]))
    position = jnp.arange(length, dtype=jnp.int32)
    visible = position[None, :] <= position[:, None]
    scores = (
        jnp.einsum("hqd,hkd->hqk", queries, keys, preferred_element_type=jnp.float32) * score_scale
    )
    log_total = jnp.log(
        jnp.sum(jnp.where(visible, jnp.exp(scores), 0.0), axis=-1, keepdims=True)
    )
    probs = jnp.where(visible, jnp.exp(scores - log_total), 0.0)
    shares = halved(probs)
    attended_heads = halved(
        jnp.einsum("hqk,hkd->hqd", shares, values, preferred_element_type=jnp.float32)
    )
    attended = by_token(attended_heads).reshape(n, tok_rows, wide)
    (attended_got,) = run(1, greet_seq, Exchange(attended))
    attended_own = side_by_side(attended, attended_got)
    stream = widened(block_input)
    middle = stream + matmul(attended_own, out_full) + out_bias_full
    normed_two = halved(layer_norm(middle, gain_two, bias_two))
    (normed_all,) = run(2, greet_near, Gather(normed_two))
    normed_ff = normed_all.reshape(nc * tok_rows, D)
    grad_out = widened(cotangent)
    d_proj_bias = jnp.sum(grad_out, axis=0)
    pre_act = matmul(normed_ff, fc_cols) + fc_bias_cols
    hidden = halved(gelu_tanh(pre_act))
    grad_hidden = matmul(grad_ff, proj_rows.T)
    _, gelu_back = jax.vjp(gelu_tanh, pre_act)
    grad_pre = gelu_back(grad_hidden)[0]
    pre_half = halved(grad_pre)
    back_two = halved(matmul(pre_half, fc_cols.T)).reshape(nc, tok_rows, D)
    ff_part = halved(matmul(hidden, proj_rows)).reshape(nc, tok_rows, D)
    d_proj = halved(matmul(hidden.T, grad_ff)).reshape(2, n, own_units, D)
    d_fc = (
        halved(matmul(normed_ff.T, pre_half))
        .reshape(nc, 2, n, rows, units)
        .transpose(1, 2, 0, 3, 4)
    )
    d_fc_bias = jnp.sum(grad_pre, axis=0)
    back_two_got, d_proj_got, d_fc_got = run(
        3, greet_near, Plane(back_two), Partner(d_proj), Partner(d_fc)
    )

    def pair(own, received):
        kept = lax.dynamic_index_in_dim(own, core, 0, keepdims=False)
        return halved(widened(kept) + widened(received))

    _, norm_back_two = jax.vjp(layer_norm, middle, gain_two, bias_two)
    mid_branch, d_ln2_gain, d_ln2_bias = norm_back_two(total(back_two, back_two_got, chip))
    grad_middle = grad_out + mid_branch
    d_out_bias = jnp.sum(grad_middle, axis=0)
    middle_half = halved(grad_middle)
    d_out = (
        halved(matmul(attended_own.T, middle_half))
        .reshape(nc, 2, n * rows, D)
        .transpose(1, 0, 2, 3)
    )
    grad_attended = halved(matmul(middle_half, out_full.T))
    grad_attended = grad_attended.reshape(tok_rows, n, wide).transpose(1, 0, 2)
    d_proj, d_fc = pair(d_proj, d_proj_got), pair(d_fc, d_fc_got)
    grad_att_got, ff_got, d_proj_parts, d_out_got = run(
        4, greet_near, Exchange(grad_attended), Plane(ff_part), Exchange(d_proj), Partner(d_out)
    )
    proj_grad = total(d_proj, d_proj_parts, s)
    output = middle + total(ff_part, ff_got, chip) + proj_bias_full
    grad_att = by_head(fill(grad_attended, grad_att_got, s).reshape(length, wide))
    row_delta = jnp.sum(widened(grad_att) * widened(attended_heads), axis=-1, keepdims=True)
    grad_shares = jnp.einsum("hqd,hkd->hqk", grad_att, values, preferred_element_type=jnp.float32)
    grad_scores = halved(probs * (grad_shares - row_delta))
    grad_q = (
        jnp.einsum("hqk,hkd->hqd", grad_scores, keys, preferred_element_type=jnp.float32)
        * score_scale
    )
    grad_k = (
        jnp.einsum("hqk,hqd->hkd", grad_scores, queries, preferred_element_type=jnp.float32)
        * score_scale
    )
    grad_v = jnp.einsum("hqk,hqd->hkd", shares, grad_att, preferred_element_type=jnp.float32)
    grad_qkv = jnp.concatenate([by_token(grad_q), by_token(grad_k), by_token(grad_v)], axis=1)
    qkv_half = halved(grad_qkv)
    back_one = halved(matmul(qkv_half, qkv_cols.T)).reshape(n, tok_rows, D)
    d_qkv = (
        halved(matmul(normed_one.T, qkv_half))
        .reshape(nc, 2, n * rows, 3 * wide)
        .transpose(1, 0, 2, 3)
    )
    sums = jnp.sum(grad_qkv, axis=0)
    d_qv = jnp.stack([sums[:wide], sums[2 * wide :]])[:, None]
    d_out = pair(d_out, d_out_got)
    back_one_got, d_fc_parts, d_out_parts, d_qkv_got = run(
        5, greet_near, Exchange(back_one), Exchange(d_fc), Plane(d_out), Partner(d_qkv)
    )
    d_qkv = pair(d_qkv, d_qkv_got)
    fc_cut = halved(total(d_fc, d_fc_parts, s))
    out_cut = halved(total(d_out, d_out_parts, chip)).reshape(n, rows, D)
    _, norm_back_one = jax.vjp(layer_norm, stream, gain_one, bias_one)
    stream_branch, d_ln1_gain, d_ln1_bias = norm_back_one(total(back_one, back_one_got, s))
    grad_stream = grad_middle + stream_branch
    turn = jnp.arange(n, dtype=jnp.int32)[None, :, None] == s
    mine = jnp.arange(nc, dtype=jnp.int32)[:, None] == chip
    vectors = jnp.concatenate(
        [
            v.reshape(ranks, rows)
            for v in (d_ln1_gain, d_ln1_bias, d_out_bias, d_ln2_gain, d_ln2_bias, d_proj_bias)
        ]
        + [
            jnp.where(turn, d_qv, 0.0).reshape(ranks, -1),
            jnp.where(mine, d_fc_bias, 0.0).reshape(ranks, own_units),
        ],
        axis=1,
    )
    used = vectors.shape[1]
    vectors = jnp.pad(vectors, ((0, 0), (0, -used % 128))).reshape(ranks, -1, 128)
    d_qkv_parts, fc_got, d_out_last, vectors_got = run(
        6, greet_all, Plane(d_qkv), Plane(fc_cut), Exchange(out_cut), Everyone(vectors)
    )
    fc_grad = widened(fill(fc_cut, fc_got, chip)).transpose(1, 0, 2).reshape(rows, FF)
    out_grad = total(out_cut, d_out_last, s)
    qkv_rows = halved(total(d_qkv, d_qkv_parts, chip)).reshape(n, rows, 3 * wide)
    vector = jnp.sum(fill(vectors, vectors_got, dp * n + s), axis=0).reshape(-1)
    firsts = [vector[i * rows : (i + 1) * rows] for i in range(6)]
    at = 6 * rows
    qv_grad = vector[at : at + qv_bias.shape[0]]
    at += qv_bias.shape[0]
    fc_bias_grad = vector[at : at + own_units]
    (qkv_got,) = run(7, greet_seq, Exchange(qkv_rows))
    qkv_grad = (
        widened(fill(qkv_rows, qkv_got, s))
        .reshape(n, rows, 3, wide)
        .transpose(1, 2, 0, 3)
        .reshape(rows, 3 * D)
    )
    return (
        output, grad_stream, firsts[0], firsts[1], qkv_grad, qv_grad, out_grad, firsts[2],
        firsts[3], firsts[4], fc_grad, fc_bias_grad, proj_grad, firsts[5],
    )


def fused(
    block_input, cotangent, ln1_gain, ln1_bias, qkv_weight, qv_bias, out_weight, out_bias, ln2_gain,
    ln2_bias, fc_weight, fc_bias, proj_weight, proj_bias,
):
    dp, s = place()
    dpc, n = counts()
    nc, ranks = dpc // 2, dpc * n
    core, chip = dp % 2, dp // 2
    tok_rows = block_input.shape[0]
    rows = qkv_weight.shape[0]
    own_units = fc_bias.shape[0]
    units = FF // nc
    heads = H // n
    wide = heads * HD
    length = n * tok_rows
    score_scale = HD ** (-0.5)

    def row_of(value, i):
        return jnp.pad(value[None], ((i, 15 - i), (0, 128 - value.shape[0])))

    parts = (ln1_gain, ln1_bias, out_bias, ln2_gain, ln2_bias, proj_bias, qv_bias, fc_bias)
    small = row_of(parts[0], 0)
    for i in range(1, 8):
        small = small + row_of(parts[i], i)
    (
        normed_all, g_all, fc_all, proj_all, _, qkv_cols, out_full, xn_all, qkv, attended, attended_own,
        middle, par, fcb, _,
    ) = forward(block_input, cotangent, qkv_weight, small, out_weight, fc_weight, proj_weight)
    grad_ff = g_all.reshape(nc * tok_rows, D)
    fc_cols = fc_all.reshape(D, units)
    proj_rows = proj_all.reshape(units, D)
    gain_one, bias_one, out_bias_full, gain_two, bias_two, proj_bias_full = (par[i] for i in range(6))
    fc_bias_cols = lax.dynamic_slice_in_dim(fcb[7], chip * units, units, 0)

    def by_head(values):
        return values.reshape(length, heads, HD).transpose(1, 0, 2)

    def by_token(values):
        return values.transpose(1, 0, 2).reshape(length, wide)

    normed_one = xn_all
    queries, keys, values = (by_head(qkv[:, i * wide : (i + 1) * wide]) for i in range(3))
    attended_heads = by_head(attended)
    position = jnp.arange(length, dtype=jnp.int32)
    visible = position[None, :] <= position[:, None]
    scores = (
        jnp.einsum("hqd,hkd->hqk", queries, keys, preferred_element_type=jnp.float32) * score_scale
    )
    log_total = jnp.log(
        jnp.sum(jnp.where(visible, jnp.exp(scores), 0.0), axis=-1, keepdims=True)
    )
    probs = jnp.where(visible, jnp.exp(scores - log_total), 0.0)
    shares = halved(probs)
    stream = widened(block_input)
    normed_ff = normed_all.reshape(nc * tok_rows, D)
    grad_out = widened(cotangent)
    d_proj_bias = jnp.sum(grad_out, axis=0)
    pre_act = matmul(normed_ff, fc_cols) + fc_bias_cols
    hidden = halved(gelu_tanh(pre_act))
    grad_hidden = matmul(grad_ff, proj_rows.T)
    _, gelu_back = jax.vjp(gelu_tanh, pre_act)
    grad_pre = gelu_back(grad_hidden)[0]
    pre_half = halved(grad_pre)
    back_two = halved(matmul(pre_half, fc_cols.T)).reshape(nc, tok_rows, D)
    ff_part = halved(matmul(hidden, proj_rows)).reshape(nc, tok_rows, D)
    d_proj = halved(matmul(hidden.T, grad_ff)).reshape(2, n, own_units, D)
    d_fc = (
        halved(matmul(normed_ff.T, pre_half))
        .reshape(nc, 2, n, rows, units)
        .transpose(1, 2, 0, 3, 4)
    )
    d_fc_bias = jnp.sum(grad_pre, axis=0)
    back_two_got, d_proj_got, d_fc_got = run(
        3, greet_near, Plane(back_two), Partner(d_proj), Partner(d_fc)
    )

    def pair(own, received):
        kept = lax.dynamic_index_in_dim(own, core, 0, keepdims=False)
        return halved(widened(kept) + widened(received))

    _, norm_back_two = jax.vjp(layer_norm, middle, gain_two, bias_two)
    mid_branch, d_ln2_gain, d_ln2_bias = norm_back_two(total(back_two, back_two_got, chip))
    grad_middle = grad_out + mid_branch
    d_out_bias = jnp.sum(grad_middle, axis=0)
    middle_half = halved(grad_middle)
    d_out = (
        halved(matmul(attended_own.T, middle_half))
        .reshape(nc, 2, n * rows, D)
        .transpose(1, 0, 2, 3)
    )
    grad_attended = halved(matmul(middle_half, out_full.T))
    grad_attended = grad_attended.reshape(tok_rows, n, wide).transpose(1, 0, 2)
    d_proj, d_fc = pair(d_proj, d_proj_got), pair(d_fc, d_fc_got)
    grad_att_got, ff_got, d_proj_parts, d_out_got = run(
        4, greet_near, Exchange(grad_attended), Plane(ff_part), Exchange(d_proj), Partner(d_out)
    )
    proj_grad = total(d_proj, d_proj_parts, s)
    output = middle + total(ff_part, ff_got, chip) + proj_bias_full
    grad_att = by_head(fill(grad_attended, grad_att_got, s).reshape(length, wide))
    row_delta = jnp.sum(widened(grad_att) * widened(attended_heads), axis=-1, keepdims=True)
    grad_shares = jnp.einsum("hqd,hkd->hqk", grad_att, values, preferred_element_type=jnp.float32)
    grad_scores = halved(probs * (grad_shares - row_delta))
    grad_q = (
        jnp.einsum("hqk,hkd->hqd", grad_scores, keys, preferred_element_type=jnp.float32)
        * score_scale
    )
    grad_k = (
        jnp.einsum("hqk,hqd->hkd", grad_scores, queries, preferred_element_type=jnp.float32)
        * score_scale
    )
    grad_v = jnp.einsum("hqk,hqd->hkd", shares, grad_att, preferred_element_type=jnp.float32)
    grad_qkv = jnp.concatenate([by_token(grad_q), by_token(grad_k), by_token(grad_v)], axis=1)
    qkv_half = halved(grad_qkv)
    back_one = halved(matmul(qkv_half, qkv_cols.T)).reshape(n, tok_rows, D)
    d_qkv = (
        halved(matmul(normed_one.T, qkv_half))
        .reshape(nc, 2, n * rows, 3 * wide)
        .transpose(1, 0, 2, 3)
    )
    sums = jnp.sum(grad_qkv, axis=0)
    d_qv = jnp.stack([sums[:wide], sums[2 * wide :]])[:, None]
    d_out = pair(d_out, d_out_got)
    back_one_got, d_fc_parts, d_out_parts, d_qkv_got = run(
        5, greet_near, Exchange(back_one), Exchange(d_fc), Plane(d_out), Partner(d_qkv)
    )
    d_qkv = pair(d_qkv, d_qkv_got)
    fc_cut = halved(total(d_fc, d_fc_parts, s))
    out_cut = halved(total(d_out, d_out_parts, chip)).reshape(n, rows, D)
    _, norm_back_one = jax.vjp(layer_norm, stream, gain_one, bias_one)
    stream_branch, d_ln1_gain, d_ln1_bias = norm_back_one(total(back_one, back_one_got, s))
    grad_stream = grad_middle + stream_branch
    turn = jnp.arange(n, dtype=jnp.int32)[None, :, None] == s
    mine = jnp.arange(nc, dtype=jnp.int32)[:, None] == chip
    vectors = jnp.concatenate(
        [
            v.reshape(ranks, rows)
            for v in (d_ln1_gain, d_ln1_bias, d_out_bias, d_ln2_gain, d_ln2_bias, d_proj_bias)
        ]
        + [
            jnp.where(turn, d_qv, 0.0).reshape(ranks, -1),
            jnp.where(mine, d_fc_bias, 0.0).reshape(ranks, own_units),
        ],
        axis=1,
    )
    used = vectors.shape[1]
    vectors = jnp.pad(vectors, ((0, 0), (0, -used % 128))).reshape(ranks, -1, 128)
    d_qkv_parts, fc_got, d_out_last, vectors_got = run(
        6, greet_all, Plane(d_qkv), Plane(fc_cut), Exchange(out_cut), Everyone(vectors)
    )
    fc_grad = widened(fill(fc_cut, fc_got, chip)).transpose(1, 0, 2).reshape(rows, FF)
    out_grad = total(out_cut, d_out_last, s)
    qkv_rows = halved(total(d_qkv, d_qkv_parts, chip)).reshape(n, rows, 3 * wide)
    vector = jnp.sum(fill(vectors, vectors_got, dp * n + s), axis=0).reshape(-1)
    firsts = [vector[i * rows : (i + 1) * rows] for i in range(6)]
    at = 6 * rows
    qv_grad = vector[at : at + qv_bias.shape[0]]
    at += qv_bias.shape[0]
    fc_bias_grad = vector[at : at + own_units]
    (qkv_got,) = run(7, greet_seq, Exchange(qkv_rows))
    qkv_grad = (
        widened(fill(qkv_rows, qkv_got, s))
        .reshape(n, rows, 3, wide)
        .transpose(1, 2, 0, 3)
        .reshape(rows, 3 * D)
    )
    return (
        output, grad_stream, firsts[0], firsts[1], qkv_grad, qv_grad, out_grad, firsts[2],
        firsts[3], firsts[4], fc_grad, fc_bias_grad, proj_grad, firsts[5],
    )


def local(*arrays):
    _, n = counts()
    fits = (D // n) % 128 == 0 and arrays[4].shape[0] % 16 == 0 and arrays[0].shape[0] % 128 == 0
    return fused(*arrays) if fits else plain(*arrays)


def solution(mesh):
    in_specs = (
        P(("dp", "seq"), None),
        P(("dp", "seq"), None),
        P(("dp", "seq")),
        P(("dp", "seq")),
        P(("dp", "seq"), None),
        P(("dp", "seq")),
        P(("dp", "seq"), None),
        P(("dp", "seq")),
        P(("dp", "seq")),
        P(("dp", "seq")),
        P(("dp", "seq"), None),
        P(("dp", "seq")),
        P(("dp", "seq"), None),
        P(("dp", "seq")),
    )
    out_specs = (
        P(("dp", "seq"), None),
        P(("dp", "seq"), None),
        P(("dp", "seq")),
        P(("dp", "seq")),
        P(("dp", "seq"), None),
        P(("dp", "seq")),
        P(("dp", "seq"), None),
        P(("dp", "seq")),
        P(("dp", "seq")),
        P(("dp", "seq")),
        P(("dp", "seq"), None),
        P(("dp", "seq")),
        P(("dp", "seq"), None),
        P(("dp", "seq")),
    )
    return jax.shard_map(local, mesh=mesh, in_specs=in_specs, out_specs=out_specs, check_vma=False)
```

```python
import math

import jax
import jax.numpy as jnp
from jax import lax
from jax.experimental import pallas as pl
from jax.experimental.pallas import tpu as pltpu
from jax.sharding import PartitionSpec as P

D = 1024
H = 16
HD = 64
FF = 4096


EPS = 1e-05
GELU_COEF = math.sqrt(2.0 / math.pi)
MESH = pl.DeviceIdType.MESH


def layer_norm(values, norm_gain, offset):
    center = jnp.mean(values, axis=-1, keepdims=True)
    centred = values - center
    spread = jnp.mean(centred * centred, axis=-1, keepdims=True)
    return centred * lax.rsqrt(spread + EPS) * norm_gain + offset


def gelu_tanh(pre_act):
    return (
        0.5
        * pre_act
        * (1.0 + jnp.tanh(GELU_COEF * (pre_act + 0.044715 * pre_act * pre_act * pre_act)))
    )


def halved(values):
    return values.astype(jnp.bfloat16)


def widened(values):
    return values.astype(jnp.float32)


def matmul(left, right):
    return jnp.dot(left, right, preferred_element_type=jnp.float32)


def place():
    return lax.axis_index("dp"), lax.axis_index("seq")


def counts():
    return lax.axis_size("dp"), lax.axis_size("seq")


def remote(src, dst, send, recv, device):
    return pltpu.make_async_remote_copy(
        src_ref=src, dst_ref=dst, send_sem=send, recv_sem=recv, device_id=device, device_id_type=MESH
    )


def dma(*shape):
    return pltpu.SemaphoreType.DMA(shape)


def greet_all():
    dp, s = place()
    dpc, n = counts()
    barrier = pltpu.get_barrier_semaphore()

    def greet(i, carry):
        @pl.when(i != dp * n + s)
        def _():
            pl.semaphore_signal(barrier, inc=1, device_id=(i // n, i % n), device_id_type=MESH)

        return carry

    lax.fori_loop(0, dpc * n, greet, 0)
    pl.semaphore_wait(barrier, dpc * n - 1)


def greet_near():
    dp, s = place()
    dpc, n = counts()
    nc = dpc // 2
    barrier = pltpu.get_barrier_semaphore()
    for k in range(1, n):
        pl.semaphore_signal(barrier, inc=1, device_id=(dp, (s + k) % n), device_id_type=MESH)
    for k in range(1, nc):
        pl.semaphore_signal(barrier, inc=1, device_id=((dp + 2 * k) % dpc, s), device_id_type=MESH)
    pl.semaphore_signal(barrier, inc=1, device_id=(other_core(dp), s), device_id_type=MESH)
    pl.semaphore_wait(barrier, n - 1 + nc)


def greet_seq():
    dp, s = place()
    _, n = counts()
    barrier = pltpu.get_barrier_semaphore()
    for k in range(1, n):
        pl.semaphore_signal(barrier, inc=1, device_id=(dp, (s + k) % n), device_id_type=MESH)
    pl.semaphore_wait(barrier, n - 1)


def other_core(dp):
    return dp + 1 - 2 * (dp % 2)


class Exchange:
    def __init__(self, value):
        _, n = counts()
        self.operands = (value,)
        self.outs = (value,)
        self.sems = (dma(n), dma(n))

    def copies(self, ins, outs, sems):
        dp, s = place()
        _, n = counts()
        return [
            remote(
                ins[0].at[(s + k) % n], outs[0].at[s], sems[0].at[k], sems[1].at[k], (dp, (s + k) % n)
            )
            for k in range(n - 1, 0, -1)
        ]

    def start(self, ins, outs, sems):
        for copy in self.copies(ins, outs, sems):
            copy.start()

    def finish(self, ins, outs, sems):
        for copy in self.copies(ins, outs, sems):
            copy.wait()


class Plane(Exchange):
    def __init__(self, value):
        dpc, _ = counts()
        self.operands = (value,)
        self.outs = (value,)
        self.sems = (dma(dpc // 2), dma(dpc // 2))

    def copies(self, ins, outs, sems):
        dp, s = place()
        dpc, _ = counts()
        chip, core, nc = dp // 2, dp % 2, dpc // 2
        return [
            remote(
                ins[0].at[(chip + k) % nc],
                outs[0].at[chip],
                sems[0].at[k],
                sems[1].at[k],
                ((chip + k) % nc * 2 + core, s),
            )
            for k in range(1, nc)
        ]


class Partner(Exchange):
    def __init__(self, value):
        self.operands = (value,)
        self.outs = (jax.ShapeDtypeStruct(value.shape[1:], value.dtype),)
        self.sems = (dma(1), dma(1))

    def copies(self, ins, outs, sems):
        dp, s = place()
        return [
            remote(
                ins[0].at[1 - dp % 2], outs[0], sems[0].at[0], sems[1].at[0], (other_core(dp), s)
            )
        ]


class Everyone:
    def __init__(self, value):
        dpc, n = counts()
        self.operands = (value,)
        self.outs = (value,)
        self.sems = (dma(dpc * n), dma(dpc * n))

    def copy(self, ins, outs, sems, k):
        dp, s = place()
        dpc, n = counts()
        me = dp * n + s
        peer = (me + k) % (dpc * n)
        return remote(
            ins[0].at[peer], outs[0].at[me], sems[0].at[k], sems[1].at[k], (peer // n, peer % n)
        )

    def start(self, ins, outs, sems):
        def step(k, carry):
            self.copy(ins, outs, sems, k).start()
            return carry

        lax.fori_loop(1, self.outs[0].shape[0], step, 0)

    def finish(self, ins, outs, sems):
        def step(k, carry):
            self.copy(ins, outs, sems, k).wait()
            return carry

        lax.fori_loop(1, self.outs[0].shape[0], step, 0)


class Walk:
    def __init__(self, source, block, sems, pair=False, keep=True):
        self.source, self.block, self.sems, self.pair, self.keep = source, block, sems, pair, keep

    @staticmethod
    def scratch(pair=False):
        _, n = counts()
        return (dma(2, n), dma(2, n), dma(1)) + ((dma(2, n), dma(2, n)) if pair else ())

    def hand_on(self, way, k):
        dp, s = place()
        sign = 1 - 2 * way
        block = self.block(s - sign * k, dp % 2)
        return remote(
            self.source if k == 0 else block, block,
            self.sems[0].at[way, k], self.sems[1].at[way, k], (dp, s + sign),
        )

    def over(self, way, k, core):
        dp, s = place()
        block = self.block(s - (1 - 2 * way) * k, core)
        return remote(
            self.source if k == 0 else block, block,
            self.sems[3].at[way, k], self.sems[4].at[way, k], (other_core(dp), s),
        )

    def own(self):
        dp, s = place()
        return pltpu.make_async_copy(self.source, self.block(s, dp % 2), self.sems[2].at[0])

    def guard(self, way, k):
        _, s = place()
        _, n = counts()
        return (s >= k) if way == 0 else (s < n - k)

    def follows(self, way):
        _, s = place()
        _, n = counts()
        return (s < n - 1) if way == 0 else (s > 0)

    def start(self):
        dp, _ = place()
        for way in (0, 1):

            @pl.when(self.follows(way))
            def _():
                self.hand_on(way, 0).start()

        if self.keep:
            self.own().start()
        if self.pair:
            self.over(0, 0, dp % 2).start()

    def step(self, k):
        dp, s = place()
        _, n = counts()
        for way in (0, 1):
            sign = 1 - 2 * way

            @pl.when(self.guard(way, k))
            def _():
                block = self.block(s - sign * k, dp % 2)
                remote(
                    block, block, self.sems[0].at[way, k - 1], self.sems[1].at[way, k - 1],
                    (dp, s - sign),
                ).wait_recv()
                if k < n - 1:

                    @pl.when(self.follows(way))
                    def _():
                        self.hand_on(way, k).start()

                if self.pair:
                    self.over(way, k, dp % 2).start()

    def close(self):
        dp, _ = place()
        _, n = counts()
        for way in (0, 1):
            for k in range(n - 1):

                @pl.when(jnp.logical_and(self.follows(way), self.guard(way, k)))
                def _():
                    self.hand_on(way, k).wait_send()

        if self.keep:
            self.own().wait()
        if self.pair:
            self.over(0, 0, dp % 2).wait_send()
            self.over(0, 0, 1 - dp % 2).wait_recv()
            for way in (0, 1):
                for k in range(1, n):

                    @pl.when(self.guard(way, k))
                    def _():
                        self.over(way, k, dp % 2).wait_send()
                        self.over(way, k, 1 - dp % 2).wait_recv()


class Spread:
    def __init__(self, source, block, sems, pair=False):
        self.source, self.block, self.sems, self.pair = source, block, sems, pair

    @staticmethod
    def scratch(pair=False):
        dpc, _ = counts()
        nc = dpc // 2
        return (dma(nc), dma(nc)) + ((dma(nc), dma(nc)) if pair else ())

    def to_chips(self):
        dp, s = place()
        dpc, _ = counts()
        nc = dpc // 2
        return [
            remote(
                self.source, self.block(dp // 2, dp % 2), self.sems[0].at[k], self.sems[1].at[k],
                ((dp // 2 + k) % nc * 2 + dp % 2, s),
            )
            for k in range(1, nc)
        ]

    def over(self, k, core):
        dp, s = place()
        dpc, _ = counts()
        nc = dpc // 2
        block = self.block((dp // 2 - k + nc) % nc, core)
        return remote(
            self.source if k == 0 else block, block, self.sems[2].at[k], self.sems[3].at[k],
            (other_core(dp), s),
        )

    def start(self):
        dp, _ = place()
        for copy in self.to_chips():
            copy.start()
        if self.pair:
            self.over(0, dp % 2).start()

    def step(self):
        dp, s = place()
        dpc, _ = counts()
        nc = dpc // 2
        for k in range(1, nc):
            chip = (dp // 2 - k + nc) % nc
            block = self.block(chip, dp % 2)
            remote(
                block, block, self.sems[0].at[k], self.sems[1].at[k], (chip * 2 + dp % 2, s)
            ).wait_recv()
            if self.pair:
                self.over(k, dp % 2).start()

    def close(self):
        dp, _ = place()
        dpc, _ = counts()
        for copy in self.to_chips():
            copy.wait_send()
        if self.pair:
            for k in range(dpc // 2):
                self.over(k, dp % 2).wait_send()
                self.over(k, 1 - dp % 2).wait_recv()


class Gather:
    def __init__(self, value):
        dpc, _ = counts()
        self.operands = (value,)
        self.outs = (jax.ShapeDtypeStruct((dpc // 2,) + value.shape, value.dtype),)
        self.sems = Spread.scratch() + (dma(1),)

    def spread(self, ins, outs, sems):
        return Spread(ins[0], lambda chip, core: outs[0].at[chip], sems)

    def own(self, ins, outs, sems):
        dp, _ = place()
        return pltpu.make_async_copy(ins[0], outs[0].at[dp // 2], sems[2].at[0])

    def start(self, ins, outs, sems):
        self.spread(ins, outs, sems).start()
        self.own(ins, outs, sems).start()

    def finish(self, ins, outs, sems):
        self.spread(ins, outs, sems).step()
        self.spread(ins, outs, sems).close()
        self.own(ins, outs, sems).wait()


def run(number, greet, *tasks):
    spans = []
    a = b = c = 0
    for task in tasks:
        spans.append((a, b, c))
        a += len(task.operands)
        b += len(task.outs)
        c += len(task.sems)
    n_in, n_out = a, b

    def kernel(*refs):
        ins, outs, sems = refs[:n_in], refs[n_in : n_in + n_out], refs[n_in + n_out :]
        greet()
        views = [
            (
                ins[i : i + len(t.operands)],
                outs[o : o + len(t.outs)],
                sems[m : m + len(t.sems)],
            )
            for t, (i, o, m) in zip(tasks, spans)
        ]
        for t, view in zip(tasks, views):
            t.start(*view)
        for t, view in zip(tasks, views):
            t.finish(*view)

    return pl.pallas_call(
        kernel,
        out_shape=[jax.ShapeDtypeStruct(o.shape, o.dtype) for t in tasks for o in t.outs],
        in_specs=[pl.BlockSpec(memory_space=pl.ANY)] * n_in,
        out_specs=[pl.BlockSpec(memory_space=pl.ANY)] * n_out,
        scratch_shapes=[s for t in tasks for s in t.sems],
        compiler_params=pltpu.CompilerParams(collective_id=number, has_side_effects=True),
    )(*[v for t in tasks for v in t.operands])


def gather_inputs(block_input, cotangent, pack, small, out_rows, fc_rows, proj_rows):
    dpc, n = counts()
    nc = dpc // 2
    units = fc_rows.shape[1] // nc
    whole = pack.ndim == 2
    wide = block_input.shape[1] // n
    pieces = 3 if whole else 1
    rows = out_rows.shape[0]

    def kernel(
        x_in, g_in, pack_in, small_in, out_in, fc_in, proj_in,
        x_all, g_all, pack_all, small_all, out_all, fc_all, proj_all, fc_own, *sems,
    ):
        dp, s = place()
        chip, core = dp // 2, dp % 2

        def take(count):
            nonlocal sems
            head, sems = sems[:count], sems[count:]
            return head

        pack_send, pack_recv, small_send, small_recv, fc_send, fc_recv, local = take(7)
        x = Walk(x_in, lambda i, c: x_all.at[i], take(3))
        out = Walk(out_in, lambda i, c: out_all.at[dp, i], take(3))
        fc = Walk(fc_own, lambda i, c: fc_all.at[:, c, i], take(5), pair=True)
        proj = Walk(proj_in, lambda i, c: proj_all.at[c, i], take(5), pair=True)
        grads = Spread(g_in, lambda p, c: g_all.at[p], take(2))
        spread_pack = Spread(pack_all.at[dp], lambda p, c: pack_all.at[p * 2 + c], take(4), pair=True)
        spread_small = Spread(small_all.at[dp], lambda p, c: small_all.at[p * 2 + c], take(4), pair=True)
        spread_out = Spread(out_all.at[dp], lambda p, c: out_all.at[p * 2 + c], take(4), pair=True)

        def piece(to, j):
            if whole:
                source = pack_in.at[:, pl.ds(pl.multiple_of(j * n * wide + to * wide, 128), wide)]
                return source, pack_all.at[dp, s, :, pl.ds(j * wide, wide)]
            return pack_in.at[to], pack_all.at[dp, s]

        shuffles = []
        for k in range(n - 1, 0, -1):
            to = (s + k) % n
            for j in range(pieces):
                source, target = piece(to, j)
                shuffles.append(
                    remote(source, target, pack_send.at[j, k], pack_recv.at[j, k], (dp, to))
                )
            shuffles.append(
                remote(small_in, small_all.at[dp, s], small_send.at[k], small_recv.at[k], (dp, to))
            )

        def cut(to):
            return fc_in.at[:, pl.ds(pl.multiple_of(to * units, 128), units)]

        turns = [
            remote(
                cut((chip + k) % nc), fc_own.at[chip], fc_send.at[k], fc_recv.at[k],
                ((chip + k) % nc * 2 + core, s),
            )
            for k in range(1, nc)
        ]
        keeps = [
            pltpu.make_async_copy(*piece(s, j), local.at[j]) for j in range(pieces)
        ] + [
            pltpu.make_async_copy(small_in, small_all.at[dp, s], local.at[3]),
            pltpu.make_async_copy(cut(chip), fc_own.at[chip], local.at[4]),
        ]
        keep_g = pltpu.make_async_copy(g_in, g_all.at[chip], local.at[5])

        greet_near()
        for copy in shuffles + keeps:
            copy.start()
        x.start()
        out.start()
        for copy in turns:
            copy.start()
        for copy in shuffles + keeps:
            copy.wait()
        spread_pack.start()
        spread_small.start()
        grads.start()
        keep_g.start()
        for k in range(1, n):
            x.step(k)
            out.step(k)
        out.own().wait()
        spread_out.start()
        for copy in turns:
            copy.wait()
        fc.start()
        proj.start()
        spread_pack.step()
        spread_small.step()
        for k in range(1, n):
            fc.step(k)
            proj.step(k)
        spread_out.step()
        grads.step()
        x.close()
        out.keep = False
        out.close()
        fc.close()
        proj.close()
        for spread in (spread_pack, spread_small, spread_out, grads):
            spread.close()
        keep_g.wait()

    def grown(value, *lead):
        return jax.ShapeDtypeStruct(lead, value.dtype)

    depth = block_input.shape[1]
    return pl.pallas_call(
        kernel,
        out_shape=[
            grown(block_input, n, *block_input.shape), grown(cotangent, nc, *cotangent.shape),
            grown(pack, dpc, n, rows, 3 * wide), grown(small, dpc, n, *small.shape),
            grown(out_rows, dpc, n, *out_rows.shape), grown(fc_rows, nc, 2, n, rows, units),
            grown(proj_rows, 2, n, *proj_rows.shape), grown(fc_rows, nc, rows, units),
        ],
        in_specs=[pl.BlockSpec(memory_space=pl.ANY)] * 7,
        out_specs=[pl.BlockSpec(memory_space=pl.ANY)] * 8,
        scratch_shapes=[
            dma(pieces, n), dma(pieces, n), dma(n), dma(n), dma(nc), dma(nc), dma(6),
            *Walk.scratch(), *Walk.scratch(), *Walk.scratch(True), *Walk.scratch(True),
            *Spread.scratch(), *Spread.scratch(True), *Spread.scratch(True), *Spread.scratch(True),
        ],
        compiler_params=pltpu.CompilerParams(collective_id=0, has_side_effects=True),
    )(block_input, cotangent, pack, small, out_rows, fc_rows, proj_rows)[:7]


def total(own, received, mine):
    picked = [
        jnp.where(k == mine, widened(own[k]), widened(received[k])) for k in range(own.shape[0])
    ]
    result = picked[0]
    for value in picked[1:]:
        result = result + value
    return result


def fill(own, received, mine):
    slots = lax.broadcasted_iota(jnp.int32, (own.shape[0],) + (1,) * (own.ndim - 1), 0)
    return jnp.where(slots == mine, own, received)


def mask_of(half, shape):
    lane = lax.broadcasted_iota(jnp.int32, shape, len(shape) - 1)
    return (lane // HD) % 2 == half


def contract(left, right, dims):
    return lax.dot_general(
        left, right, ((dims[:1], dims[1:]), ((), ())), preferred_element_type=jnp.float32
    )


def unit_rows(values):
    center = jnp.mean(values, axis=-1, keepdims=True)
    centred = values - center
    spread = jnp.mean(centred * centred, axis=-1, keepdims=True)
    return centred, lax.rsqrt(spread + EPS)


def part(ref, i, size):
    return ref.at[pl.ds(pl.multiple_of(i * size, size), size)]


def lanes(ref, i, size):
    return ref.at[:, pl.ds(pl.multiple_of(i * size, size), size)]


def softmax_block(q_masked, k, log_total, diagonal):
    scores = contract(q_masked, k, (1, 1)) * HD ** (-0.5)
    row = lax.broadcasted_iota(jnp.int32, scores.shape, 0) + diagonal
    visible = lax.broadcasted_iota(jnp.int32, scores.shape, 1) <= row
    if log_total is None:
        log_total = jnp.log(
            jnp.sum(jnp.where(visible, jnp.exp(scores), 0.0), axis=-1, keepdims=True)
        )
    return jnp.where(visible, jnp.exp(scores - log_total), 0.0), log_total


def forward(block_input, cotangent, qkv_weight, small, out_weight, fc_weight, proj_weight):
    dpc, n = counts()
    nc, ranks = dpc // 2, dpc * n
    tok, depth = block_input.shape
    rows, units, own_units = out_weight.shape[0], fc_weight.shape[1] // nc, proj_weight.shape[0]
    wide, length = depth // n, n * tok
    heads = wide // HD
    bias_own = 2 * depth // ranks

    def kernel(*refs):
        refs = list(refs)

        def take(count):
            head = refs[:count]
            del refs[:count]
            return head

        x_in, g_in, qkv_in, small_in, out_in, fc_in, proj_in = take(7)
        (
            nv_o, g_o, wf_o, wp_o, fc_own, wq_o, wo_o, xn_o, qkv_o, att_o, atto_o, mid_o, par_o,
            fcb_o, lt_o,
        ) = take(15)
        xv, xn, wq, wo, sm, qkv, att, atto, mid, n2, par, qvb, fcb, lt = take(14)
        (
            pack_send, pack_recv, small_send, small_recv, fc_send, fc_recv, local, att_send,
            att_recv, save,
        ) = take(10)
        dp, s = place()
        chip, core = dp // 2, dp % 2
        me = dp * n + s

        x = Walk(x_in, lambda i, c: part(xv, i, tok), take(3))
        out = Walk(out_in, lambda i, c: part(wo, dp * n + i, rows), take(3))
        fc = Walk(fc_own, lambda i, c: wf_o.at[:, c, i], take(5), pair=True)
        proj = Walk(proj_in, lambda i, c: wp_o.at[c, i], take(5), pair=True)
        grads = Spread(g_in, lambda p, c: g_o.at[p], take(2))

        def strip(ref, size):
            return lambda p, c: part(ref, p * 2 + c, size)

        spread_pack = Spread(part(wq, dp, n * rows), strip(wq, n * rows), take(4), pair=True)
        spread_small = Spread(part(sm, dp, n * 16), strip(sm, n * 16), take(4), pair=True)
        spread_out = Spread(part(wo, dp, n * rows), strip(wo, n * rows), take(4), pair=True)
        normed = Spread(n2, lambda p, c: nv_o.at[p], take(2))

        def piece(to, j):
            return (
                qkv_in.at[:, pl.ds(pl.multiple_of(j * depth + to * wide, 128), wide)],
                part(wq, me, rows).at[:, pl.ds(j * wide, wide)],
            )

        shuffles = []
        for k in range(n - 1, 0, -1):
            to = (s + k) % n
            for j in range(3):
                source, target = piece(to, j)
                shuffles.append(
                    remote(source, target, pack_send.at[j, k], pack_recv.at[j, k], (dp, to))
                )
            shuffles.append(
                remote(small_in, part(sm, me, 16), small_send.at[k], small_recv.at[k], (dp, to))
            )

        turns = [
            remote(
                lanes(fc_in, (chip + k) % nc, units), fc_own.at[chip], fc_send.at[k], fc_recv.at[k],
                ((chip + k) % nc * 2 + core, s),
            )
            for k in range(1, nc)
        ]
        keeps = [pltpu.make_async_copy(*piece(s, j), local.at[j]) for j in range(3)] + [
            pltpu.make_async_copy(small_in, part(sm, me, 16), local.at[3]),
            pltpu.make_async_copy(lanes(fc_in, chip, units), fc_own.at[chip], local.at[4]),
        ]
        keep_g = pltpu.make_async_copy(g_in, g_o.at[chip], local.at[5])

        greet_near()
        for copy in shuffles + keeps:
            copy.start()
        x.start()
        out.start()
        for copy in turns:
            copy.start()
        for copy in shuffles + keeps:
            copy.wait()
        spread_pack.start()
        spread_small.start()
        x.step(1)
        out.step(1)
        spread_small.step()
        spread_small.close()
        for size, target, width, at in (
            (rows, par, depth, 0), (bias_own, qvb, 2 * depth, 6), (own_units, fcb, FF, 7)
        ):
            group = 128 // size
            for j in range(width // 128):
                total_tile = widened(sm[pl.ds(j * group * 16, 16)])
                for r in range(1, group):
                    tile = widened(sm[pl.ds((j * group + r) * 16, 16)])
                    total_tile = total_tile + pltpu.roll(tile, r * size, 1)
                target[:, pl.ds(j * 128, 128)] = total_tile
        for k in range(2, n):
            x.step(k)
            out.step(k)
        out.own().wait()
        out.keep = False
        spread_out.start()
        for copy in turns:
            copy.wait()
        fc.start()
        proj.start()
        grads.start()
        keep_g.start()
        spread_pack.step()
        spread_pack.close()
        x.close()
        qv_rows = [
            qvb[6:7, pl.ds(pl.multiple_of(j * depth + s * wide, 128), wide)] for j in range(2)
        ]
        shift = jnp.concatenate([qv_rows[0], jnp.zeros((1, wide), jnp.float32), qv_rows[1]], axis=1)

        def project(i, carry):
            at = pl.ds(pl.multiple_of(i * tok, tok), tok)
            centred, scale = unit_rows(widened(xv[at]))
            normed_one = halved(centred * scale * par[0:1] + par[1:2])
            xn[at] = normed_one
            qkv[at] = halved(matmul(normed_one, wq[...]) + shift)
            return carry

        lax.fori_loop(0, n, project, 0)
        saves = [
            pltpu.make_async_copy(a, b, save.at[i])
            for i, (a, b) in enumerate(
                ((wq, wq_o), (xn, xn_o), (qkv, qkv_o), (par, par_o), (fcb, fcb_o), (att, att_o),
                 (lt, lt_o), (wo, wo_o), (atto, atto_o), (mid, mid_o))
            )
        ]
        for copy in saves[:5]:
            copy.start()

        def att_copy(i):
            k = (i - s + n) % n
            return remote(
                part(att, i, tok), lanes(atto, s, wide), att_send.at[k], att_recv.at[k], (dp, i)
            )

        for i in range(n - 1, -1, -1):
            seen = (i + 1) * tok
            here = pl.ds(i * tok, tok)
            for p in range(wide // 128):
                q2 = qkv[here, pl.ds(p * 128, 128)]
                k2 = qkv[pl.ds(0, seen), pl.ds(wide + p * 128, 128)]
                v2 = qkv[pl.ds(0, seen), pl.ds(2 * wide + p * 128, 128)]
                outs = []
                for h in range(2):
                    probs, log_total = softmax_block(
                        jnp.where(mask_of(h, q2.shape), q2, jnp.zeros_like(q2)), k2, None, i * tok
                    )
                    lt[2 * p + h, here] = log_total
                    outs.append(matmul(halved(probs), v2))
                att[here, pl.ds(p * 128, 128)] = halved(
                    jnp.where(mask_of(0, outs[0].shape), outs[0], outs[1])
                )

            @pl.when(i != s)
            def _():
                att_copy(i).start()

            @pl.when(i == s)
            def _():
                pltpu.make_async_copy(
                    part(att, i, tok), lanes(atto, s, wide), local.at[6]
                ).start()

            if i == n - 1:
                fc.step(1)
            if i == 1:
                proj.step(1)
        for copy in saves[5:7]:
            copy.start()
        spread_out.step()
        spread_out.close()
        saves[7].start()
        pltpu.make_async_copy(part(att, s, tok), lanes(atto, s, wide), local.at[6]).wait()
        for k in range(1, n):
            to = (s + k) % n
            remote(
                part(att, to, tok), lanes(atto, s, wide), att_send.at[k], att_recv.at[k], (dp, to)
            ).wait_send()
            back = (s - k + n) % n
            remote(
                part(att, s, tok), lanes(atto, back, wide), att_send.at[k], att_recv.at[k],
                (dp, back),
            ).wait_recv()
        middle = widened(xv[pl.ds(pl.multiple_of(s * tok, tok), tok)]) + matmul(
            atto[...], wo[...]
        ) + par[2:3]
        mid[...] = middle
        centred, scale = unit_rows(middle)
        n2[...] = halved(centred * scale * par[3:4] + par[4:5])
        normed.start()
        keep_n = pltpu.make_async_copy(n2, nv_o.at[chip], local.at[7])
        keep_n.start()
        for copy in saves[8:]:
            copy.start()
        for k in range(2, n):
            fc.step(k)
            proj.step(k)
        grads.step()
        normed.step()
        out.close()
        fc.close()
        proj.close()
        grads.close()
        normed.close()
        keep_g.wait()
        keep_n.wait()
        for copy in saves:
            copy.wait()

    half = jnp.bfloat16

    def shape(kind, *dims):
        return jax.ShapeDtypeStruct(dims, kind)

    return pl.pallas_call(
        kernel,
        out_shape=[
            shape(half, nc, tok, depth), shape(half, nc, tok, depth),
            shape(half, nc, 2, n, rows, units), shape(half, 2, n, own_units, depth),
            shape(half, nc, rows, units), shape(half, depth, 3 * wide), shape(half, depth, depth),
            shape(half, length, depth), shape(half, length, 3 * wide), shape(half, length, wide),
            shape(half, tok, depth), shape(jnp.float32, tok, depth), shape(jnp.float32, 16, depth),
            shape(jnp.float32, 16, FF), shape(jnp.float32, heads, length, 1),
        ],
        in_specs=[pl.BlockSpec(memory_space=pl.ANY)] * 7,
        out_specs=[pl.BlockSpec(memory_space=pl.ANY)] * 15,
        scratch_shapes=[
            pltpu.VMEM((length, depth), half), pltpu.VMEM((length, depth), half),
            pltpu.VMEM((depth, 3 * wide), half), pltpu.VMEM((depth, depth), half),
            pltpu.VMEM((ranks * 16, 128), half), pltpu.VMEM((length, 3 * wide), half),
            pltpu.VMEM((length, wide), half), pltpu.VMEM((tok, depth), half),
            pltpu.VMEM((tok, depth), jnp.float32), pltpu.VMEM((tok, depth), half),
            pltpu.VMEM((16, depth), jnp.float32), pltpu.VMEM((16, 2 * depth), jnp.float32),
            pltpu.VMEM((16, FF), jnp.float32), pltpu.VMEM((heads, length, 1), jnp.float32),
            dma(3, n), dma(3, n), dma(n), dma(n), dma(nc), dma(nc), dma(8), dma(n), dma(n), dma(10),
            *Walk.scratch(), *Walk.scratch(), *Walk.scratch(True), *Walk.scratch(True),
            *Spread.scratch(), *Spread.scratch(True), *Spread.scratch(True), *Spread.scratch(True),
            *Spread.scratch(),
        ],
        compiler_params=pltpu.CompilerParams(collective_id=10, has_side_effects=True),
    )(block_input, cotangent, qkv_weight, small, out_weight, fc_weight, proj_weight)


def across(source, target, sems):
    dp, s = place()
    _, n = counts()
    return [
        remote(
            source((s + k) % n), target(s), sems[0].at[k], sems[1].at[k], (dp, (s + k) % n)
        )
        for k in range(n - 1, 0, -1)
    ]


def around(source, target, sems):
    dp, s = place()
    dpc, _ = counts()
    chip, core, nc = dp // 2, dp % 2, dpc // 2
    return [
        remote(
            source((chip + k) % nc), target(chip), sems[0].at[k], sems[1].at[k],
            ((chip + k) % nc * 2 + core, s),
        )
        for k in range(1, nc)
    ]


def norm_back(values, gain, upstream):
    centred, scale = unit_rows(values)
    unit = centred * scale
    inner = upstream * gain
    along = jnp.mean(inner * unit, axis=-1, keepdims=True)
    branch = scale * (inner - jnp.mean(inner, axis=-1, keepdims=True) - unit * along)
    return branch, upstream * unit


def column_sum(values):
    return jnp.sum(values, axis=0, keepdims=True)


def backward(x_own, nv_all, g_all, fc_cols, proj_rows, qkv_cols, out_full, xn_all, qkv_all, att_all, att_own, mid_own, par_all, fcb_all, lt_all):
    dpc, n = counts()
    nc, ranks = dpc // 2, dpc * n
    tok, depth = x_own.shape
    units, rows = fc_cols.shape[1], depth // ranks
    wide, length, many = depth // n, n * tok, nc * tok
    heads, own_units, strip = wide // HD, units // (2 * n), n * rows
    half, full = jnp.bfloat16, jnp.float32
    sources = (
        nv_all, g_all, fc_cols, proj_rows, fcb_all, mid_own, par_all, out_full, att_own, qkv_all,
        att_all, lt_all, qkv_cols, xn_all, x_own,
    )
    count = len(sources)
    tile = 256
    buffers = (
        ((many, tile), full), ((many, tile), full), ((many, units), half), ((many, units), half),
        ((many, depth), half), ((many, depth), half), ((many, depth), half), ((many, depth), half),
        ((units, depth), half), ((units // 2, depth), half), ((units // 2, depth), half),
        ((units // 2, depth), half), ((depth, units), half), ((nc * strip, units), half),
        ((n * nc * rows, units), half), ((n * nc * rows, units), half), ((tok, depth), half),
        ((length, wide), half), ((depth, depth), half), ((nc * strip, depth), half),
        ((nc * strip, depth), half), ((nc * strip, depth), half), ((tok, depth), full),
        ((length, wide), full), ((length, wide), full), ((length, 3 * wide), half),
        ((length, depth), half), ((length, depth), half), ((depth, 3 * wide), half),
        ((nc * strip, 3 * wide), half), ((nc * strip, 3 * wide), half),
        ((nc * strip, 3 * wide), half),
    )

    def kernel(*refs):
        refs = list(refs)

        def take(amount):
            head = refs[:amount]
            del refs[:amount]
            return head

        sources_in = take(count)
        output, stream_out, proj_out, fc_out, out_out, qkv_out, vec_out, qv_out, fb_out = take(9)
        held = take(count)
        nv, g, wf, wp, fcb, mid, par, wo, atto, qkv, att, lt, wq, xn, xo = held
        (
            pre_s, gh_s, hid, ph, b2, b2g, fp, fpg, dp_, dpr, dpp, dpg, df, dfr, dfp, dfg, gas, gat,
            do, dor, dop, dog, gm, dk, dv, grad, b1, b1g, dq_, dqr, dqp, dqg,
        ) = take(len(buffers))
        load = take(1)[0]
        s_b2, s_fp, s_dp, s_dpz, s_df, s_dfz, s_ga, s_do, s_dop, s_b1, s_dq, s_dqp = (
            take(2) for _ in range(12)
        )
        dp, s = place()
        chip, core = dp // 2, dp % 2
        mine = pl.ds(pl.multiple_of(s * tok, tok), tok)

        loads = [
            pltpu.make_async_copy(a, b, load.at[i])
            for i, (a, b) in enumerate(zip(sources_in, held))
        ]
        for copy in loads:
            copy.start()
        greet_near()
        for copy in loads[:5]:
            copy.wait()

        def feed(u, carry):
            cols = pl.ds(pl.multiple_of(u * tile, tile), tile)
            pre_s[...] = matmul(nv[...], wf[:, cols])
            gh_s[...] = contract(g[...], wp[cols, :], (1, 1))
            bias = fcb[7:8, pl.ds(pl.multiple_of(chip * units + u * tile, tile), tile)]

            def block(r, summed):
                at = pl.ds(pl.multiple_of(r * tok, tok), tok)
                act = pre_s[at] + bias
                square = act * act
                bent = jnp.tanh(GELU_COEF * (act + 0.044715 * act * square))
                hid[at, cols] = halved(0.5 * act * (1.0 + bent))
                slope = 0.5 * (1.0 + bent) + (0.5 * act) * (1.0 - bent * bent) * (
                    GELU_COEF * (1.0 + 3.0 * 0.044715 * square)
                )
                grad_pre = gh_s[at] * slope
                ph[at, cols] = halved(grad_pre)
                return summed + column_sum(grad_pre)

            fb_out[0:1, cols] = lax.fori_loop(0, nc, block, jnp.zeros((1, tile), full))
            return carry

        lax.fori_loop(0, units // tile, feed, 0)

        def ring(values, weight, dims, target, got, sems):
            def block(k, carry):
                to = (chip + k) % nc
                at = pl.ds(pl.multiple_of(to * tok, tok), tok)
                target[at] = halved(contract(values[at], weight[...], dims))

                @pl.when(k < nc)
                def _():
                    remote(
                        part(target, to, tok), part(got, chip, tok), sems[0].at[k], sems[1].at[k],
                        (to * 2 + core, s),
                    ).start()

                return carry

            lax.fori_loop(1, nc + 1, block, 0)

        def ring_waits(target, got, sems):
            return around(lambda i: part(target, i, tok), lambda i: part(got, i, tok), sems)

        def summed(own, got, at, size, amount):
            value = widened(part(own, at, size)[...])
            for k in range(1, amount):
                value = value + widened(part(got, (at + k) % amount, size)[...])
            return value

        ring(ph, wf, (1, 1), b2, b2g, s_b2)

        def outer(left, right, target, size):
            def block(r, carry):
                at = pl.ds(pl.multiple_of(r * tile, tile), tile)
                target[at] = halved(contract(left[:, at], right[...], (0, 0)))
                return carry

            lax.fori_loop(0, size // tile, block, 0)

        def halves(target, got, sems, size):
            return [
                remote(
                    part(target, c * 2 + 1 - core, size), part(got, c, size), sems[0].at[c],
                    sems[1].at[c], (other_core(dp), s),
                )
                for c in range(nc)
            ]

        outer(hid, g, dp_, units)
        swap_dp = remote(
            part(dp_, 1 - core, units // 2), dpr, s_dp[0].at[0], s_dp[1].at[0],
            (other_core(dp), s),
        )
        swap_dp.start()
        outer(nv, ph, df, depth)
        swap_df = halves(df, dfr, s_df, strip)
        for copy in swap_df:
            copy.start()
        swap_dp.wait()

        def add_dp(i, carry):
            at = pl.ds(pl.multiple_of(i * own_units, own_units), own_units)
            dpp[at] = halved(
                widened(part(dp_, core * n + i, own_units)[...]) + widened(dpr[at])
            )
            return carry

        lax.fori_loop(0, n, add_dp, 0)
        send_dp = across(
            lambda i: part(dpp, i, own_units), lambda i: part(dpg, i, own_units), s_dpz
        )
        for copy in send_dp:
            copy.start()
        ring(hid, wp, (1, 0), fp, fpg, s_fp)
        for copy in swap_df:
            copy.wait()

        def add_df(j, carry):
            c, i = j // n, j % n
            own = part(df, (c * 2 + core) * n + i, rows)[...]
            part(dfp, i * nc + c, rows)[...] = halved(
                widened(own) + widened(part(dfr, j, rows)[...])
            )
            return carry

        lax.fori_loop(0, nc * n, add_df, 0)
        for copy in loads[5:]:
            copy.wait()
        for copy in ring_waits(b2, b2g, s_b2):
            copy.wait()
        grad_out = widened(part(g, chip, tok)[...])
        upstream = summed(b2, b2g, chip, tok, nc)
        branch, gains = norm_back(mid[...], par[3:4], upstream)
        grad_middle = grad_out + branch
        gm[...] = grad_middle
        middle_half = halved(grad_middle)
        gas[...] = halved(contract(middle_half, wo[...], (1, 1)))
        send_ga = across(lambda i: lanes(gas, i, wide), lambda i: part(gat, i, tok), s_ga)
        for copy in send_ga:
            copy.start()
        vec_out[2:3] = column_sum(grad_middle)
        vec_out[3:4] = column_sum(gains)
        vec_out[4:5] = column_sum(upstream)
        vec_out[5:6] = column_sum(grad_out)
        gat[mine] = gas[:, pl.ds(pl.multiple_of(s * wide, wide), wide)]
        b1[pl.ds(0, tok)] = middle_half
        outer(atto, b1.at[pl.ds(0, tok)], do, depth)
        swap_do = halves(do, dor, s_do, strip)
        for copy in swap_do:
            copy.start()
        dk[...] = jnp.zeros_like(dk)
        dv[...] = jnp.zeros_like(dv)
        for copy in send_ga:
            copy.wait()
        send_df = across(
            lambda i: part(dfp, i, nc * rows), lambda i: part(dfg, i, nc * rows), s_dfz
        )
        for copy in send_df:
            copy.start()
        for copy in swap_do:
            copy.wait()

        def add_halves(own, got, target):
            def block(c, carry):
                part(target, c, strip)[...] = halved(
                    widened(part(own, c * 2 + core, strip)[...])
                    + widened(part(got, c, strip)[...])
                )
                return carry

            lax.fori_loop(0, nc, block, 0)

        add_halves(do, dor, dop)
        send_do = around(lambda i: part(dop, i, strip), lambda i: part(dog, i, strip), s_dop)
        for copy in send_do:
            copy.start()
        scale = HD ** (-0.5)
        sums = jnp.zeros((1, 3 * wide), full)
        for i in range(n - 1, -1, -1):
            seen = (i + 1) * tok
            here, past = pl.ds(i * tok, tok), pl.ds(0, seen)
            queries_back = []
            for p in range(wide // 128):
                group = pl.ds(p * 128, 128)
                q2 = qkv[here, group]
                k2 = qkv[past, pl.ds(wide + p * 128, 128)]
                v2 = qkv[past, pl.ds(2 * wide + p * 128, 128)]
                ga2, att2 = gat[here, group], widened(att[here, group])
                d_query = jnp.zeros((tok, 128), full)
                d_key = jnp.zeros((seen, 128), full)
                d_value = jnp.zeros((seen, 128), full)
                for h in range(2):
                    mask = mask_of(h, q2.shape)
                    qm = jnp.where(mask, q2, jnp.zeros_like(q2))
                    gam = jnp.where(mask, ga2, jnp.zeros_like(ga2))
                    km = jnp.where(mask_of(h, k2.shape), k2, jnp.zeros_like(k2))
                    probs, _ = softmax_block(qm, k2, lt[2 * p + h, here], i * tok)
                    delta = jnp.sum(widened(gam) * att2, axis=-1, keepdims=True)
                    grad_scores = halved(probs * (contract(gam, v2, (1, 1)) - delta))
                    d_query = d_query + matmul(grad_scores, km)
                    d_key = d_key + contract(grad_scores, qm, (0, 0))
                    d_value = d_value + contract(halved(probs), gam, (0, 0))
                dk[past, group] = dk[past, group] + d_key
                dv[past, group] = dv[past, group] + d_value
                queries_back.append(d_query * scale)
            packed = jnp.concatenate(queries_back + [dk[here] * scale, dv[here]], axis=1)
            sums = sums + column_sum(packed)
            packed = halved(packed)
            grad[here] = packed
            b1[here] = halved(contract(packed, wq[...], (1, 1)))

            @pl.when(i != s)
            def _():
                k = (i - s + n) % n
                remote(
                    part(b1, i, tok), part(b1g, s, tok), s_b1[0].at[k], s_b1[1].at[k], (dp, i)
                ).start()

        qv_out[0:1] = sums
        outer(xn, grad, dq_, depth)
        swap_dq = halves(dq_, dqr, s_dq, strip)
        for copy in swap_dq:
            copy.start()
        for copy in ring_waits(fp, fpg, s_fp):
            copy.wait()
        output[...] = mid[...] + summed(fp, fpg, chip, tok, nc) + par[5:6]
        for copy in swap_dq:
            copy.wait()
        add_halves(dq_, dqr, dqp)
        send_dq = around(lambda i: part(dqp, i, strip), lambda i: part(dqg, i, strip), s_dqp)
        for copy in send_dq:
            copy.start()
        for copy in send_dp:
            copy.wait()
        proj_out[...] = summed(dpp, dpg, s, own_units, n)
        for copy in send_do:
            copy.wait()
        out_out[...] = halved(summed(dop, dog, chip, strip, nc))
        for copy in send_dq:
            copy.wait()
        qkv_out[...] = halved(summed(dqp, dqg, chip, strip, nc))
        for copy in across(lambda i: part(b1, i, tok), lambda i: part(b1g, i, tok), s_b1):
            copy.wait()
        upstream = summed(b1, b1g, s, tok, n)
        branch, gains = norm_back(widened(xo[...]), par[0:1], upstream)
        stream_out[...] = gm[...] + branch
        vec_out[0:1] = column_sum(gains)
        vec_out[1:2] = column_sum(upstream)
        for copy in send_df:
            copy.wait()
        fc_out[...] = halved(summed(dfp, dfg, s, nc * rows, n))

    def shape(kind, *dims):
        return jax.ShapeDtypeStruct(dims, kind)

    return pl.pallas_call(
        kernel,
        out_shape=[
            shape(full, tok, depth), shape(full, tok, depth), shape(full, own_units, depth),
            shape(half, nc * rows, units), shape(half, strip, depth), shape(half, strip, 3 * wide),
            shape(full, 8, depth), shape(full, 8, 3 * wide), shape(full, 8, units),
        ],
        in_specs=[pl.BlockSpec(memory_space=pl.ANY)] * count,
        out_specs=[pl.BlockSpec(memory_space=pltpu.VMEM)] * 9,
        scratch_shapes=[pltpu.VMEM(a.shape, a.dtype) for a in sources]
        + [pltpu.VMEM(dims, kind) for dims, kind in buffers]
        + [
            dma(count),
            *[dma(nc)] * 4, *[dma(1)] * 2, *[dma(n)] * 2, *[dma(nc)] * 2, *[dma(n)] * 4,
            *[dma(nc)] * 4, *[dma(n)] * 2, *[dma(nc)] * 4,
        ],
        compiler_params=pltpu.CompilerParams(
            collective_id=11, has_side_effects=True, vmem_limit_bytes=67043328
        ),
    )(*sources)


def plain(
    block_input, cotangent, ln1_gain, ln1_bias, qkv_weight, qv_bias, out_weight, out_bias, ln2_gain,
    ln2_bias, fc_weight, fc_bias, proj_weight, proj_bias,
):
    dp, s = place()
    dpc, n = counts()
    nc, ranks = dpc // 2, dpc * n
    core, chip = dp % 2, dp // 2
    tok_rows = block_input.shape[0]
    rows = qkv_weight.shape[0]
    own_units = fc_bias.shape[0]
    units = FF // nc
    heads = H // n
    wide = heads * HD
    length = n * tok_rows
    score_scale = HD ** (-0.5)

    def row_of(value, i):
        return jnp.pad(value[None], ((i, 15 - i), (0, 128 - value.shape[0])))

    parts = (ln1_gain, ln1_bias, out_bias, ln2_gain, ln2_bias, proj_bias, qv_bias, fc_bias)
    small = row_of(parts[0], 0)
    for i in range(1, 8):
        small = small + row_of(parts[i], i)
    pack = qkv_weight
    if wide % 128:
        pack = (
            qkv_weight.reshape(rows, 3, n, wide).transpose(2, 0, 1, 3).reshape(n, rows, 3 * wide)
        )
    x_all, g_all, pack_all, small_all, out_all, fc_all, proj_all = gather_inputs(
        block_input, cotangent, pack, small, out_weight, fc_weight, proj_weight
    )
    stream_seq = widened(x_all.reshape(length, D))
    grad_ff = g_all.reshape(nc * tok_rows, D)
    qkv_cols = pack_all.reshape(D, 3 * wide)
    out_full = out_all.reshape(D, D)
    fc_cols = fc_all.reshape(D, units)
    proj_rows = proj_all.reshape(units, D)
    smalls = small_all.reshape(ranks, 16, 128)
    gain_one, bias_one, out_bias_full, gain_two, bias_two, proj_bias_full = (
        widened(smalls[:, i, :rows].reshape(D)) for i in range(6)
    )
    qv_full = smalls[:, 6, : qv_bias.shape[0]].reshape(2, n, wide)
    qv_own = widened(lax.dynamic_index_in_dim(qv_full, s, 1, keepdims=False))
    fc_bias_cols = widened(
        lax.dynamic_index_in_dim(
            smalls[:, 7, :own_units].reshape(nc, units), chip, 0, keepdims=False
        )
    )

    normed_one = halved(layer_norm(stream_seq, gain_one, bias_one))
    projected = matmul(normed_one, qkv_cols)

    def by_head(values):
        return values.reshape(length, heads, HD).transpose(1, 0, 2)

    def by_token(values):
        return values.transpose(1, 0, 2).reshape(length, wide)

    def side_by_side(own, got):
        return fill(own, got, s).transpose(1, 0, 2).reshape(tok_rows, n * wide)

    queries = by_head(halved(projected[:, :wide] + qv_own[0]))
    keys = by_head(halved(projected[:, wide : 2 * wide]))
    values = by_head(halved(projected[:, 2 * wide :] + qv_own[1]))
    position = jnp.arange(length, dtype=jnp.int32)
    visible = position[None, :] <= position[:, None]
    scores = (
        jnp.einsum("hqd,hkd->hqk", queries, keys, preferred_element_type=jnp.float32) * score_scale
    )
    log_total = jnp.log(
        jnp.sum(jnp.where(visible, jnp.exp(scores), 0.0), axis=-1, keepdims=True)
    )
    probs = jnp.where(visible, jnp.exp(scores - log_total), 0.0)
    shares = halved(probs)
    attended_heads = halved(
        jnp.einsum("hqk,hkd->hqd", shares, values, preferred_element_type=jnp.float32)
    )
    attended = by_token(attended_heads).reshape(n, tok_rows, wide)
    (attended_got,) = run(1, greet_seq, Exchange(attended))
    attended_own = side_by_side(attended, attended_got)
    stream = widened(block_input)
    middle = stream + matmul(attended_own, out_full) + out_bias_full
    normed_two = halved(layer_norm(middle, gain_two, bias_two))
    (normed_all,) = run(2, greet_near, Gather(normed_two))
    normed_ff = normed_all.reshape(nc * tok_rows, D)
    grad_out = widened(cotangent)
    d_proj_bias = jnp.sum(grad_out, axis=0)
    pre_act = matmul(normed_ff, fc_cols) + fc_bias_cols
    hidden = halved(gelu_tanh(pre_act))
    grad_hidden = matmul(grad_ff, proj_rows.T)
    _, gelu_back = jax.vjp(gelu_tanh, pre_act)
    grad_pre = gelu_back(grad_hidden)[0]
    pre_half = halved(grad_pre)
    back_two = halved(matmul(pre_half, fc_cols.T)).reshape(nc, tok_rows, D)
    ff_part = halved(matmul(hidden, proj_rows)).reshape(nc, tok_rows, D)
    d_proj = halved(matmul(hidden.T, grad_ff)).reshape(2, n, own_units, D)
    d_fc = (
        halved(matmul(normed_ff.T, pre_half))
        .reshape(nc, 2, n, rows, units)
        .transpose(1, 2, 0, 3, 4)
    )
    d_fc_bias = jnp.sum(grad_pre, axis=0)
    back_two_got, d_proj_got, d_fc_got = run(
        3, greet_near, Plane(back_two), Partner(d_proj), Partner(d_fc)
    )

    def pair(own, received):
        kept = lax.dynamic_index_in_dim(own, core, 0, keepdims=False)
        return halved(widened(kept) + widened(received))

    _, norm_back_two = jax.vjp(layer_norm, middle, gain_two, bias_two)
    mid_branch, d_ln2_gain, d_ln2_bias = norm_back_two(total(back_two, back_two_got, chip))
    grad_middle = grad_out + mid_branch
    d_out_bias = jnp.sum(grad_middle, axis=0)
    middle_half = halved(grad_middle)
    d_out = (
        halved(matmul(attended_own.T, middle_half))
        .reshape(nc, 2, n * rows, D)
        .transpose(1, 0, 2, 3)
    )
    grad_attended = halved(matmul(middle_half, out_full.T))
    grad_attended = grad_attended.reshape(tok_rows, n, wide).transpose(1, 0, 2)
    d_proj, d_fc = pair(d_proj, d_proj_got), pair(d_fc, d_fc_got)
    grad_att_got, ff_got, d_proj_parts, d_out_got = run(
        4, greet_near, Exchange(grad_attended), Plane(ff_part), Exchange(d_proj), Partner(d_out)
    )
    proj_grad = total(d_proj, d_proj_parts, s)
    output = middle + total(ff_part, ff_got, chip) + proj_bias_full
    grad_att = by_head(fill(grad_attended, grad_att_got, s).reshape(length, wide))
    row_delta = jnp.sum(widened(grad_att) * widened(attended_heads), axis=-1, keepdims=True)
    grad_shares = jnp.einsum("hqd,hkd->hqk", grad_att, values, preferred_element_type=jnp.float32)
    grad_scores = halved(probs * (grad_shares - row_delta))
    grad_q = (
        jnp.einsum("hqk,hkd->hqd", grad_scores, keys, preferred_element_type=jnp.float32)
        * score_scale
    )
    grad_k = (
        jnp.einsum("hqk,hqd->hkd", grad_scores, queries, preferred_element_type=jnp.float32)
        * score_scale
    )
    grad_v = jnp.einsum("hqk,hqd->hkd", shares, grad_att, preferred_element_type=jnp.float32)
    grad_qkv = jnp.concatenate([by_token(grad_q), by_token(grad_k), by_token(grad_v)], axis=1)
    qkv_half = halved(grad_qkv)
    back_one = halved(matmul(qkv_half, qkv_cols.T)).reshape(n, tok_rows, D)
    d_qkv = (
        halved(matmul(normed_one.T, qkv_half))
        .reshape(nc, 2, n * rows, 3 * wide)
        .transpose(1, 0, 2, 3)
    )
    sums = jnp.sum(grad_qkv, axis=0)
    d_qv = jnp.stack([sums[:wide], sums[2 * wide :]])[:, None]
    d_out = pair(d_out, d_out_got)
    back_one_got, d_fc_parts, d_out_parts, d_qkv_got = run(
        5, greet_near, Exchange(back_one), Exchange(d_fc), Plane(d_out), Partner(d_qkv)
    )
    d_qkv = pair(d_qkv, d_qkv_got)
    fc_cut = halved(total(d_fc, d_fc_parts, s))
    out_cut = halved(total(d_out, d_out_parts, chip)).reshape(n, rows, D)
    _, norm_back_one = jax.vjp(layer_norm, stream, gain_one, bias_one)
    stream_branch, d_ln1_gain, d_ln1_bias = norm_back_one(total(back_one, back_one_got, s))
    grad_stream = grad_middle + stream_branch
    turn = jnp.arange(n, dtype=jnp.int32)[None, :, None] == s
    mine = jnp.arange(nc, dtype=jnp.int32)[:, None] == chip
    vectors = jnp.concatenate(
        [
            v.reshape(ranks, rows)
            for v in (d_ln1_gain, d_ln1_bias, d_out_bias, d_ln2_gain, d_ln2_bias, d_proj_bias)
        ]
        + [
            jnp.where(turn, d_qv, 0.0).reshape(ranks, -1),
            jnp.where(mine, d_fc_bias, 0.0).reshape(ranks, own_units),
        ],
        axis=1,
    )
    used = vectors.shape[1]
    vectors = jnp.pad(vectors, ((0, 0), (0, -used % 128))).reshape(ranks, -1, 128)
    d_qkv_parts, fc_got, d_out_last, vectors_got = run(
        6, greet_all, Plane(d_qkv), Plane(fc_cut), Exchange(out_cut), Everyone(vectors)
    )
    fc_grad = widened(fill(fc_cut, fc_got, chip)).transpose(1, 0, 2).reshape(rows, FF)
    out_grad = total(out_cut, d_out_last, s)
    qkv_rows = halved(total(d_qkv, d_qkv_parts, chip)).reshape(n, rows, 3 * wide)
    vector = jnp.sum(fill(vectors, vectors_got, dp * n + s), axis=0).reshape(-1)
    firsts = [vector[i * rows : (i + 1) * rows] for i in range(6)]
    at = 6 * rows
    qv_grad = vector[at : at + qv_bias.shape[0]]
    at += qv_bias.shape[0]
    fc_bias_grad = vector[at : at + own_units]
    (qkv_got,) = run(7, greet_seq, Exchange(qkv_rows))
    qkv_grad = (
        widened(fill(qkv_rows, qkv_got, s))
        .reshape(n, rows, 3, wide)
        .transpose(1, 2, 0, 3)
        .reshape(rows, 3 * D)
    )
    return (
        output, grad_stream, firsts[0], firsts[1], qkv_grad, qv_grad, out_grad, firsts[2],
        firsts[3], firsts[4], fc_grad, fc_bias_grad, proj_grad, firsts[5],
    )


def fused(
    block_input, cotangent, ln1_gain, ln1_bias, qkv_weight, qv_bias, out_weight, out_bias, ln2_gain,
    ln2_bias, fc_weight, fc_bias, proj_weight, proj_bias,
):
    dp, s = place()
    dpc, n = counts()
    nc, ranks = dpc // 2, dpc * n
    core, chip = dp % 2, dp // 2
    tok_rows = block_input.shape[0]
    rows = qkv_weight.shape[0]
    own_units = fc_bias.shape[0]
    units = FF // nc
    heads = H // n
    wide = heads * HD
    length = n * tok_rows
    score_scale = HD ** (-0.5)

    def row_of(value, i):
        return jnp.pad(value[None], ((i, 15 - i), (0, 128 - value.shape[0])))

    parts = (ln1_gain, ln1_bias, out_bias, ln2_gain, ln2_bias, proj_bias, qv_bias, fc_bias)
    small = row_of(parts[0], 0)
    for i in range(1, 8):
        small = small + row_of(parts[i], i)
    (
        normed_all, g_all, fc_all, proj_all, _, qkv_cols, out_full, xn_all, qkv, attended, attended_own,
        middle, par, fcb, log_totals,
    ) = forward(block_input, cotangent, qkv_weight, small, out_weight, fc_weight, proj_weight)
    output, grad_stream, proj_grad, fc_cut, out_cut, qkv_rows, vecs, qv_sums, fc_sums = backward(
        block_input, normed_all.reshape(nc * tok_rows, D), g_all.reshape(nc * tok_rows, D),
        fc_all.reshape(D, units), proj_all.reshape(units, D), qkv_cols, out_full, xn_all, qkv, attended,
        attended_own, middle, par, fcb, log_totals,
    )
    fc_cut = fc_cut.reshape(nc, rows, units)
    out_cut = out_cut.reshape(n, rows, D)
    qkv_rows = qkv_rows.reshape(n, rows, 3 * wide)
    d_qv = jnp.stack([qv_sums[0, :wide], qv_sums[0, 2 * wide :]])[:, None]
    d_fc_bias = fc_sums[0]
    turn = jnp.arange(n, dtype=jnp.int32)[None, :, None] == s
    mine = jnp.arange(nc, dtype=jnp.int32)[:, None] == chip
    vectors = jnp.concatenate(
        [vecs[:6].reshape(6, ranks, rows).transpose(1, 0, 2).reshape(ranks, 6 * rows)]
        + [
            jnp.where(turn, d_qv, 0.0).reshape(ranks, -1),
            jnp.where(mine, d_fc_bias, 0.0).reshape(ranks, own_units),
        ],
        axis=1,
    )
    used = vectors.shape[1]
    vectors = jnp.pad(vectors, ((0, 0), (0, -used % 128))).reshape(ranks, -1, 128)
    qkv_got, fc_got, d_out_last, vectors_got = run(
        6, greet_all, Exchange(qkv_rows), Plane(fc_cut), Exchange(out_cut), Everyone(vectors)
    )
    fc_grad = widened(fill(fc_cut, fc_got, chip)).transpose(1, 0, 2).reshape(rows, FF)
    out_grad = total(out_cut, d_out_last, s)
    vector = jnp.sum(fill(vectors, vectors_got, dp * n + s), axis=0).reshape(-1)
    firsts = [vector[i * rows : (i + 1) * rows] for i in range(6)]
    at = 6 * rows
    qv_grad = vector[at : at + qv_bias.shape[0]]
    at += qv_bias.shape[0]
    fc_bias_grad = vector[at : at + own_units]
    qkv_grad = (
        widened(fill(qkv_rows, qkv_got, s))
        .reshape(n, rows, 3, wide)
        .transpose(1, 2, 0, 3)
        .reshape(rows, 3 * D)
    )
    return (
        output, grad_stream, firsts[0], firsts[1], qkv_grad, qv_grad, out_grad, firsts[2],
        firsts[3], firsts[4], fc_grad, fc_bias_grad, proj_grad, firsts[5],
    )


def local(*arrays):
    dpc, n = counts()
    fits = (D // n) % 128 == 0 and arrays[4].shape[0] % 16 == 0 and arrays[0].shape[0] % 128 == 0
    return fused(*arrays) if fits and FF // (dpc // 2) % 256 == 0 else plain(*arrays)


def solution(mesh):
    in_specs = (
        P(("dp", "seq"), None),
        P(("dp", "seq"), None),
        P(("dp", "seq")),
        P(("dp", "seq")),
        P(("dp", "seq"), None),
        P(("dp", "seq")),
        P(("dp", "seq"), None),
        P(("dp", "seq")),
        P(("dp", "seq")),
        P(("dp", "seq")),
        P(("dp", "seq"), None),
        P(("dp", "seq")),
        P(("dp", "seq"), None),
        P(("dp", "seq")),
    )
    out_specs = (
        P(("dp", "seq"), None),
        P(("dp", "seq"), None),
        P(("dp", "seq")),
        P(("dp", "seq")),
        P(("dp", "seq"), None),
        P(("dp", "seq")),
        P(("dp", "seq"), None),
        P(("dp", "seq")),
        P(("dp", "seq")),
        P(("dp", "seq")),
        P(("dp", "seq"), None),
        P(("dp", "seq")),
        P(("dp", "seq"), None),
        P(("dp", "seq")),
    )
    return jax.shard_map(local, mesh=mesh, in_specs=in_specs, out_specs=out_specs, check_vma=False)
```

```python
import math

import jax
import jax.numpy as jnp
from jax import lax
from jax.experimental import pallas as pl
from jax.experimental.pallas import tpu as pltpu
from jax.sharding import PartitionSpec as P

D = 1024
H = 16
HD = 64
FF = 4096


EPS = 1e-05
GELU_COEF = math.sqrt(2.0 / math.pi)
MESH = pl.DeviceIdType.MESH


def layer_norm(values, norm_gain, offset):
    center = jnp.mean(values, axis=-1, keepdims=True)
    centred = values - center
    spread = jnp.mean(centred * centred, axis=-1, keepdims=True)
    return centred * lax.rsqrt(spread + EPS) * norm_gain + offset


def gelu_tanh(pre_act):
    return (
        0.5
        * pre_act
        * (1.0 + jnp.tanh(GELU_COEF * (pre_act + 0.044715 * pre_act * pre_act * pre_act)))
    )


def halved(values):
    return values.astype(jnp.bfloat16)


def widened(values):
    return values.astype(jnp.float32)


def matmul(left, right):
    return jnp.dot(left, right, preferred_element_type=jnp.float32)


def place():
    return lax.axis_index("dp"), lax.axis_index("seq")


def counts():
    return lax.axis_size("dp"), lax.axis_size("seq")


def remote(src, dst, send, recv, device):
    return pltpu.make_async_remote_copy(
        src_ref=src, dst_ref=dst, send_sem=send, recv_sem=recv, device_id=device, device_id_type=MESH
    )


def dma(*shape):
    return pltpu.SemaphoreType.DMA(shape)


def greet_all():
    dp, s = place()
    dpc, n = counts()
    barrier = pltpu.get_barrier_semaphore()

    def greet(i, carry):
        @pl.when(i != dp * n + s)
        def _():
            pl.semaphore_signal(barrier, inc=1, device_id=(i // n, i % n), device_id_type=MESH)

        return carry

    lax.fori_loop(0, dpc * n, greet, 0)
    pl.semaphore_wait(barrier, dpc * n - 1)


def greet_near():
    dp, s = place()
    dpc, n = counts()
    nc = dpc // 2
    barrier = pltpu.get_barrier_semaphore()
    for k in range(1, n):
        pl.semaphore_signal(barrier, inc=1, device_id=(dp, (s + k) % n), device_id_type=MESH)
    for k in range(1, nc):
        pl.semaphore_signal(barrier, inc=1, device_id=((dp + 2 * k) % dpc, s), device_id_type=MESH)
    pl.semaphore_signal(barrier, inc=1, device_id=(other_core(dp), s), device_id_type=MESH)
    pl.semaphore_wait(barrier, n - 1 + nc)


def greet_seq():
    dp, s = place()
    _, n = counts()
    barrier = pltpu.get_barrier_semaphore()
    for k in range(1, n):
        pl.semaphore_signal(barrier, inc=1, device_id=(dp, (s + k) % n), device_id_type=MESH)
    pl.semaphore_wait(barrier, n - 1)


def other_core(dp):
    return dp + 1 - 2 * (dp % 2)


class Exchange:
    def __init__(self, value):
        _, n = counts()
        self.operands = (value,)
        self.outs = (value,)
        self.sems = (dma(n), dma(n))

    def copies(self, ins, outs, sems):
        dp, s = place()
        _, n = counts()
        return [
            remote(
                ins[0].at[(s + k) % n], outs[0].at[s], sems[0].at[k], sems[1].at[k], (dp, (s + k) % n)
            )
            for k in range(n - 1, 0, -1)
        ]

    def start(self, ins, outs, sems):
        for copy in self.copies(ins, outs, sems):
            copy.start()

    def finish(self, ins, outs, sems):
        for copy in self.copies(ins, outs, sems):
            copy.wait()


class Plane(Exchange):
    def __init__(self, value):
        dpc, _ = counts()
        self.operands = (value,)
        self.outs = (value,)
        self.sems = (dma(dpc // 2), dma(dpc // 2))

    def copies(self, ins, outs, sems):
        dp, s = place()
        dpc, _ = counts()
        chip, core, nc = dp // 2, dp % 2, dpc // 2
        return [
            remote(
                ins[0].at[(chip + k) % nc],
                outs[0].at[chip],
                sems[0].at[k],
                sems[1].at[k],
                ((chip + k) % nc * 2 + core, s),
            )
            for k in range(1, nc)
        ]


class Partner(Exchange):
    def __init__(self, value):
        self.operands = (value,)
        self.outs = (jax.ShapeDtypeStruct(value.shape[1:], value.dtype),)
        self.sems = (dma(1), dma(1))

    def copies(self, ins, outs, sems):
        dp, s = place()
        return [
            remote(
                ins[0].at[1 - dp % 2], outs[0], sems[0].at[0], sems[1].at[0], (other_core(dp), s)
            )
        ]


class Everyone:
    def __init__(self, value):
        dpc, n = counts()
        self.operands = (value,)
        self.outs = (value,)
        self.sems = (dma(dpc * n), dma(dpc * n))

    def copy(self, ins, outs, sems, k):
        dp, s = place()
        dpc, n = counts()
        me = dp * n + s
        peer = (me + k) % (dpc * n)
        return remote(
            ins[0].at[peer], outs[0].at[me], sems[0].at[k], sems[1].at[k], (peer // n, peer % n)
        )

    def start(self, ins, outs, sems):
        def step(k, carry):
            self.copy(ins, outs, sems, k).start()
            return carry

        lax.fori_loop(1, self.outs[0].shape[0], step, 0)

    def finish(self, ins, outs, sems):
        def step(k, carry):
            self.copy(ins, outs, sems, k).wait()
            return carry

        lax.fori_loop(1, self.outs[0].shape[0], step, 0)


class Walk:
    def __init__(self, source, block, sems, pair=False, keep=True):
        self.source, self.block, self.sems, self.pair, self.keep = source, block, sems, pair, keep

    @staticmethod
    def scratch(pair=False):
        _, n = counts()
        return (dma(2, n), dma(2, n), dma(1)) + ((dma(2, n), dma(2, n)) if pair else ())

    def hand_on(self, way, k):
        dp, s = place()
        sign = 1 - 2 * way
        block = self.block(s - sign * k, dp % 2)
        return remote(
            self.source if k == 0 else block, block,
            self.sems[0].at[way, k], self.sems[1].at[way, k], (dp, s + sign),
        )

    def over(self, way, k, core):
        dp, s = place()
        block = self.block(s - (1 - 2 * way) * k, core)
        return remote(
            self.source if k == 0 else block, block,
            self.sems[3].at[way, k], self.sems[4].at[way, k], (other_core(dp), s),
        )

    def own(self):
        dp, s = place()
        return pltpu.make_async_copy(self.source, self.block(s, dp % 2), self.sems[2].at[0])

    def guard(self, way, k):
        _, s = place()
        _, n = counts()
        return (s >= k) if way == 0 else (s < n - k)

    def follows(self, way):
        _, s = place()
        _, n = counts()
        return (s < n - 1) if way == 0 else (s > 0)

    def start(self):
        dp, _ = place()
        for way in (0, 1):

            @pl.when(self.follows(way))
            def _():
                self.hand_on(way, 0).start()

        if self.keep:
            self.own().start()
        if self.pair:
            self.over(0, 0, dp % 2).start()

    def step(self, k):
        dp, s = place()
        _, n = counts()
        for way in (0, 1):
            sign = 1 - 2 * way

            @pl.when(self.guard(way, k))
            def _():
                block = self.block(s - sign * k, dp % 2)
                remote(
                    block, block, self.sems[0].at[way, k - 1], self.sems[1].at[way, k - 1],
                    (dp, s - sign),
                ).wait_recv()
                if k < n - 1:

                    @pl.when(self.follows(way))
                    def _():
                        self.hand_on(way, k).start()

                if self.pair:
                    self.over(way, k, dp % 2).start()

    def close(self):
        dp, _ = place()
        _, n = counts()
        for way in (0, 1):
            for k in range(n - 1):

                @pl.when(jnp.logical_and(self.follows(way), self.guard(way, k)))
                def _():
                    self.hand_on(way, k).wait_send()

        if self.keep:
            self.own().wait()
        if self.pair:
            self.over(0, 0, dp % 2).wait_send()
            self.over(0, 0, 1 - dp % 2).wait_recv()
            for way in (0, 1):
                for k in range(1, n):

                    @pl.when(self.guard(way, k))
                    def _():
                        self.over(way, k, dp % 2).wait_send()
                        self.over(way, k, 1 - dp % 2).wait_recv()


class Spread:
    def __init__(self, source, block, sems, pair=False):
        self.source, self.block, self.sems, self.pair = source, block, sems, pair

    @staticmethod
    def scratch(pair=False):
        dpc, _ = counts()
        nc = dpc // 2
        return (dma(nc), dma(nc)) + ((dma(nc), dma(nc)) if pair else ())

    def to_chips(self):
        dp, s = place()
        dpc, _ = counts()
        nc = dpc // 2
        return [
            remote(
                self.source, self.block(dp // 2, dp % 2), self.sems[0].at[k], self.sems[1].at[k],
                ((dp // 2 + k) % nc * 2 + dp % 2, s),
            )
            for k in range(1, nc)
        ]

    def over(self, k, core):
        dp, s = place()
        dpc, _ = counts()
        nc = dpc // 2
        block = self.block((dp // 2 - k + nc) % nc, core)
        return remote(
            self.source if k == 0 else block, block, self.sems[2].at[k], self.sems[3].at[k],
            (other_core(dp), s),
        )

    def start(self):
        dp, _ = place()
        for copy in self.to_chips():
            copy.start()
        if self.pair:
            self.over(0, dp % 2).start()

    def step(self):
        dp, s = place()
        dpc, _ = counts()
        nc = dpc // 2
        for k in range(1, nc):
            chip = (dp // 2 - k + nc) % nc
            block = self.block(chip, dp % 2)
            remote(
                block, block, self.sems[0].at[k], self.sems[1].at[k], (chip * 2 + dp % 2, s)
            ).wait_recv()
            if self.pair:
                self.over(k, dp % 2).start()

    def close(self):
        dp, _ = place()
        dpc, _ = counts()
        for copy in self.to_chips():
            copy.wait_send()
        if self.pair:
            for k in range(dpc // 2):
                self.over(k, dp % 2).wait_send()
                self.over(k, 1 - dp % 2).wait_recv()


class Gather:
    def __init__(self, value):
        dpc, _ = counts()
        self.operands = (value,)
        self.outs = (jax.ShapeDtypeStruct((dpc // 2,) + value.shape, value.dtype),)
        self.sems = Spread.scratch() + (dma(1),)

    def spread(self, ins, outs, sems):
        return Spread(ins[0], lambda chip, core: outs[0].at[chip], sems)

    def own(self, ins, outs, sems):
        dp, _ = place()
        return pltpu.make_async_copy(ins[0], outs[0].at[dp // 2], sems[2].at[0])

    def start(self, ins, outs, sems):
        self.spread(ins, outs, sems).start()
        self.own(ins, outs, sems).start()

    def finish(self, ins, outs, sems):
        self.spread(ins, outs, sems).step()
        self.spread(ins, outs, sems).close()
        self.own(ins, outs, sems).wait()


def run(number, greet, *tasks):
    spans = []
    a = b = c = 0
    for task in tasks:
        spans.append((a, b, c))
        a += len(task.operands)
        b += len(task.outs)
        c += len(task.sems)
    n_in, n_out = a, b

    def kernel(*refs):
        ins, outs, sems = refs[:n_in], refs[n_in : n_in + n_out], refs[n_in + n_out :]
        greet()
        views = [
            (
                ins[i : i + len(t.operands)],
                outs[o : o + len(t.outs)],
                sems[m : m + len(t.sems)],
            )
            for t, (i, o, m) in zip(tasks, spans)
        ]
        for t, view in zip(tasks, views):
            t.start(*view)
        for t, view in zip(tasks, views):
            t.finish(*view)

    return pl.pallas_call(
        kernel,
        out_shape=[jax.ShapeDtypeStruct(o.shape, o.dtype) for t in tasks for o in t.outs],
        in_specs=[pl.BlockSpec(memory_space=pl.ANY)] * n_in,
        out_specs=[pl.BlockSpec(memory_space=pl.ANY)] * n_out,
        scratch_shapes=[s for t in tasks for s in t.sems],
        compiler_params=pltpu.CompilerParams(collective_id=number, has_side_effects=True),
    )(*[v for t in tasks for v in t.operands])


def gather_inputs(block_input, cotangent, pack, small, out_rows, fc_rows, proj_rows):
    dpc, n = counts()
    nc = dpc // 2
    units = fc_rows.shape[1] // nc
    whole = pack.ndim == 2
    wide = block_input.shape[1] // n
    pieces = 3 if whole else 1
    rows = out_rows.shape[0]

    def kernel(
        x_in, g_in, pack_in, small_in, out_in, fc_in, proj_in,
        x_all, g_all, pack_all, small_all, out_all, fc_all, proj_all, fc_own, *sems,
    ):
        dp, s = place()
        chip, core = dp // 2, dp % 2

        def take(count):
            nonlocal sems
            head, sems = sems[:count], sems[count:]
            return head

        pack_send, pack_recv, small_send, small_recv, fc_send, fc_recv, local = take(7)
        x = Walk(x_in, lambda i, c: x_all.at[i], take(3))
        out = Walk(out_in, lambda i, c: out_all.at[dp, i], take(3))
        fc = Walk(fc_own, lambda i, c: fc_all.at[:, c, i], take(5), pair=True)
        proj = Walk(proj_in, lambda i, c: proj_all.at[c, i], take(5), pair=True)
        grads = Spread(g_in, lambda p, c: g_all.at[p], take(2))
        spread_pack = Spread(pack_all.at[dp], lambda p, c: pack_all.at[p * 2 + c], take(4), pair=True)
        spread_small = Spread(small_all.at[dp], lambda p, c: small_all.at[p * 2 + c], take(4), pair=True)
        spread_out = Spread(out_all.at[dp], lambda p, c: out_all.at[p * 2 + c], take(4), pair=True)

        def piece(to, j):
            if whole:
                source = pack_in.at[:, pl.ds(pl.multiple_of(j * n * wide + to * wide, 128), wide)]
                return source, pack_all.at[dp, s, :, pl.ds(j * wide, wide)]
            return pack_in.at[to], pack_all.at[dp, s]

        shuffles = []
        for k in range(n - 1, 0, -1):
            to = (s + k) % n
            for j in range(pieces):
                source, target = piece(to, j)
                shuffles.append(
                    remote(source, target, pack_send.at[j, k], pack_recv.at[j, k], (dp, to))
                )
            shuffles.append(
                remote(small_in, small_all.at[dp, s], small_send.at[k], small_recv.at[k], (dp, to))
            )

        def cut(to):
            return fc_in.at[:, pl.ds(pl.multiple_of(to * units, 128), units)]

        turns = [
            remote(
                cut((chip + k) % nc), fc_own.at[chip], fc_send.at[k], fc_recv.at[k],
                ((chip + k) % nc * 2 + core, s),
            )
            for k in range(1, nc)
        ]
        keeps = [
            pltpu.make_async_copy(*piece(s, j), local.at[j]) for j in range(pieces)
        ] + [
            pltpu.make_async_copy(small_in, small_all.at[dp, s], local.at[3]),
            pltpu.make_async_copy(cut(chip), fc_own.at[chip], local.at[4]),
        ]
        keep_g = pltpu.make_async_copy(g_in, g_all.at[chip], local.at[5])

        greet_near()
        for copy in shuffles + keeps:
            copy.start()
        x.start()
        out.start()
        for copy in turns:
            copy.start()
        for copy in shuffles + keeps:
            copy.wait()
        spread_pack.start()
        spread_small.start()
        grads.start()
        keep_g.start()
        for k in range(1, n):
            x.step(k)
            out.step(k)
        out.own().wait()
        spread_out.start()
        for copy in turns:
            copy.wait()
        fc.start()
        proj.start()
        spread_pack.step()
        spread_small.step()
        for k in range(1, n):
            fc.step(k)
            proj.step(k)
        spread_out.step()
        grads.step()
        x.close()
        out.keep = False
        out.close()
        fc.close()
        proj.close()
        for spread in (spread_pack, spread_small, spread_out, grads):
            spread.close()
        keep_g.wait()

    def grown(value, *lead):
        return jax.ShapeDtypeStruct(lead, value.dtype)

    depth = block_input.shape[1]
    return pl.pallas_call(
        kernel,
        out_shape=[
            grown(block_input, n, *block_input.shape), grown(cotangent, nc, *cotangent.shape),
            grown(pack, dpc, n, rows, 3 * wide), grown(small, dpc, n, *small.shape),
            grown(out_rows, dpc, n, *out_rows.shape), grown(fc_rows, nc, 2, n, rows, units),
            grown(proj_rows, 2, n, *proj_rows.shape), grown(fc_rows, nc, rows, units),
        ],
        in_specs=[pl.BlockSpec(memory_space=pl.ANY)] * 7,
        out_specs=[pl.BlockSpec(memory_space=pl.ANY)] * 8,
        scratch_shapes=[
            dma(pieces, n), dma(pieces, n), dma(n), dma(n), dma(nc), dma(nc), dma(6),
            *Walk.scratch(), *Walk.scratch(), *Walk.scratch(True), *Walk.scratch(True),
            *Spread.scratch(), *Spread.scratch(True), *Spread.scratch(True), *Spread.scratch(True),
        ],
        compiler_params=pltpu.CompilerParams(collective_id=0, has_side_effects=True),
    )(block_input, cotangent, pack, small, out_rows, fc_rows, proj_rows)[:7]


def total(own, received, mine):
    picked = [
        jnp.where(k == mine, widened(own[k]), widened(received[k])) for k in range(own.shape[0])
    ]
    result = picked[0]
    for value in picked[1:]:
        result = result + value
    return result


def fill(own, received, mine):
    slots = lax.broadcasted_iota(jnp.int32, (own.shape[0],) + (1,) * (own.ndim - 1), 0)
    return jnp.where(slots == mine, own, received)


def mask_of(half, shape):
    lane = lax.broadcasted_iota(jnp.int32, shape, len(shape) - 1)
    return (lane // HD) % 2 == half


def contract(left, right, dims):
    return lax.dot_general(
        left, right, ((dims[:1], dims[1:]), ((), ())), preferred_element_type=jnp.float32
    )


def unit_rows(values):
    center = jnp.mean(values, axis=-1, keepdims=True)
    centred = values - center
    spread = jnp.mean(centred * centred, axis=-1, keepdims=True)
    return centred, lax.rsqrt(spread + EPS)


def part(ref, i, size):
    return ref.at[pl.ds(pl.multiple_of(i * size, size), size)]


def lanes(ref, i, size):
    return ref.at[:, pl.ds(pl.multiple_of(i * size, size), size)]


def softmax_block(q_masked, k, log_total, diagonal):
    scores = contract(q_masked, k, (1, 1)) * HD ** (-0.5)
    row = lax.broadcasted_iota(jnp.int32, scores.shape, 0) + diagonal
    visible = lax.broadcasted_iota(jnp.int32, scores.shape, 1) <= row
    if log_total is None:
        log_total = jnp.log(
            jnp.sum(jnp.where(visible, jnp.exp(scores), 0.0), axis=-1, keepdims=True)
        )
    return jnp.where(visible, jnp.exp(scores - log_total), 0.0), log_total


def forward(block_input, cotangent, qkv_weight, small, out_weight, fc_weight, proj_weight):
    dpc, n = counts()
    nc, ranks = dpc // 2, dpc * n
    tok, depth = block_input.shape
    rows, units, own_units = out_weight.shape[0], fc_weight.shape[1] // nc, proj_weight.shape[0]
    wide, length = depth // n, n * tok
    heads = wide // HD
    bias_own = 2 * depth // ranks

    def kernel(*refs):
        refs = list(refs)

        def take(count):
            head = refs[:count]
            del refs[:count]
            return head

        x_in, g_in, qkv_in, small_in, out_in, fc_in, proj_in = take(7)
        (
            nv_o, g_o, wf_o, wp_o, fc_own, wq_o, wo_o, xn_o, qkv_o, att_o, atto_o, mid_o, par_o,
            fcb_o, lt_o,
        ) = take(15)
        xv, xn, wq, wo, sm, qkv, att, atto, mid, n2, par, qvb, fcb, lt = take(14)
        (
            pack_send, pack_recv, small_send, small_recv, fc_send, fc_recv, local, att_send,
            att_recv, save,
        ) = take(10)
        dp, s = place()
        chip, core = dp // 2, dp % 2
        me = dp * n + s

        x = Walk(x_in, lambda i, c: part(xv, i, tok), take(3))
        out = Walk(out_in, lambda i, c: part(wo, dp * n + i, rows), take(3))
        fc = Walk(fc_own, lambda i, c: wf_o.at[:, c, i], take(5), pair=True)
        proj = Walk(proj_in, lambda i, c: wp_o.at[c, i], take(5), pair=True)
        grads = Spread(g_in, lambda p, c: g_o.at[p], take(2))

        def strip(ref, size):
            return lambda p, c: part(ref, p * 2 + c, size)

        spread_pack = Spread(part(wq, dp, n * rows), strip(wq, n * rows), take(4), pair=True)
        spread_small = Spread(part(sm, dp, n * 16), strip(sm, n * 16), take(4), pair=True)
        spread_out = Spread(part(wo, dp, n * rows), strip(wo, n * rows), take(4), pair=True)
        normed = Spread(n2, lambda p, c: nv_o.at[p], take(2))

        def piece(to, j):
            return (
                qkv_in.at[:, pl.ds(pl.multiple_of(j * depth + to * wide, 128), wide)],
                part(wq, me, rows).at[:, pl.ds(j * wide, wide)],
            )

        shuffles = []
        for k in range(n - 1, 0, -1):
            to = (s + k) % n
            for j in range(3):
                source, target = piece(to, j)
                shuffles.append(
                    remote(source, target, pack_send.at[j, k], pack_recv.at[j, k], (dp, to))
                )
            shuffles.append(
                remote(small_in, part(sm, me, 16), small_send.at[k], small_recv.at[k], (dp, to))
            )

        turns = [
            remote(
                lanes(fc_in, (chip + k) % nc, units), fc_own.at[chip], fc_send.at[k], fc_recv.at[k],
                ((chip + k) % nc * 2 + core, s),
            )
            for k in range(1, nc)
        ]
        keeps = [pltpu.make_async_copy(*piece(s, j), local.at[j]) for j in range(3)] + [
            pltpu.make_async_copy(small_in, part(sm, me, 16), local.at[3]),
            pltpu.make_async_copy(lanes(fc_in, chip, units), fc_own.at[chip], local.at[4]),
        ]
        keep_g = pltpu.make_async_copy(g_in, g_o.at[chip], local.at[5])

        greet_near()
        for copy in shuffles + keeps:
            copy.start()
        x.start()
        out.start()
        for copy in turns:
            copy.start()
        for copy in shuffles + keeps:
            copy.wait()
        spread_pack.start()
        spread_small.start()
        x.step(1)
        out.step(1)
        spread_small.step()
        spread_small.close()
        for size, target, width, at in (
            (rows, par, depth, 0), (bias_own, qvb, 2 * depth, 6), (own_units, fcb, FF, 7)
        ):
            group = 128 // size
            for j in range(width // 128):
                total_tile = widened(sm[pl.ds(j * group * 16, 16)])
                for r in range(1, group):
                    tile = widened(sm[pl.ds((j * group + r) * 16, 16)])
                    total_tile = total_tile + pltpu.roll(tile, r * size, 1)
                target[:, pl.ds(j * 128, 128)] = total_tile
        for k in range(2, n):
            x.step(k)
            out.step(k)
        out.own().wait()
        out.keep = False
        spread_out.start()
        for copy in turns:
            copy.wait()
        fc.start()
        proj.start()
        grads.start()
        keep_g.start()
        spread_pack.step()
        spread_pack.close()
        x.close()
        qv_rows = [
            qvb[6:7, pl.ds(pl.multiple_of(j * depth + s * wide, 128), wide)] for j in range(2)
        ]
        shift = jnp.concatenate([qv_rows[0], jnp.zeros((1, wide), jnp.float32), qv_rows[1]], axis=1)

        def project(i, carry):
            at = pl.ds(pl.multiple_of(i * tok, tok), tok)
            centred, scale = unit_rows(widened(xv[at]))
            normed_one = halved(centred * scale * par[0:1] + par[1:2])
            xn[at] = normed_one
            qkv[at] = halved(matmul(normed_one, wq[...]) + shift)
            return carry

        lax.fori_loop(0, n, project, 0)
        saves = [
            pltpu.make_async_copy(a, b, save.at[i])
            for i, (a, b) in enumerate(
                ((wq, wq_o), (xn, xn_o), (qkv, qkv_o), (par, par_o), (fcb, fcb_o), (att, att_o),
                 (lt, lt_o), (wo, wo_o), (atto, atto_o), (mid, mid_o))
            )
        ]
        for copy in saves[:5]:
            copy.start()

        def att_copy(i):
            k = (i - s + n) % n
            return remote(
                part(att, i, tok), lanes(atto, s, wide), att_send.at[k], att_recv.at[k], (dp, i)
            )

        for i in range(n - 1, -1, -1):
            seen = (i + 1) * tok
            here = pl.ds(i * tok, tok)
            for p in range(wide // 128):
                q2 = qkv[here, pl.ds(p * 128, 128)]
                k2 = qkv[pl.ds(0, seen), pl.ds(wide + p * 128, 128)]
                v2 = qkv[pl.ds(0, seen), pl.ds(2 * wide + p * 128, 128)]
                outs = []
                for h in range(2):
                    probs, log_total = softmax_block(
                        jnp.where(mask_of(h, q2.shape), q2, jnp.zeros_like(q2)), k2, None, i * tok
                    )
                    lt[2 * p + h, here] = log_total
                    outs.append(matmul(halved(probs), v2))
                att[here, pl.ds(p * 128, 128)] = halved(
                    jnp.where(mask_of(0, outs[0].shape), outs[0], outs[1])
                )

            @pl.when(i != s)
            def _():
                att_copy(i).start()

            @pl.when(i == s)
            def _():
                pltpu.make_async_copy(
                    part(att, i, tok), lanes(atto, s, wide), local.at[6]
                ).start()

            if i == n - 1:
                fc.step(1)
            if i == 1:
                proj.step(1)
        for copy in saves[5:7]:
            copy.start()
        spread_out.step()
        spread_out.close()
        saves[7].start()
        pltpu.make_async_copy(part(att, s, tok), lanes(atto, s, wide), local.at[6]).wait()
        for k in range(1, n):
            to = (s + k) % n
            remote(
                part(att, to, tok), lanes(atto, s, wide), att_send.at[k], att_recv.at[k], (dp, to)
            ).wait_send()
            back = (s - k + n) % n
            remote(
                part(att, s, tok), lanes(atto, back, wide), att_send.at[k], att_recv.at[k],
                (dp, back),
            ).wait_recv()
        for k in range(2, min(n, 3)):
            fc.step(k)
            proj.step(k)
        middle = widened(xv[pl.ds(pl.multiple_of(s * tok, tok), tok)]) + matmul(
            atto[...], wo[...]
        ) + par[2:3]
        mid[...] = middle
        centred, scale = unit_rows(middle)
        n2[...] = halved(centred * scale * par[3:4] + par[4:5])
        normed.start()
        keep_n = pltpu.make_async_copy(n2, nv_o.at[chip], local.at[7])
        keep_n.start()
        for copy in saves[8:]:
            copy.start()
        for k in range(3, n):
            fc.step(k)
            proj.step(k)
        grads.step()
        normed.step()
        out.close()
        fc.close()
        proj.close()
        grads.close()
        normed.close()
        keep_g.wait()
        keep_n.wait()
        for copy in saves:
            copy.wait()

    half = jnp.bfloat16

    def shape(kind, *dims):
        return jax.ShapeDtypeStruct(dims, kind)

    return pl.pallas_call(
        kernel,
        out_shape=[
            shape(half, nc, tok, depth), shape(half, nc, tok, depth),
            shape(half, nc, 2, n, rows, units), shape(half, 2, n, own_units, depth),
            shape(half, nc, rows, units), shape(half, depth, 3 * wide), shape(half, depth, depth),
            shape(half, length, depth), shape(half, length, 3 * wide), shape(half, length, wide),
            shape(half, tok, depth), shape(jnp.float32, tok, depth), shape(jnp.float32, 16, depth),
            shape(jnp.float32, 16, FF), shape(jnp.float32, heads, length, 1),
        ],
        in_specs=[pl.BlockSpec(memory_space=pl.ANY)] * 7,
        out_specs=[pl.BlockSpec(memory_space=pl.ANY)] * 15,
        scratch_shapes=[
            pltpu.VMEM((length, depth), half), pltpu.VMEM((length, depth), half),
            pltpu.VMEM((depth, 3 * wide), half), pltpu.VMEM((depth, depth), half),
            pltpu.VMEM((ranks * 16, 128), half), pltpu.VMEM((length, 3 * wide), half),
            pltpu.VMEM((length, wide), half), pltpu.VMEM((tok, depth), half),
            pltpu.VMEM((tok, depth), jnp.float32), pltpu.VMEM((tok, depth), half),
            pltpu.VMEM((16, depth), jnp.float32), pltpu.VMEM((16, 2 * depth), jnp.float32),
            pltpu.VMEM((16, FF), jnp.float32), pltpu.VMEM((heads, length, 1), jnp.float32),
            dma(3, n), dma(3, n), dma(n), dma(n), dma(nc), dma(nc), dma(8), dma(n), dma(n), dma(10),
            *Walk.scratch(), *Walk.scratch(), *Walk.scratch(True), *Walk.scratch(True),
            *Spread.scratch(), *Spread.scratch(True), *Spread.scratch(True), *Spread.scratch(True),
            *Spread.scratch(),
        ],
        compiler_params=pltpu.CompilerParams(collective_id=10, has_side_effects=True),
    )(block_input, cotangent, qkv_weight, small, out_weight, fc_weight, proj_weight)


def across(source, target, sems):
    dp, s = place()
    _, n = counts()
    return [
        remote(
            source((s + k) % n), target(s), sems[0].at[k], sems[1].at[k], (dp, (s + k) % n)
        )
        for k in range(n - 1, 0, -1)
    ]


def around(source, target, sems):
    dp, s = place()
    dpc, _ = counts()
    chip, core, nc = dp // 2, dp % 2, dpc // 2
    return [
        remote(
            source((chip + k) % nc), target(chip), sems[0].at[k], sems[1].at[k],
            ((chip + k) % nc * 2 + core, s),
        )
        for k in range(1, nc)
    ]


def norm_back(values, gain, upstream):
    centred, scale = unit_rows(values)
    unit = centred * scale
    inner = upstream * gain
    along = jnp.mean(inner * unit, axis=-1, keepdims=True)
    branch = scale * (inner - jnp.mean(inner, axis=-1, keepdims=True) - unit * along)
    return branch, upstream * unit


def column_sum(values):
    return jnp.sum(values, axis=0, keepdims=True)


def backward(x_own, nv_all, g_all, fc_cols, proj_rows, qkv_cols, out_full, xn_all, qkv_all, att_all, att_own, mid_own, par_all, fcb_all, lt_all):
    dpc, n = counts()
    nc, ranks = dpc // 2, dpc * n
    tok, depth = x_own.shape
    units, rows = fc_cols.shape[1], depth // ranks
    wide, length, many = depth // n, n * tok, nc * tok
    heads, own_units, strip = wide // HD, units // (2 * n), n * rows
    half, full = jnp.bfloat16, jnp.float32
    sources = (
        nv_all, g_all, fc_cols, proj_rows, fcb_all, mid_own, par_all, out_full, att_own, qkv_all,
        att_all, lt_all, qkv_cols, xn_all, x_own,
    )
    count = len(sources)
    tile = 256
    buffers = (
        ((many, tile), full), ((many, tile), full), ((many, units), half), ((many, units), half),
        ((many, depth), half), ((many, depth), half), ((many, depth), half), ((many, depth), half),
        ((units, depth), half), ((units // 2, depth), half), ((units // 2, depth), half),
        ((units // 2, depth), half), ((depth, units), half), ((nc * strip, units), half),
        ((n * nc * rows, units), half), ((n * nc * rows, units), half), ((tok, depth), half),
        ((length, wide), half), ((depth, depth), half), ((nc * strip, depth), half),
        ((nc * strip, depth), half), ((nc * strip, depth), half), ((tok, depth), full),
        ((length, wide), full), ((length, wide), full), ((length, 3 * wide), half),
        ((length, depth), half), ((length, depth), half), ((depth, 3 * wide), half),
        ((nc * strip, 3 * wide), half), ((nc * strip, 3 * wide), half),
        ((nc * strip, 3 * wide), half),
    )

    def kernel(*refs):
        refs = list(refs)

        def take(amount):
            head = refs[:amount]
            del refs[:amount]
            return head

        sources_in = take(count)
        output, stream_out, proj_out, fc_out, out_out, qkv_out, vec_out, qv_out, fb_out = take(9)
        held = take(count)
        nv, g, wf, wp, fcb, mid, par, wo, atto, qkv, att, lt, wq, xn, xo = held
        (
            pre_s, gh_s, hid, ph, b2, b2g, fp, fpg, dp_, dpr, dpp, dpg, df, dfr, dfp, dfg, gas, gat,
            do, dor, dop, dog, gm, dk, dv, grad, b1, b1g, dq_, dqr, dqp, dqg,
        ) = take(len(buffers))
        load = take(1)[0]
        s_b2, s_fp, s_dp, s_dpz, s_df, s_dfz, s_ga, s_do, s_dop, s_b1, s_dq, s_dqp = (
            take(2) for _ in range(12)
        )
        dp, s = place()
        chip, core = dp // 2, dp % 2
        mine = pl.ds(pl.multiple_of(s * tok, tok), tok)

        loads = [
            pltpu.make_async_copy(a, b, load.at[i])
            for i, (a, b) in enumerate(zip(sources_in, held))
        ]
        for copy in loads:
            copy.start()
        greet_near()
        for copy in loads[:5]:
            copy.wait()

        def feed(u, carry):
            cols = pl.ds(pl.multiple_of(u * tile, tile), tile)
            pre_s[...] = matmul(nv[...], wf[:, cols])
            gh_s[...] = contract(g[...], wp[cols, :], (1, 1))
            bias = fcb[7:8, pl.ds(pl.multiple_of(chip * units + u * tile, tile), tile)]

            def block(r, summed):
                at = pl.ds(pl.multiple_of(r * tok, tok), tok)
                act = pre_s[at] + bias
                square = act * act
                bent = jnp.tanh(GELU_COEF * (act + 0.044715 * act * square))
                hid[at, cols] = halved(0.5 * act * (1.0 + bent))
                slope = 0.5 * (1.0 + bent) + (0.5 * act) * (1.0 - bent * bent) * (
                    GELU_COEF * (1.0 + 3.0 * 0.044715 * square)
                )
                grad_pre = gh_s[at] * slope
                ph[at, cols] = halved(grad_pre)
                return summed + column_sum(grad_pre)

            fb_out[0:1, cols] = lax.fori_loop(0, nc, block, jnp.zeros((1, tile), full))
            return carry

        lax.fori_loop(0, units // tile, feed, 0)

        def ring(values, weight, dims, target, got, sems):
            def block(k, carry):
                to = (chip + k) % nc
                at = pl.ds(pl.multiple_of(to * tok, tok), tok)
                target[at] = halved(contract(values[at], weight[...], dims))

                @pl.when(k < nc)
                def _():
                    remote(
                        part(target, to, tok), part(got, chip, tok), sems[0].at[k], sems[1].at[k],
                        (to * 2 + core, s),
                    ).start()

                return carry

            lax.fori_loop(1, nc + 1, block, 0)

        def ring_waits(target, got, sems):
            return around(lambda i: part(target, i, tok), lambda i: part(got, i, tok), sems)

        def summed(own, got, at, size, amount):
            value = widened(part(own, at, size)[...])
            for k in range(1, amount):
                value = value + widened(part(got, (at + k) % amount, size)[...])
            return value

        ring(ph, wf, (1, 1), b2, b2g, s_b2)

        def outer(left, right, target, size):
            def block(r, carry):
                at = pl.ds(pl.multiple_of(r * tile, tile), tile)
                target[at] = halved(contract(left[:, at], right[...], (0, 0)))
                return carry

            lax.fori_loop(0, size // tile, block, 0)

        def halves(target, got, sems, size):
            return [
                remote(
                    part(target, c * 2 + 1 - core, size), part(got, c, size), sems[0].at[c],
                    sems[1].at[c], (other_core(dp), s),
                )
                for c in range(nc)
            ]

        outer(hid, g, dp_, units)
        swap_dp = remote(
            part(dp_, 1 - core, units // 2), dpr, s_dp[0].at[0], s_dp[1].at[0],
            (other_core(dp), s),
        )
        swap_dp.start()
        outer(nv, ph, df, depth)
        swap_df = halves(df, dfr, s_df, strip)
        for copy in swap_df:
            copy.start()
        swap_dp.wait()

        def add_dp(i, carry):
            at = pl.ds(pl.multiple_of(i * own_units, own_units), own_units)
            dpp[at] = halved(
                widened(part(dp_, core * n + i, own_units)[...]) + widened(dpr[at])
            )
            return carry

        lax.fori_loop(0, n, add_dp, 0)
        send_dp = across(
            lambda i: part(dpp, i, own_units), lambda i: part(dpg, i, own_units), s_dpz
        )
        for copy in send_dp:
            copy.start()
        ring(hid, wp, (1, 0), fp, fpg, s_fp)
        for copy in swap_df:
            copy.wait()

        def add_df(j, carry):
            c, i = j // n, j % n
            own = part(df, (c * 2 + core) * n + i, rows)[...]
            part(dfp, i * nc + c, rows)[...] = halved(
                widened(own) + widened(part(dfr, j, rows)[...])
            )
            return carry

        lax.fori_loop(0, nc * n, add_df, 0)
        for copy in loads[5:]:
            copy.wait()
        for copy in ring_waits(b2, b2g, s_b2):
            copy.wait()
        grad_out = widened(part(g, chip, tok)[...])
        upstream = summed(b2, b2g, chip, tok, nc)
        branch, gains = norm_back(mid[...], par[3:4], upstream)
        grad_middle = grad_out + branch
        gm[...] = grad_middle
        middle_half = halved(grad_middle)
        gas[...] = halved(contract(middle_half, wo[...], (1, 1)))
        send_ga = across(lambda i: lanes(gas, i, wide), lambda i: part(gat, i, tok), s_ga)
        for copy in send_ga:
            copy.start()
        vec_out[2:3] = column_sum(grad_middle)
        vec_out[3:4] = column_sum(gains)
        vec_out[4:5] = column_sum(upstream)
        vec_out[5:6] = column_sum(grad_out)
        gat[mine] = gas[:, pl.ds(pl.multiple_of(s * wide, wide), wide)]
        b1[pl.ds(0, tok)] = middle_half
        outer(atto, b1.at[pl.ds(0, tok)], do, depth)
        swap_do = halves(do, dor, s_do, strip)
        for copy in swap_do:
            copy.start()
        dk[...] = jnp.zeros_like(dk)
        dv[...] = jnp.zeros_like(dv)
        for copy in send_ga:
            copy.wait()
        send_df = across(
            lambda i: part(dfp, i, nc * rows), lambda i: part(dfg, i, nc * rows), s_dfz
        )
        for copy in send_df:
            copy.start()
        for copy in swap_do:
            copy.wait()

        def add_halves(own, got, target):
            def block(c, carry):
                part(target, c, strip)[...] = halved(
                    widened(part(own, c * 2 + core, strip)[...])
                    + widened(part(got, c, strip)[...])
                )
                return carry

            lax.fori_loop(0, nc, block, 0)

        add_halves(do, dor, dop)
        send_do = around(lambda i: part(dop, i, strip), lambda i: part(dog, i, strip), s_dop)
        for copy in send_do:
            copy.start()
        scale = HD ** (-0.5)
        sums = jnp.zeros((1, 3 * wide), full)
        for i in range(n - 1, -1, -1):
            seen = (i + 1) * tok
            here, past = pl.ds(i * tok, tok), pl.ds(0, seen)
            queries_back = []
            for p in range(wide // 128):
                group = pl.ds(p * 128, 128)
                q2 = qkv[here, group]
                k2 = qkv[past, pl.ds(wide + p * 128, 128)]
                v2 = qkv[past, pl.ds(2 * wide + p * 128, 128)]
                ga2, att2 = gat[here, group], widened(att[here, group])
                d_query = jnp.zeros((tok, 128), full)
                d_key = jnp.zeros((seen, 128), full)
                d_value = jnp.zeros((seen, 128), full)
                for h in range(2):
                    mask = mask_of(h, q2.shape)
                    qm = jnp.where(mask, q2, jnp.zeros_like(q2))
                    gam = jnp.where(mask, ga2, jnp.zeros_like(ga2))
                    km = jnp.where(mask_of(h, k2.shape), k2, jnp.zeros_like(k2))
                    probs, _ = softmax_block(qm, k2, lt[2 * p + h, here], i * tok)
                    delta = jnp.sum(widened(gam) * att2, axis=-1, keepdims=True)
                    grad_scores = halved(probs * (contract(gam, v2, (1, 1)) - delta))
                    d_query = d_query + matmul(grad_scores, km)
                    d_key = d_key + contract(grad_scores, qm, (0, 0))
                    d_value = d_value + contract(halved(probs), gam, (0, 0))
                dk[past, group] = dk[past, group] + d_key
                dv[past, group] = dv[past, group] + d_value
                queries_back.append(d_query * scale)
            packed = jnp.concatenate(queries_back + [dk[here] * scale, dv[here]], axis=1)
            sums = sums + column_sum(packed)
            packed = halved(packed)
            grad[here] = packed
            b1[here] = halved(contract(packed, wq[...], (1, 1)))

            @pl.when(i != s)
            def _():
                k = (i - s + n) % n
                remote(
                    part(b1, i, tok), part(b1g, s, tok), s_b1[0].at[k], s_b1[1].at[k], (dp, i)
                ).start()

        qv_out[0:1] = sums
        outer(xn, grad, dq_, depth)
        swap_dq = halves(dq_, dqr, s_dq, strip)
        for copy in swap_dq:
            copy.start()
        for copy in ring_waits(fp, fpg, s_fp):
            copy.wait()
        output[...] = mid[...] + summed(fp, fpg, chip, tok, nc) + par[5:6]
        for copy in swap_dq:
            copy.wait()
        add_halves(dq_, dqr, dqp)
        send_dq = around(lambda i: part(dqp, i, strip), lambda i: part(dqg, i, strip), s_dqp)
        for copy in send_dq:
            copy.start()
        for copy in send_dp:
            copy.wait()
        proj_out[...] = summed(dpp, dpg, s, own_units, n)
        for copy in send_do:
            copy.wait()
        out_out[...] = halved(summed(dop, dog, chip, strip, nc))
        for copy in send_dq:
            copy.wait()
        qkv_out[...] = halved(summed(dqp, dqg, chip, strip, nc))
        for copy in across(lambda i: part(b1, i, tok), lambda i: part(b1g, i, tok), s_b1):
            copy.wait()
        upstream = summed(b1, b1g, s, tok, n)
        branch, gains = norm_back(widened(xo[...]), par[0:1], upstream)
        stream_out[...] = gm[...] + branch
        vec_out[0:1] = column_sum(gains)
        vec_out[1:2] = column_sum(upstream)
        for copy in send_df:
            copy.wait()
        fc_out[...] = halved(summed(dfp, dfg, s, nc * rows, n))

    def shape(kind, *dims):
        return jax.ShapeDtypeStruct(dims, kind)

    return pl.pallas_call(
        kernel,
        out_shape=[
            shape(full, tok, depth), shape(full, tok, depth), shape(full, own_units, depth),
            shape(half, nc * rows, units), shape(half, strip, depth), shape(half, strip, 3 * wide),
            shape(full, 8, depth), shape(full, 8, 3 * wide), shape(full, 8, units),
        ],
        in_specs=[pl.BlockSpec(memory_space=pl.ANY)] * count,
        out_specs=[pl.BlockSpec(memory_space=pltpu.VMEM)] * 9,
        scratch_shapes=[pltpu.VMEM(a.shape, a.dtype) for a in sources]
        + [pltpu.VMEM(dims, kind) for dims, kind in buffers]
        + [
            dma(count),
            *[dma(nc)] * 4, *[dma(1)] * 2, *[dma(n)] * 2, *[dma(nc)] * 2, *[dma(n)] * 4,
            *[dma(nc)] * 4, *[dma(n)] * 2, *[dma(nc)] * 4,
        ],
        compiler_params=pltpu.CompilerParams(
            collective_id=11, has_side_effects=True, vmem_limit_bytes=67043328
        ),
    )(*sources)


def plain(
    block_input, cotangent, ln1_gain, ln1_bias, qkv_weight, qv_bias, out_weight, out_bias, ln2_gain,
    ln2_bias, fc_weight, fc_bias, proj_weight, proj_bias,
):
    dp, s = place()
    dpc, n = counts()
    nc, ranks = dpc // 2, dpc * n
    core, chip = dp % 2, dp // 2
    tok_rows = block_input.shape[0]
    rows = qkv_weight.shape[0]
    own_units = fc_bias.shape[0]
    units = FF // nc
    heads = H // n
    wide = heads * HD
    length = n * tok_rows
    score_scale = HD ** (-0.5)

    def row_of(value, i):
        return jnp.pad(value[None], ((i, 15 - i), (0, 128 - value.shape[0])))

    parts = (ln1_gain, ln1_bias, out_bias, ln2_gain, ln2_bias, proj_bias, qv_bias, fc_bias)
    small = row_of(parts[0], 0)
    for i in range(1, 8):
        small = small + row_of(parts[i], i)
    pack = qkv_weight
    if wide % 128:
        pack = (
            qkv_weight.reshape(rows, 3, n, wide).transpose(2, 0, 1, 3).reshape(n, rows, 3 * wide)
        )
    x_all, g_all, pack_all, small_all, out_all, fc_all, proj_all = gather_inputs(
        block_input, cotangent, pack, small, out_weight, fc_weight, proj_weight
    )
    stream_seq = widened(x_all.reshape(length, D))
    grad_ff = g_all.reshape(nc * tok_rows, D)
    qkv_cols = pack_all.reshape(D, 3 * wide)
    out_full = out_all.reshape(D, D)
    fc_cols = fc_all.reshape(D, units)
    proj_rows = proj_all.reshape(units, D)
    smalls = small_all.reshape(ranks, 16, 128)
    gain_one, bias_one, out_bias_full, gain_two, bias_two, proj_bias_full = (
        widened(smalls[:, i, :rows].reshape(D)) for i in range(6)
    )
    qv_full = smalls[:, 6, : qv_bias.shape[0]].reshape(2, n, wide)
    qv_own = widened(lax.dynamic_index_in_dim(qv_full, s, 1, keepdims=False))
    fc_bias_cols = widened(
        lax.dynamic_index_in_dim(
            smalls[:, 7, :own_units].reshape(nc, units), chip, 0, keepdims=False
        )
    )

    normed_one = halved(layer_norm(stream_seq, gain_one, bias_one))
    projected = matmul(normed_one, qkv_cols)

    def by_head(values):
        return values.reshape(length, heads, HD).transpose(1, 0, 2)

    def by_token(values):
        return values.transpose(1, 0, 2).reshape(length, wide)

    def side_by_side(own, got):
        return fill(own, got, s).transpose(1, 0, 2).reshape(tok_rows, n * wide)

    queries = by_head(halved(projected[:, :wide] + qv_own[0]))
    keys = by_head(halved(projected[:, wide : 2 * wide]))
    values = by_head(halved(projected[:, 2 * wide :] + qv_own[1]))
    position = jnp.arange(length, dtype=jnp.int32)
    visible = position[None, :] <= position[:, None]
    scores = (
        jnp.einsum("hqd,hkd->hqk", queries, keys, preferred_element_type=jnp.float32) * score_scale
    )
    log_total = jnp.log(
        jnp.sum(jnp.where(visible, jnp.exp(scores), 0.0), axis=-1, keepdims=True)
    )
    probs = jnp.where(visible, jnp.exp(scores - log_total), 0.0)
    shares = halved(probs)
    attended_heads = halved(
        jnp.einsum("hqk,hkd->hqd", shares, values, preferred_element_type=jnp.float32)
    )
    attended = by_token(attended_heads).reshape(n, tok_rows, wide)
    (attended_got,) = run(1, greet_seq, Exchange(attended))
    attended_own = side_by_side(attended, attended_got)
    stream = widened(block_input)
    middle = stream + matmul(attended_own, out_full) + out_bias_full
    normed_two = halved(layer_norm(middle, gain_two, bias_two))
    (normed_all,) = run(2, greet_near, Gather(normed_two))
    normed_ff = normed_all.reshape(nc * tok_rows, D)
    grad_out = widened(cotangent)
    d_proj_bias = jnp.sum(grad_out, axis=0)
    pre_act = matmul(normed_ff, fc_cols) + fc_bias_cols
    hidden = halved(gelu_tanh(pre_act))
    grad_hidden = matmul(grad_ff, proj_rows.T)
    _, gelu_back = jax.vjp(gelu_tanh, pre_act)
    grad_pre = gelu_back(grad_hidden)[0]
    pre_half = halved(grad_pre)
    back_two = halved(matmul(pre_half, fc_cols.T)).reshape(nc, tok_rows, D)
    ff_part = halved(matmul(hidden, proj_rows)).reshape(nc, tok_rows, D)
    d_proj = halved(matmul(hidden.T, grad_ff)).reshape(2, n, own_units, D)
    d_fc = (
        halved(matmul(normed_ff.T, pre_half))
        .reshape(nc, 2, n, rows, units)
        .transpose(1, 2, 0, 3, 4)
    )
    d_fc_bias = jnp.sum(grad_pre, axis=0)
    back_two_got, d_proj_got, d_fc_got = run(
        3, greet_near, Plane(back_two), Partner(d_proj), Partner(d_fc)
    )

    def pair(own, received):
        kept = lax.dynamic_index_in_dim(own, core, 0, keepdims=False)
        return halved(widened(kept) + widened(received))

    _, norm_back_two = jax.vjp(layer_norm, middle, gain_two, bias_two)
    mid_branch, d_ln2_gain, d_ln2_bias = norm_back_two(total(back_two, back_two_got, chip))
    grad_middle = grad_out + mid_branch
    d_out_bias = jnp.sum(grad_middle, axis=0)
    middle_half = halved(grad_middle)
    d_out = (
        halved(matmul(attended_own.T, middle_half))
        .reshape(nc, 2, n * rows, D)
        .transpose(1, 0, 2, 3)
    )
    grad_attended = halved(matmul(middle_half, out_full.T))
    grad_attended = grad_attended.reshape(tok_rows, n, wide).transpose(1, 0, 2)
    d_proj, d_fc = pair(d_proj, d_proj_got), pair(d_fc, d_fc_got)
    grad_att_got, ff_got, d_proj_parts, d_out_got = run(
        4, greet_near, Exchange(grad_attended), Plane(ff_part), Exchange(d_proj), Partner(d_out)
    )
    proj_grad = total(d_proj, d_proj_parts, s)
    output = middle + total(ff_part, ff_got, chip) + proj_bias_full
    grad_att = by_head(fill(grad_attended, grad_att_got, s).reshape(length, wide))
    row_delta = jnp.sum(widened(grad_att) * widened(attended_heads), axis=-1, keepdims=True)
    grad_shares = jnp.einsum("hqd,hkd->hqk", grad_att, values, preferred_element_type=jnp.float32)
    grad_scores = halved(probs * (grad_shares - row_delta))
    grad_q = (
        jnp.einsum("hqk,hkd->hqd", grad_scores, keys, preferred_element_type=jnp.float32)
        * score_scale
    )
    grad_k = (
        jnp.einsum("hqk,hqd->hkd", grad_scores, queries, preferred_element_type=jnp.float32)
        * score_scale
    )
    grad_v = jnp.einsum("hqk,hqd->hkd", shares, grad_att, preferred_element_type=jnp.float32)
    grad_qkv = jnp.concatenate([by_token(grad_q), by_token(grad_k), by_token(grad_v)], axis=1)
    qkv_half = halved(grad_qkv)
    back_one = halved(matmul(qkv_half, qkv_cols.T)).reshape(n, tok_rows, D)
    d_qkv = (
        halved(matmul(normed_one.T, qkv_half))
        .reshape(nc, 2, n * rows, 3 * wide)
        .transpose(1, 0, 2, 3)
    )
    sums = jnp.sum(grad_qkv, axis=0)
    d_qv = jnp.stack([sums[:wide], sums[2 * wide :]])[:, None]
    d_out = pair(d_out, d_out_got)
    back_one_got, d_fc_parts, d_out_parts, d_qkv_got = run(
        5, greet_near, Exchange(back_one), Exchange(d_fc), Plane(d_out), Partner(d_qkv)
    )
    d_qkv = pair(d_qkv, d_qkv_got)
    fc_cut = halved(total(d_fc, d_fc_parts, s))
    out_cut = halved(total(d_out, d_out_parts, chip)).reshape(n, rows, D)
    _, norm_back_one = jax.vjp(layer_norm, stream, gain_one, bias_one)
    stream_branch, d_ln1_gain, d_ln1_bias = norm_back_one(total(back_one, back_one_got, s))
    grad_stream = grad_middle + stream_branch
    turn = jnp.arange(n, dtype=jnp.int32)[None, :, None] == s
    mine = jnp.arange(nc, dtype=jnp.int32)[:, None] == chip
    vectors = jnp.concatenate(
        [
            v.reshape(ranks, rows)
            for v in (d_ln1_gain, d_ln1_bias, d_out_bias, d_ln2_gain, d_ln2_bias, d_proj_bias)
        ]
        + [
            jnp.where(turn, d_qv, 0.0).reshape(ranks, -1),
            jnp.where(mine, d_fc_bias, 0.0).reshape(ranks, own_units),
        ],
        axis=1,
    )
    used = vectors.shape[1]
    vectors = jnp.pad(vectors, ((0, 0), (0, -used % 128))).reshape(ranks, -1, 128)
    d_qkv_parts, fc_got, d_out_last, vectors_got = run(
        6, greet_all, Plane(d_qkv), Plane(fc_cut), Exchange(out_cut), Everyone(vectors)
    )
    fc_grad = widened(fill(fc_cut, fc_got, chip)).transpose(1, 0, 2).reshape(rows, FF)
    out_grad = total(out_cut, d_out_last, s)
    qkv_rows = halved(total(d_qkv, d_qkv_parts, chip)).reshape(n, rows, 3 * wide)
    vector = jnp.sum(fill(vectors, vectors_got, dp * n + s), axis=0).reshape(-1)
    firsts = [vector[i * rows : (i + 1) * rows] for i in range(6)]
    at = 6 * rows
    qv_grad = vector[at : at + qv_bias.shape[0]]
    at += qv_bias.shape[0]
    fc_bias_grad = vector[at : at + own_units]
    (qkv_got,) = run(7, greet_seq, Exchange(qkv_rows))
    qkv_grad = (
        widened(fill(qkv_rows, qkv_got, s))
        .reshape(n, rows, 3, wide)
        .transpose(1, 2, 0, 3)
        .reshape(rows, 3 * D)
    )
    return (
        output, grad_stream, firsts[0], firsts[1], qkv_grad, qv_grad, out_grad, firsts[2],
        firsts[3], firsts[4], fc_grad, fc_bias_grad, proj_grad, firsts[5],
    )


def fused(
    block_input, cotangent, ln1_gain, ln1_bias, qkv_weight, qv_bias, out_weight, out_bias, ln2_gain,
    ln2_bias, fc_weight, fc_bias, proj_weight, proj_bias,
):
    dp, s = place()
    dpc, n = counts()
    nc, ranks = dpc // 2, dpc * n
    core, chip = dp % 2, dp // 2
    tok_rows = block_input.shape[0]
    rows = qkv_weight.shape[0]
    own_units = fc_bias.shape[0]
    units = FF // nc
    heads = H // n
    wide = heads * HD
    length = n * tok_rows
    score_scale = HD ** (-0.5)

    def row_of(value, i):
        return jnp.pad(value[None], ((i, 15 - i), (0, 128 - value.shape[0])))

    parts = (ln1_gain, ln1_bias, out_bias, ln2_gain, ln2_bias, proj_bias, qv_bias, fc_bias)
    small = row_of(parts[0], 0)
    for i in range(1, 8):
        small = small + row_of(parts[i], i)
    (
        normed_all, g_all, fc_all, proj_all, _, qkv_cols, out_full, xn_all, qkv, attended, attended_own,
        middle, par, fcb, log_totals,
    ) = forward(block_input, cotangent, qkv_weight, small, out_weight, fc_weight, proj_weight)
    output, grad_stream, proj_grad, fc_cut, out_cut, qkv_rows, vecs, qv_sums, fc_sums = backward(
        block_input, normed_all.reshape(nc * tok_rows, D), g_all.reshape(nc * tok_rows, D),
        fc_all.reshape(D, units), proj_all.reshape(units, D), qkv_cols, out_full, xn_all, qkv, attended,
        attended_own, middle, par, fcb, log_totals,
    )
    fc_cut = fc_cut.reshape(nc, rows, units)
    out_cut = out_cut.reshape(n, rows, D)
    qkv_rows = qkv_rows.reshape(n, rows, 3 * wide)
    d_qv = jnp.stack([qv_sums[0, :wide], qv_sums[0, 2 * wide :]])[:, None]
    d_fc_bias = fc_sums[0]
    turn = jnp.arange(n, dtype=jnp.int32)[None, :, None] == s
    mine = jnp.arange(nc, dtype=jnp.int32)[:, None] == chip
    vectors = jnp.concatenate(
        [vecs[:6].reshape(6, ranks, rows).transpose(1, 0, 2).reshape(ranks, 6 * rows)]
        + [
            jnp.where(turn, d_qv, 0.0).reshape(ranks, -1),
            jnp.where(mine, d_fc_bias, 0.0).reshape(ranks, own_units),
        ],
        axis=1,
    )
    used = vectors.shape[1]
    vectors = jnp.pad(vectors, ((0, 0), (0, -used % 128))).reshape(ranks, -1, 128)
    qkv_got, fc_got, d_out_last, vectors_got = run(
        6, greet_all, Exchange(qkv_rows), Plane(fc_cut), Exchange(out_cut), Everyone(vectors)
    )
    fc_grad = widened(fill(fc_cut, fc_got, chip)).transpose(1, 0, 2).reshape(rows, FF)
    out_grad = total(out_cut, d_out_last, s)
    vector = jnp.sum(fill(vectors, vectors_got, dp * n + s), axis=0).reshape(-1)
    firsts = [vector[i * rows : (i + 1) * rows] for i in range(6)]
    at = 6 * rows
    qv_grad = vector[at : at + qv_bias.shape[0]]
    at += qv_bias.shape[0]
    fc_bias_grad = vector[at : at + own_units]
    qkv_grad = (
        widened(fill(qkv_rows, qkv_got, s))
        .reshape(n, rows, 3, wide)
        .transpose(1, 2, 0, 3)
        .reshape(rows, 3 * D)
    )
    return (
        output, grad_stream, firsts[0], firsts[1], qkv_grad, qv_grad, out_grad, firsts[2],
        firsts[3], firsts[4], fc_grad, fc_bias_grad, proj_grad, firsts[5],
    )


def local(*arrays):
    dpc, n = counts()
    fits = (D // n) % 128 == 0 and arrays[4].shape[0] % 16 == 0 and arrays[0].shape[0] % 128 == 0
    return fused(*arrays) if fits and FF // (dpc // 2) % 256 == 0 else plain(*arrays)


def solution(mesh):
    in_specs = (
        P(("dp", "seq"), None),
        P(("dp", "seq"), None),
        P(("dp", "seq")),
        P(("dp", "seq")),
        P(("dp", "seq"), None),
        P(("dp", "seq")),
        P(("dp", "seq"), None),
        P(("dp", "seq")),
        P(("dp", "seq")),
        P(("dp", "seq")),
        P(("dp", "seq"), None),
        P(("dp", "seq")),
        P(("dp", "seq"), None),
        P(("dp", "seq")),
    )
    out_specs = (
        P(("dp", "seq"), None),
        P(("dp", "seq"), None),
        P(("dp", "seq")),
        P(("dp", "seq")),
        P(("dp", "seq"), None),
        P(("dp", "seq")),
        P(("dp", "seq"), None),
        P(("dp", "seq")),
        P(("dp", "seq")),
        P(("dp", "seq")),
        P(("dp", "seq"), None),
        P(("dp", "seq")),
        P(("dp", "seq"), None),
        P(("dp", "seq")),
    )
    return jax.shard_map(local, mesh=mesh, in_specs=in_specs, out_specs=out_specs, check_vma=False)
```
